32 devices in a mesh: dap: 8 (over y, x, core), dp: 4 (over z).
Axes of the slice: x: 2, y: 2, z: 4, core: 2. Of those that a mesh axis runs over, the one named last changes fastest.
Arguments:
- family_matrix: bfloat16 [512, 32, 256], P(('dp', 'dap')), parts along dimension 0, may hold values from -6 to 6
- edge_matrix: bfloat16 [128, 32, 128], P(('dp', 'dap')), parts along dimension 0, may hold values from -6 to 6
- edge_validity: int32 [128, 32], P(('dp', 'dap')), parts along dimension 0, may hold values 0 or 1
- query_key_value_gate_matrix: bfloat16 [256, 1024], replicated, may hold values from -0.375 to 0.375
- logit_offset_matrix: bfloat16 [128, 8], replicated, as said below
- heads_merge_matrix: bfloat16 [256, 256], replicated, may hold values from -0.375 to 0.375
- left_right_factor_matrix: bfloat16 [256, 64], replicated, may hold values from -0.375 to 0.375
- covariance_merge_matrix: bfloat16 [1024, 128], replicated, may hold values from -1 to 1
- edges_gate_factor_matrix: bfloat16 [128, 384], replicated, may hold values from -0.5 to 0.5
- cycle_merge_matrix: bfloat16 [128, 128], replicated, may hold values from -0.5 to 0.5
- loss_sensitivity: bfloat16 [128, 32, 128], P(('dp', 'dap')), parts along dimension 0, may hold values from -6 to 6
Outputs:
- family_after_heads: bfloat16 [512, 32, 256], P(('dp', 'dap')), parts along dimension 0
- pair_output: bfloat16 [128, 32, 128], P(('dp', 'dap')), parts along dimension 0
- pair_gradient: float32 [128, 32, 128], P(('dp', 'dap')), parts along dimension 0
The draws below stay inside these ranges and needn't reach their ends.
There are 4 independent parts, one for each index of `dp`. The reference program is written for one: setup_inputs(seed, part) draws one part's arguments, and reference() takes and returns one part's arrays. A program takes and returns all parts, laid end to end along the dimension named above; an argument that names none is the same for every part. Nothing has to cross between parts.
Inputs may be any that keep to these rules, and one draw needn't show every extreme that they name: `logit_offset_matrix`: independent entries of a fixed spread clipped at four deviations.
All inputs are finite; a program needn't handle non-finite values. No bound on the sum of `edge_validity` on one device may be relied on, other than what follows from the above.
Results may differ from the reference program's by a relative error of at most 0.02.
Values may be sent and summed in bfloat16 or wider, within the bound.
No kernel may reach another device: no remote copies, remote signals or barrier semaphores. Data moves between devices by JAX's collectives and lax.ppermute only.
A program may use at most 64 MiB of HBM per device.

```python
import math
import jax
import jax.numpy as jnp
from jax import lax

FEATURE_DEPTH = 256
CZ = 128
HIDDEN_DIM = 32
HEADS = 8
RES_DEV = 4
SHARD_SEQS_NUM = 16
CROP_LENGTH = 32
ALIGNED_SEQS_NUM = 128
N_DAP = 8


def draw_logit_offset_matrix(key, part):
    values = jnp.clip(jax.random.normal(key, (CZ, HEADS), jnp.float32), -4.0, 4.0) / math.sqrt(CZ)
    return values.astype(jnp.bfloat16)


def plant(array, stream_key, low, high):
    place = [jax.random.randint(jax.random.fold_in(stream_key, axis), (), 0, length) for axis, length in enumerate(array.shape)]
    widest = array.shape.index(max(array.shape))
    neighbour = place[:widest] + [(place[widest] + 1) % array.shape[widest]] + place[widest + 1:]
    return array.at[tuple(place)].set(low).at[tuple(neighbour)].set(high)


def steps_of(rng, dims, pieces, low, high):
    level = 1.0
    for dim, blocks in pieces:
        steps = jax.random.uniform(jax.random.fold_in(jax.random.fold_in(rng, 6), dim), (blocks,), jnp.float32, low / len(pieces), high / len(pieces))
        level = level * jnp.repeat(jnp.exp(steps), dims[dim] // blocks).reshape((-1,) + (1,) * (len(dims) - 1 - dim))
    return level


def noise(key, shape, spread, limit, cuts=(), held_as=jnp.bfloat16):
    level = steps_of(key, shape, cuts, -0.22, 0.18) if cuts else 1.0
    drawn = jax.random.normal(key, shape, jnp.float32) * spread * level
    return jnp.minimum(jnp.maximum(drawn, -limit), limit).astype(held_as)


def setup_inputs(seed: int = 0, part: int = 0) -> dict:
    key_of = jax.random.split(jax.random.key(seed), 12)
    part_keys = jax.random.split(jax.random.fold_in(key_of[11], part), 12)
    family_matrix = noise(part_keys[0], (ALIGNED_SEQS_NUM, CROP_LENGTH, FEATURE_DEPTH), 1.0, 6.0, ((0, 8),))
    edge_matrix = noise(part_keys[1], (CROP_LENGTH, CROP_LENGTH, CZ), 1.0, 6.0, ((0, 8),))
    edge_validity = plant((jax.random.randint(part_keys[2], (CROP_LENGTH, CROP_LENGTH), 0, 4) < 3).astype(jnp.int32), jax.random.fold_in(part_keys[2], 1), 0, 1)
    query_key_value_gate_matrix = noise(key_of[3], (FEATURE_DEPTH, 4 * FEATURE_DEPTH), FEATURE_DEPTH ** -0.5, 0.375)
    logit_offset_matrix = draw_logit_offset_matrix(jax.random.fold_in(key_of[11], 71), part)
    heads_merge_matrix = noise(key_of[5], (FEATURE_DEPTH, FEATURE_DEPTH), FEATURE_DEPTH ** -0.5, 0.375)
    left_right_factor_matrix = noise(key_of[6], (FEATURE_DEPTH, 2 * HIDDEN_DIM), FEATURE_DEPTH ** -0.5, 0.375)
    covariance_merge_matrix = noise(key_of[7], (HIDDEN_DIM * HIDDEN_DIM, CZ), HIDDEN_DIM ** -0.5, 1.0)
    edges_gate_factor_matrix = noise(key_of[8], (CZ, 3 * CZ), CZ ** -0.5, 0.5)
    cycle_merge_matrix = noise(key_of[9], (CZ, CZ), CZ ** -0.5, 0.5)
    loss_sensitivity = noise(part_keys[10], (CROP_LENGTH, CROP_LENGTH, CZ), 1.0, 6.0, ((0, 8),))
    return {"family_matrix": family_matrix, "edge_matrix": edge_matrix, "edge_validity": edge_validity, "query_key_value_gate_matrix": query_key_value_gate_matrix, "logit_offset_matrix": logit_offset_matrix, "heads_merge_matrix": heads_merge_matrix, "left_right_factor_matrix": left_right_factor_matrix, "covariance_merge_matrix": covariance_merge_matrix, "edges_gate_factor_matrix": edges_gate_factor_matrix, "cycle_merge_matrix": cycle_merge_matrix, "loss_sensitivity": loss_sensitivity}


EPSILON = 1e-05

def standardize_features(values):
    center = values - lax.optimization_barrier(jnp.mean(values, -1, keepdims=True))
    scale_inv = lax.rsqrt(lax.optimization_barrier(jnp.mean(center * center, -1, keepdims=True)) + EPSILON)
    return center * scale_inv

def norm_back(values, grad_out):
    center = values - lax.optimization_barrier(jnp.mean(values, -1, keepdims=True))
    scale_inv = lax.rsqrt(lax.optimization_barrier(jnp.mean(center * center, -1, keepdims=True)) + EPSILON)
    standardized_source = center * scale_inv
    return scale_inv * (grad_out - lax.optimization_barrier(jnp.mean(grad_out, -1, keepdims=True)) - standardized_source * lax.optimization_barrier(jnp.mean(grad_out * standardized_source, -1, keepdims=True)))

def lateral_heads_mixing(family_shard_slice, logit_offset_whole, query_key_value_gate_matrix, heads_merge_matrix):
    homolog_number, amino_number, feature_depth = family_shard_slice.shape
    head_count = logit_offset_whole.shape[1]
    head_size = feature_depth // head_count
    standardized_source = standardize_features(family_shard_slice.astype(jnp.float32)).astype(jnp.bfloat16)
    projected = jnp.dot(standardized_source.reshape(-1, feature_depth), query_key_value_gate_matrix, preferred_element_type=jnp.float32)
    projected = projected.reshape(homolog_number, amino_number, 4 * feature_depth)
    shape_heads = (homolog_number, amino_number, head_count, head_size)
    queries = projected[..., :feature_depth].astype(jnp.bfloat16).reshape(shape_heads)
    key_rows = projected[..., feature_depth:2 * feature_depth].astype(jnp.bfloat16).reshape(shape_heads)
    value_rows = projected[..., 2 * feature_depth:3 * feature_depth].astype(jnp.bfloat16).reshape(shape_heads)
    gating = jax.nn.sigmoid(projected[..., 3 * feature_depth:])
    logits = jnp.einsum('sihd,sjhd->sihj', queries.astype(jnp.float32), key_rows.astype(jnp.float32))
    logits = logits / math.sqrt(head_size) + logit_offset_whole.astype(jnp.float32)[None]
    weights = jax.nn.softmax(logits, axis=-1).astype(jnp.bfloat16)
    mixed = jnp.einsum('sihj,sjhd->sihd', weights.astype(jnp.float32), value_rows.astype(jnp.float32))
    gated = (gating * mixed.reshape(homolog_number, amino_number, feature_depth)).astype(jnp.bfloat16)
    edge_increment = jnp.dot(gated.reshape(-1, feature_depth), heads_merge_matrix, preferred_element_type=jnp.float32)
    return (family_shard_slice.astype(jnp.float32) + edge_increment.reshape(homolog_number, amino_number, feature_depth)).astype(jnp.bfloat16)

def reference(family_matrix, edge_matrix, edge_validity, query_key_value_gate_matrix, logit_offset_matrix, heads_merge_matrix, left_right_factor_matrix, covariance_merge_matrix, edges_gate_factor_matrix, cycle_merge_matrix, loss_sensitivity):
    pair_normed = standardize_features(edge_matrix.astype(jnp.float32)).astype(jnp.bfloat16)
    logit_offset_whole = jnp.einsum('ijc,ch->ihj', pair_normed.astype(jnp.float32), logit_offset_matrix.astype(jnp.float32)).astype(jnp.bfloat16)
    batched_lines = family_matrix.reshape(N_DAP, SHARD_SEQS_NUM, CROP_LENGTH, FEATURE_DEPTH)
    family_after_heads = lax.map(lambda family_shard_slice: lateral_heads_mixing(family_shard_slice, logit_offset_whole, query_key_value_gate_matrix, heads_merge_matrix), batched_lines).reshape(ALIGNED_SEQS_NUM, CROP_LENGTH, FEATURE_DEPTH)
    standardized_family = standardize_features(family_after_heads.astype(jnp.float32)).astype(jnp.bfloat16)
    edge_result = jnp.dot(standardized_family.reshape(-1, FEATURE_DEPTH), left_right_factor_matrix, preferred_element_type=jnp.float32)
    edge_result = edge_result.reshape(ALIGNED_SEQS_NUM, CROP_LENGTH, 2 * HIDDEN_DIM).astype(jnp.bfloat16)
    left_rows = edge_result[..., :HIDDEN_DIM]
    right_rows = edge_result[..., HIDDEN_DIM:]
    left_blocks = jnp.transpose(left_rows.reshape(ALIGNED_SEQS_NUM, N_DAP, RES_DEV, HIDDEN_DIM), (1, 0, 2, 3))
    weight_f32 = covariance_merge_matrix.astype(jnp.float32)

    def outer_rows(left_block):
        outer_sum = jnp.einsum('sia,sjb->ijab', left_block.astype(jnp.float32), right_rows.astype(jnp.float32)) / ALIGNED_SEQS_NUM
        flat = outer_sum.reshape(RES_DEV * CROP_LENGTH, HIDDEN_DIM * HIDDEN_DIM)
        return jnp.dot(flat, weight_f32, precision=lax.Precision.HIGHEST).reshape(RES_DEV, CROP_LENGTH, CZ)
    edge_increment = lax.map(outer_rows, left_blocks).reshape(CROP_LENGTH, CROP_LENGTH, CZ)
    pair_mid = (edge_matrix.astype(jnp.float32) + edge_increment).astype(jnp.bfloat16)
    tri_normed = standardize_features(pair_mid.astype(jnp.float32)).astype(jnp.bfloat16)
    tri_proj = jnp.dot(tri_normed.reshape(-1, CZ), edges_gate_factor_matrix, preferred_element_type=jnp.float32).reshape(CROP_LENGTH, CROP_LENGTH, 3 * CZ)
    mask_f = edge_validity.astype(jnp.float32)[..., None]
    side_a = (mask_f * tri_proj[..., :CZ]).astype(jnp.bfloat16)
    side_b = (mask_f * tri_proj[..., CZ:2 * CZ]).astype(jnp.bfloat16)
    gating = jax.nn.sigmoid(tri_proj[..., 2 * CZ:])
    tri_prod = jnp.einsum('ikc,jkc->ijc', side_a.astype(jnp.float32), side_b.astype(jnp.float32))
    prod_normed = standardize_features(tri_prod).astype(jnp.bfloat16)
    tri_update = jnp.dot(prod_normed.reshape(-1, CZ), cycle_merge_matrix, preferred_element_type=jnp.float32).reshape(CROP_LENGTH, CROP_LENGTH, CZ)
    pair_output = (pair_mid.astype(jnp.float32) + gating * tri_update).astype(jnp.bfloat16)
    cot_f32 = loss_sensitivity.astype(jnp.float32)
    grad_update = (cot_f32 * gating).astype(jnp.bfloat16)
    grad_normed = jnp.dot(grad_update.reshape(-1, CZ), cycle_merge_matrix.T, preferred_element_type=jnp.float32).reshape(CROP_LENGTH, CROP_LENGTH, CZ)
    grad_prod = norm_back(tri_prod, grad_normed).astype(jnp.bfloat16)
    grad_a = jnp.einsum('ijc,jkc->ikc', grad_prod.astype(jnp.float32), side_b.astype(jnp.float32))
    prod_blocks = grad_prod.reshape(N_DAP, RES_DEV, CROP_LENGTH, CZ)
    side_blocks = side_a.reshape(N_DAP, RES_DEV, CROP_LENGTH, CZ)

    def add_block(running, items):
        partial_sum = jnp.einsum('ijc,ikc->jkc', items[0].astype(jnp.float32), items[1].astype(jnp.float32))
        rounded = lax.optimization_barrier(partial_sum.astype(jnp.bfloat16))
        return (running + rounded.astype(jnp.float32), None)
    grad_b, unused = lax.scan(add_block, jnp.zeros((CROP_LENGTH, CROP_LENGTH, CZ), jnp.float32), (prod_blocks, side_blocks))
    grad_gate = cot_f32 * tri_update * gating * (1.0 - gating)
    grad_proj = jnp.concatenate([mask_f * grad_a, mask_f * grad_b, grad_gate], -1).astype(jnp.bfloat16)
    grad_input = jnp.dot(grad_proj.reshape(-1, 3 * CZ), edges_gate_factor_matrix.T, preferred_element_type=jnp.float32).reshape(CROP_LENGTH, CROP_LENGTH, CZ)
    pair_gradient = cot_f32 + norm_back(pair_mid.astype(jnp.float32), grad_input)
    return (family_after_heads, pair_output, pair_gradient)
```

```python
import functools
import math

import jax
import jax.numpy as jnp
from jax import lax
from jax.experimental import pallas as pl
from jax.experimental.pallas import tpu as pltpu
from jax.sharding import PartitionSpec as P

EPSILON = 1e-05


def standardize_features(values):
    center = values - jnp.mean(values, -1, keepdims=True)
    scale_inv = lax.rsqrt(jnp.mean(center * center, -1, keepdims=True) + EPSILON)
    return center * scale_inv


def norm_back(values, grad_out):
    center = values - jnp.mean(values, -1, keepdims=True)
    scale_inv = lax.rsqrt(jnp.mean(center * center, -1, keepdims=True) + EPSILON)
    standardized_source = center * scale_inv
    return scale_inv * (
        grad_out
        - jnp.mean(grad_out, -1, keepdims=True)
        - standardized_source * jnp.mean(grad_out * standardized_source, -1, keepdims=True)
    )


def lateral_heads_mixing(
    family_shard_slice, logit_offset_whole, query_key_value_gate_matrix, heads_merge_matrix
):
    homolog_number, amino_number, feature_depth = family_shard_slice.shape
    head_count = logit_offset_whole.shape[1]
    head_size = feature_depth // head_count
    standardized_source = standardize_features(family_shard_slice.astype(jnp.float32)).astype(
        jnp.bfloat16
    )
    projected = jnp.dot(
        standardized_source.reshape(-1, feature_depth),
        query_key_value_gate_matrix,
        preferred_element_type=jnp.float32,
    )
    projected = projected.reshape(homolog_number, amino_number, 4 * feature_depth)
    shape_heads = (homolog_number, amino_number, head_count, head_size)
    queries = projected[..., :feature_depth].astype(jnp.bfloat16).reshape(shape_heads)
    key_rows = (
        projected[..., feature_depth : 2 * feature_depth].astype(jnp.bfloat16).reshape(shape_heads)
    )
    value_rows = (
        projected[..., 2 * feature_depth : 3 * feature_depth]
        .astype(jnp.bfloat16)
        .reshape(shape_heads)
    )
    gating = jax.nn.sigmoid(projected[..., 3 * feature_depth :])
    logits = jnp.einsum("sihd,sjhd->sihj", queries, key_rows, preferred_element_type=jnp.float32)
    logits = logits / math.sqrt(head_size) + logit_offset_whole.astype(jnp.float32)[None]
    weights = jax.nn.softmax(logits, axis=-1).astype(jnp.bfloat16)
    mixed = jnp.einsum("sihj,sjhd->sihd", weights, value_rows, preferred_element_type=jnp.float32)
    gated = (gating * mixed.reshape(homolog_number, amino_number, feature_depth)).astype(
        jnp.bfloat16
    )
    edge_increment = jnp.dot(
        gated.reshape(-1, feature_depth), heads_merge_matrix, preferred_element_type=jnp.float32
    )
    return (
        family_shard_slice.astype(jnp.float32)
        + edge_increment.reshape(homolog_number, amino_number, feature_depth)
    ).astype(jnp.bfloat16)


def pair_projection_step(alignment_rows, left_right_factor_matrix):
    standardized_source = standardize_features(alignment_rows.astype(jnp.float32)).astype(
        jnp.bfloat16
    )
    edge_result = jnp.dot(
        standardized_source.reshape(-1, alignment_rows.shape[2]),
        left_right_factor_matrix,
        preferred_element_type=jnp.float32,
    )
    return edge_result.reshape(alignment_rows.shape[0], alignment_rows.shape[1], -1).astype(
        jnp.bfloat16
    )


def body_general(
    family_matrix,
    edge_matrix,
    edge_validity,
    query_key_value_gate_matrix,
    logit_offset_matrix,
    heads_merge_matrix,
    left_right_factor_matrix,
    covariance_merge_matrix,
    edges_gate_factor_matrix,
    cycle_merge_matrix,
    loss_sensitivity,
):
    res_rows, width, pair_chans = edge_matrix.shape
    pair_normed = standardize_features(edge_matrix.astype(jnp.float32)).astype(jnp.bfloat16)
    bias_local = jnp.einsum(
        "ijc,ch->ihj", pair_normed, logit_offset_matrix, preferred_element_type=jnp.float32
    ).astype(jnp.bfloat16)
    logit_offset_whole = lax.all_gather(bias_local, "dap", axis=0, tiled=True)
    homolog_lines = family_matrix.shape[0]
    homolog_subset = math.gcd(homolog_lines, 8)
    batched_lines = family_matrix.reshape(
        homolog_lines // homolog_subset,
        homolog_subset,
        family_matrix.shape[1],
        family_matrix.shape[2],
    )
    family_after_heads = lax.map(
        lambda family_shard_slice: lateral_heads_mixing(
            family_shard_slice, logit_offset_whole, query_key_value_gate_matrix, heads_merge_matrix
        ),
        batched_lines,
    ).reshape(family_matrix.shape)
    hidden = left_right_factor_matrix.shape[1] // 2
    weight_f32 = covariance_merge_matrix.astype(jnp.float32)
    alignment_columns = lax.all_to_all(
        family_after_heads, "dap", split_axis=1, concat_axis=0, tiled=True
    )
    edge_result = pair_projection_step(alignment_columns, left_right_factor_matrix)
    left_part = edge_result[..., :hidden]
    right_part = edge_result[..., hidden:]
    sequence_full_count = alignment_columns.shape[0]
    shard_in = lax.all_gather(right_part, "dap", axis=1, tiled=True)
    outer_sum = (
        jnp.einsum("sia,sjb->ijab", left_part, shard_in, preferred_element_type=jnp.float32)
        / sequence_full_count
    )
    row_count = shard_in.shape[1]
    flat = outer_sum.reshape(res_rows * row_count, hidden * hidden)
    edge_increment = jnp.dot(flat, weight_f32, precision=lax.Precision.HIGHEST).reshape(
        res_rows, row_count, pair_chans
    )
    pair_mid = (edge_matrix.astype(jnp.float32) + edge_increment).astype(jnp.bfloat16)
    tri_normed = standardize_features(pair_mid.astype(jnp.float32)).astype(jnp.bfloat16)
    tri_proj = jnp.dot(
        tri_normed.reshape(-1, pair_chans),
        edges_gate_factor_matrix,
        preferred_element_type=jnp.float32,
    ).reshape(res_rows, width, 3 * pair_chans)
    mask_f = edge_validity.astype(jnp.float32)[..., None]
    side_a = (mask_f * tri_proj[..., :pair_chans]).astype(jnp.bfloat16)
    side_b = (mask_f * tri_proj[..., pair_chans : 2 * pair_chans]).astype(jnp.bfloat16)
    gating = jax.nn.sigmoid(tri_proj[..., 2 * pair_chans :])
    tri_prod = jnp.einsum(
        "ikc,jkc->ijc",
        side_a,
        lax.all_gather(side_b, "dap", axis=0, tiled=True),
        preferred_element_type=jnp.float32,
    )
    prod_normed = standardize_features(tri_prod).astype(jnp.bfloat16)
    tri_update = jnp.dot(
        prod_normed.reshape(-1, pair_chans), cycle_merge_matrix, preferred_element_type=jnp.float32
    ).reshape(res_rows, width, pair_chans)
    pair_output = (pair_mid.astype(jnp.float32) + gating * tri_update).astype(jnp.bfloat16)
    cot_f32 = loss_sensitivity.astype(jnp.float32)
    grad_update = (cot_f32 * gating).astype(jnp.bfloat16)
    grad_normed = jnp.dot(
        grad_update.reshape(-1, pair_chans),
        cycle_merge_matrix.T,
        preferred_element_type=jnp.float32,
    ).reshape(res_rows, width, pair_chans)
    grad_prod = norm_back(tri_prod, grad_normed).astype(jnp.bfloat16)
    grad_part = grad_prod
    grad_a = jnp.einsum(
        "ijc,jkc->ikc",
        grad_part,
        lax.all_gather(side_b, "dap", axis=0, tiled=True),
        preferred_element_type=jnp.float32,
    )
    grad_part = grad_prod
    grad_b = lax.psum_scatter(
        jnp.einsum("ijc,ikc->jkc", grad_part, side_a, preferred_element_type=jnp.float32).astype(
            jnp.bfloat16
        ),
        "dap",
        scatter_dimension=0,
        tiled=True,
    ).astype(jnp.float32)
    grad_gate = cot_f32 * tri_update * gating * (1.0 - gating)
    grad_proj = jnp.concatenate([mask_f * grad_a, mask_f * grad_b, grad_gate], -1).astype(
        jnp.bfloat16
    )
    grad_input = jnp.dot(
        grad_proj.reshape(-1, 3 * pair_chans),
        edges_gate_factor_matrix.T,
        preferred_element_type=jnp.float32,
    ).reshape(res_rows, width, pair_chans)
    pair_gradient = cot_f32 + norm_back(pair_mid.astype(jnp.float32), grad_input)
    return (family_after_heads, pair_output, pair_gradient)


F32 = jnp.float32
BF16 = jnp.bfloat16
NT = (((1,), (1,)), ((), ()))


def dot(a, b):
    return jnp.dot(a, b, preferred_element_type=F32)


def dot_nt(a, b):
    return lax.dot_general(a, b, NT, preferred_element_type=F32)


def iota(shape, dim):
    return lax.broadcasted_iota(jnp.int32, shape, dim)


def bias_kernel(edge_ref, weight_ref, out_ref):
    rows, chans = edge_ref.shape
    own, lanes = out_ref.shape
    width = rows // own
    heads = weight_ref.shape[1]
    normed = standardize_features(edge_ref[...].astype(F32)).astype(BF16)
    spread = (iota((heads, lanes), 0) == iota((heads, lanes), 1) // width).astype(F32)
    weight = dot(weight_ref[...], spread.astype(BF16)).astype(BF16)
    every = dot(normed, weight)
    keep = iota((rows, lanes), 0) % width == iota((rows, lanes), 1) % width
    picked = jnp.where(keep, every, 0.0).reshape(own, width, lanes)
    out_ref[...] = jnp.sum(picked, 1).astype(BF16)


def attention_kernel(
    width,
    heads,
    family_ref,
    bias_ref,
    project_ref,
    merge_ref,
    factor_ref,
    edge_ref,
    loss_ref,
    mask_ref,
    family_out_ref,
    send_ref,
    query_s,
    key_s,
    value_s,
    weight_s,
    row_s,
    mask_s,
):
    rows, depth = family_ref.shape
    seqs = rows // width
    tiles = depth // 128
    group = 128 // width
    source = family_ref[...].astype(F32)
    normed = standardize_features(source).astype(BF16)
    query_s[...] = dot(normed, project_ref[:, :depth]).astype(BF16)
    key_s[...] = dot(normed, project_ref[:, depth : 2 * depth]).astype(BF16)
    value_s[...] = dot(normed, project_ref[:, 2 * depth : 3 * depth]).astype(BF16)
    gating = jax.nn.sigmoid(dot(normed, project_ref[:, 3 * depth :]))
    same = (iota((128, 128), 0) // width == iota((128, 128), 1) // width).astype(F32).astype(BF16)
    lane_group = iota((rows, 128), 1) // width
    scale = 1.0 / math.sqrt(depth // heads)
    gated = []
    for t in range(tiles):
        cols = slice(128 * t, 128 * t + 128)
        bias = bias_ref[:, cols].astype(F32)
        parts = []
        for s in range(seqs):
            span = slice(width * s, width * s + width)
            keys = jnp.concatenate([key_s[span, cols]] * group, 0) * same
            parts.append(dot_nt(query_s[span, cols], keys) * scale + bias)
        logits = jnp.concatenate(parts, 0)
        top = jnp.full(logits.shape, -jnp.inf, F32)
        for h in range(group):
            best = jnp.max(
                jnp.where(lane_group == h, logits, -jnp.inf), axis=-1, keepdims=True
            )
            top = jnp.where(lane_group == h, best, top)
        weight_s[...] = jnp.exp(logits - top).astype(BF16)
        total = dot(weight_s[...], same)
        parts = []
        for s in range(seqs):
            span = slice(width * s, width * s + width)
            values = jnp.concatenate([value_s[span, cols]] * group, 0) * same
            parts.append(dot(weight_s[span, :], values))
        mixed = jnp.concatenate(parts, 0) / total
        gated.append((gating[:, cols] * mixed).astype(BF16))
    after = (source + dot(jnp.concatenate(gated, 1), merge_ref[...])).astype(BF16)
    family_out_ref[...] = after
    ready = standardize_features(after.astype(F32))
    for t in range(tiles):
        row_s[rows * t : rows * (t + 1), :] = ready[:, 128 * t : 128 * t + 128]
    hidden = factor_ref.shape[1] // 2
    placed = jnp.zeros((width // group * seqs, 256), F32)
    for q in range(group):
        picked = jnp.concatenate(
            [
                jnp.concatenate(
                    [
                        row_s[pl.ds(rows * t + group * g + q, seqs, stride=width), :]
                        for g in range(width // group)
                    ],
                    0,
                )
                for t in range(tiles)
            ],
            1,
        ).astype(BF16)
        both = dot(picked, factor_ref[...]).astype(BF16)
        src = iota((2 * hidden, 256), 0)
        dst = iota((2 * hidden, 256), 1)
        goal = src % hidden + hidden * q + 128 * (src // hidden)
        placed = placed + dot(both, (goal == dst).astype(F32).astype(BF16))
    groups = width // group
    for g in range(groups):
        span = slice(seqs * g, seqs * g + seqs)
        send_ref[seqs * g : seqs * (g + 1), :] = placed[span, :128].astype(BF16)
        base = seqs * groups
        send_ref[base + seqs * g : base + seqs * (g + 1), :] = placed[span, 128:].astype(BF16)
    base = 2 * seqs * groups
    pairs = edge_ref.shape[0]
    send_ref[base : base + pairs, :] = edge_ref[...]
    send_ref[base + pairs : base + 2 * pairs, :] = loss_ref[...]
    own = mask_ref.shape[0]
    mask_s[...] = jnp.zeros(mask_s.shape, F32)
    mask_s[:own, :] = mask_ref[...].astype(F32)
    eye = (iota((width, width), 0) == iota((width, width), 1)).astype(F32).astype(BF16)
    send_ref[base + 2 * pairs :, :] = dot_nt(eye, mask_s[...].astype(BF16)).astype(BF16)


def block_transpose(blocks, step):
    lane = iota(blocks[0].shape, 1)
    for shift in (2 * step, step):
        low = lane // shift % 2 == 0
        stride = shift // step
        out = list(blocks)
        for q in range(len(blocks)):
            if q // stride % 2 == 0:
                x, y = blocks[q], blocks[q + stride]
                up = pltpu.roll(y, shift, 1)
                down = pltpu.roll(x, 4 * step - shift, 1)
                out[q] = jnp.where(low, x, up)
                out[q + stride] = jnp.where(low, down, y)
        blocks = out
    return blocks


def pair_kernel(
    axis,
    width,
    own,
    hidden,
    seqs,
    all_ref,
    covariance_ref,
    edges_ref,
    cycle_ref,
    out_ref,
    grad_ref,
    turn_s,
    right_s,
    cov_s,
    cov_bf_s,
    mid_s,
    a_s,
    b_s,
    loss_s,
    own_a_s,
    own_b_s,
    tri_s,
):
    me = lax.axis_index(axis)
    n = all_ref.shape[0]
    group = 128 // hidden
    groups = width // group
    base = 2 * seqs * groups
    pairs = own * width
    chans = 128

    def gathered(first, count):
        return jnp.concatenate([all_ref[d, first : first + count, :] for d in range(n)], 0)

    for g in range(groups):
        right = gathered(seqs * groups + seqs * g, seqs).astype(F32)
        turn_s[128 * g : 128 * g + 128, :] = right.T
    cov_s[...] = covariance_ref[...].astype(F32)
    for b in range(hidden):
        span = slice(width * b, width * b + width)
        right_s[span, :] = turn_s[pl.ds(b, width, stride=hidden), :].astype(BF16)
        span = slice(hidden * b, hidden * b + hidden)
        cov_bf_s[span, :] = cov_s[pl.ds(b, hidden, stride=hidden), :].astype(BF16)
    for g in range(groups):
        left = gathered(seqs * g, seqs)
        outer = dot(right_s[...], left)
        columns = []
        for p in range(hidden // group):
            first = 128 * p
            columns.append(
                block_transpose(
                    [outer[first + width * q : first + width * (q + 1), :] for q in range(group)],
                    hidden,
                )
            )
        flat = jnp.concatenate(
            [jnp.concatenate([c[i] for c in columns], 1) for i in range(group)], 0
        )
        high = flat.astype(BF16)
        low = (flat - high.astype(F32)).astype(BF16)
        added = (dot(high, cov_bf_s[...]) + dot(low, cov_bf_s[...])) * (1.0 / (seqs * n))
        span = slice(pairs * g, pairs * (g + 1))
        edge = all_ref[g, base : base + pairs, :].astype(F32)
        mid = (edge + added).astype(BF16).astype(F32)
        mid_s[span, :] = mid
        normed = standardize_features(mid).astype(BF16)
        sides = dot(normed, edges_ref[:, : 2 * chans])
        mask = all_ref[g, base + 2 * pairs :, :].astype(F32)
        keep = jnp.concatenate(
            [jnp.broadcast_to(mask[:, r : r + 1], (width, chans)) for r in range(own)], 0
        )
        a_s[span, :] = (keep * sides[:, :chans]).astype(BF16).astype(F32)
        b_s[span, :] = (keep * sides[:, chans:]).astype(BF16).astype(F32)
        loss_s[span, :] = all_ref[g, base + pairs : base + 2 * pairs, :].astype(F32)

    rows = pl.ds(pl.multiple_of(me * pairs, pairs), pairs)

    def rows_and_columns(ref):
        return jnp.concatenate(
            [ref[rows, :]] + [ref[pl.ds(me * own + r, width, stride=width), :] for r in range(own)],
            0,
        )

    mid = rows_and_columns(mid_s)
    loss = rows_and_columns(loss_s)
    own_a_s[...] = a_s[rows, :]
    own_b_s[...] = b_s[rows, :]
    normed = standardize_features(mid).astype(BF16)
    gating = jax.nn.sigmoid(dot(normed, edges_ref[:, 2 * chans :]))

    def row(ref, r):
        return jnp.broadcast_to(ref[r : r + 1, :], (width, chans))

    acc = [jnp.zeros((width, chans), F32) for _ in range(2 * own)]
    for k in range(width):
        b_k = b_s[pl.ds(k, width, stride=width), :]
        a_k = a_s[pl.ds(k, width, stride=width), :]
        for r in range(own):
            acc[r] = acc[r] + row(own_a_s, width * r + k) * b_k
            acc[own + r] = acc[own + r] + row(own_b_s, width * r + k) * a_k
    tri = jnp.concatenate(acc, 0)
    center = tri - jnp.mean(tri, -1, keepdims=True)
    scale_inv = lax.rsqrt(jnp.mean(center * center, -1, keepdims=True) + EPSILON)
    unit = center * scale_inv
    update = dot(unit[:pairs].astype(BF16), cycle_ref[...])
    out_ref[...] = (mid[:pairs] + gating[:pairs] * update).astype(BF16)
    grad_normed = dot_nt((loss * gating).astype(BF16), cycle_ref[...])
    tri_s[...] = (
        (
            scale_inv
            * (
                grad_normed
                - jnp.mean(grad_normed, -1, keepdims=True)
                - unit * jnp.mean(grad_normed * unit, -1, keepdims=True)
            )
        )
        .astype(BF16)
        .astype(F32)
    )
    acc = [jnp.zeros((width, chans), F32) for _ in range(2 * own)]
    for j in range(width):
        span = slice(width * j, width * j + width)
        b_j = b_s[span, :]
        a_j = a_s[span, :]
        for r in range(own):
            acc[r] = acc[r] + row(tri_s, width * r + j) * b_j
            acc[own + r] = acc[own + r] + row(tri_s, pairs + width * r + j) * a_j
    mask = all_ref[me, base + 2 * pairs :, :].astype(F32)
    keep = jnp.concatenate(
        [jnp.broadcast_to(mask[:, r : r + 1], (width, chans)) for r in range(own)], 0
    )
    gate_own = gating[:pairs]
    grad_gate = loss[:pairs] * update * gate_own * (1.0 - gate_own)
    grad_proj = jnp.concatenate(
        [
            keep * jnp.concatenate(acc[:own], 0),
            keep * jnp.concatenate(acc[own:], 0),
            grad_gate,
        ],
        1,
    ).astype(BF16)
    grad_input = dot_nt(grad_proj, edges_ref[...])
    grad_ref[...] = loss[:pairs] + norm_back(mid[:pairs], grad_input)


def body_resident(
    family_matrix,
    edge_matrix,
    edge_validity,
    query_key_value_gate_matrix,
    logit_offset_matrix,
    heads_merge_matrix,
    left_right_factor_matrix,
    covariance_merge_matrix,
    edges_gate_factor_matrix,
    cycle_merge_matrix,
    loss_sensitivity,
):
    seqs, width, depth = family_matrix.shape
    own, _, chans = edge_matrix.shape
    heads = logit_offset_matrix.shape[1]
    hidden = left_right_factor_matrix.shape[1] // 2
    pairs = own * width
    every = width * width
    edge = edge_matrix.reshape(pairs, chans)
    loss = loss_sensitivity.reshape(pairs, chans)
    vmem = pl.BlockSpec(memory_space=pltpu.VMEM)
    bias = pl.pallas_call(
        bias_kernel,
        out_shape=jax.ShapeDtypeStruct((own, heads * width), BF16),
        in_specs=[vmem] * 2,
        out_specs=vmem,
        name="pair_bias",
    )(edge, logit_offset_matrix)
    bias_all = lax.all_gather(bias, "dap", axis=0, tiled=True)
    sent = 2 * seqs * width * hidden // 128 + 2 * pairs + width
    family_out, send = pl.pallas_call(
        functools.partial(attention_kernel, width, heads),
        out_shape=(
            jax.ShapeDtypeStruct((seqs * width, depth), BF16),
            jax.ShapeDtypeStruct((sent, chans), BF16),
        ),
        in_specs=[vmem] * 8,
        out_specs=(vmem, vmem),
        scratch_shapes=[pltpu.VMEM((seqs * width, depth), BF16)] * 3
        + [
            pltpu.VMEM((seqs * width, 128), BF16),
            pltpu.VMEM((seqs * width * depth // 128, 128), F32),
            pltpu.VMEM((128, width), F32),
        ],
        name="row_attention",
    )(
        family_matrix.reshape(seqs * width, depth),
        bias_all,
        query_key_value_gate_matrix,
        heads_merge_matrix,
        left_right_factor_matrix,
        edge,
        loss,
        edge_validity,
    )
    gathered = lax.all_gather(send, "dap", axis=0, tiled=False)
    pair_out, pair_grad = pl.pallas_call(
        functools.partial(pair_kernel, "dap", width, own, hidden, seqs),
        out_shape=(
            jax.ShapeDtypeStruct((pairs, chans), BF16),
            jax.ShapeDtypeStruct((pairs, chans), F32),
        ),
        in_specs=[vmem] * 4,
        out_specs=(vmem, vmem),
        scratch_shapes=[
            pltpu.VMEM((hidden * width, 128), F32),
            pltpu.VMEM((hidden * width, 128), BF16),
            pltpu.VMEM((hidden * hidden, chans), F32),
            pltpu.VMEM((hidden * hidden, chans), BF16),
            pltpu.VMEM((every, chans), F32),
            pltpu.VMEM((every, chans), F32),
            pltpu.VMEM((every, chans), F32),
            pltpu.VMEM((every, chans), F32),
            pltpu.VMEM((pairs, chans), F32),
            pltpu.VMEM((pairs, chans), F32),
            pltpu.VMEM((2 * pairs, chans), F32),
        ],
        name="pair_update",
    )(gathered, covariance_merge_matrix, edges_gate_factor_matrix, cycle_merge_matrix)
    return (
        family_out.reshape(seqs, width, depth),
        pair_out.reshape(own, width, chans),
        pair_grad.reshape(own, width, chans),
    )


def fits_resident(dap, family, edge, logit, factor):
    seqs, width, depth = family.shape
    own, _, chans = edge.shape
    return (
        own * dap == width
        and width == 32
        and factor.shape[1] == 64
        and depth == 32 * logit.shape[1]
        and depth % 128 == 0
        and chans == 128
        and own * width == 128
        and seqs % 16 == 0
        and seqs * dap == 128
    )


def body(*args):
    dap = lax.axis_size("dap")
    if fits_resident(dap, args[0], args[1], args[4], args[6]):
        return body_resident(*args)
    return body_general(*args)


def solution(mesh):
    in_specs = (
        P(("dp", "dap"), None, None),
        P(("dp", "dap"), None, None),
        P(("dp", "dap"), None),
        P(),
        P(),
        P(),
        P(),
        P(),
        P(),
        P(),
        P(("dp", "dap"), None, None),
    )
    out_specs = (
        P(("dp", "dap"), None, None),
        P(("dp", "dap"), None, None),
        P(("dp", "dap"), None, None),
    )
    return jax.shard_map(body, mesh=mesh, in_specs=in_specs, out_specs=out_specs, check_vma=False)
```

```python
import functools
import math

import jax
import jax.numpy as jnp
from jax import lax
from jax.experimental import pallas as pl
from jax.experimental.pallas import tpu as pltpu
from jax.sharding import PartitionSpec as P

EPSILON = 1e-05


def standardize_features(values):
    center = values - jnp.mean(values, -1, keepdims=True)
    scale_inv = lax.rsqrt(jnp.mean(center * center, -1, keepdims=True) + EPSILON)
    return center * scale_inv


def norm_back(values, grad_out):
    center = values - jnp.mean(values, -1, keepdims=True)
    scale_inv = lax.rsqrt(jnp.mean(center * center, -1, keepdims=True) + EPSILON)
    standardized_source = center * scale_inv
    return scale_inv * (
        grad_out
        - jnp.mean(grad_out, -1, keepdims=True)
        - standardized_source * jnp.mean(grad_out * standardized_source, -1, keepdims=True)
    )


def lateral_heads_mixing(
    family_shard_slice, logit_offset_whole, query_key_value_gate_matrix, heads_merge_matrix
):
    homolog_number, amino_number, feature_depth = family_shard_slice.shape
    head_count = logit_offset_whole.shape[1]
    head_size = feature_depth // head_count
    standardized_source = standardize_features(family_shard_slice.astype(jnp.float32)).astype(
        jnp.bfloat16
    )
    projected = jnp.dot(
        standardized_source.reshape(-1, feature_depth),
        query_key_value_gate_matrix,
        preferred_element_type=jnp.float32,
    )
    projected = projected.reshape(homolog_number, amino_number, 4 * feature_depth)
    shape_heads = (homolog_number, amino_number, head_count, head_size)
    queries = projected[..., :feature_depth].astype(jnp.bfloat16).reshape(shape_heads)
    key_rows = (
        projected[..., feature_depth : 2 * feature_depth].astype(jnp.bfloat16).reshape(shape_heads)
    )
    value_rows = (
        projected[..., 2 * feature_depth : 3 * feature_depth]
        .astype(jnp.bfloat16)
        .reshape(shape_heads)
    )
    gating = jax.nn.sigmoid(projected[..., 3 * feature_depth :])
    logits = jnp.einsum("sihd,sjhd->sihj", queries, key_rows, preferred_element_type=jnp.float32)
    logits = logits / math.sqrt(head_size) + logit_offset_whole.astype(jnp.float32)[None]
    weights = jax.nn.softmax(logits, axis=-1).astype(jnp.bfloat16)
    mixed = jnp.einsum("sihj,sjhd->sihd", weights, value_rows, preferred_element_type=jnp.float32)
    gated = (gating * mixed.reshape(homolog_number, amino_number, feature_depth)).astype(
        jnp.bfloat16
    )
    edge_increment = jnp.dot(
        gated.reshape(-1, feature_depth), heads_merge_matrix, preferred_element_type=jnp.float32
    )
    return (
        family_shard_slice.astype(jnp.float32)
        + edge_increment.reshape(homolog_number, amino_number, feature_depth)
    ).astype(jnp.bfloat16)


def pair_projection_step(alignment_rows, left_right_factor_matrix):
    standardized_source = standardize_features(alignment_rows.astype(jnp.float32)).astype(
        jnp.bfloat16
    )
    edge_result = jnp.dot(
        standardized_source.reshape(-1, alignment_rows.shape[2]),
        left_right_factor_matrix,
        preferred_element_type=jnp.float32,
    )
    return edge_result.reshape(alignment_rows.shape[0], alignment_rows.shape[1], -1).astype(
        jnp.bfloat16
    )


def body_general(
    family_matrix,
    edge_matrix,
    edge_validity,
    query_key_value_gate_matrix,
    logit_offset_matrix,
    heads_merge_matrix,
    left_right_factor_matrix,
    covariance_merge_matrix,
    edges_gate_factor_matrix,
    cycle_merge_matrix,
    loss_sensitivity,
):
    res_rows, width, pair_chans = edge_matrix.shape
    pair_normed = standardize_features(edge_matrix.astype(jnp.float32)).astype(jnp.bfloat16)
    bias_local = jnp.einsum(
        "ijc,ch->ihj", pair_normed, logit_offset_matrix, preferred_element_type=jnp.float32
    ).astype(jnp.bfloat16)
    logit_offset_whole = lax.all_gather(bias_local, "dap", axis=0, tiled=True)
    homolog_lines = family_matrix.shape[0]
    homolog_subset = math.gcd(homolog_lines, 8)
    batched_lines = family_matrix.reshape(
        homolog_lines // homolog_subset,
        homolog_subset,
        family_matrix.shape[1],
        family_matrix.shape[2],
    )
    family_after_heads = lax.map(
        lambda family_shard_slice: lateral_heads_mixing(
            family_shard_slice, logit_offset_whole, query_key_value_gate_matrix, heads_merge_matrix
        ),
        batched_lines,
    ).reshape(family_matrix.shape)
    hidden = left_right_factor_matrix.shape[1] // 2
    weight_f32 = covariance_merge_matrix.astype(jnp.float32)
    alignment_columns = lax.all_to_all(
        family_after_heads, "dap", split_axis=1, concat_axis=0, tiled=True
    )
    edge_result = pair_projection_step(alignment_columns, left_right_factor_matrix)
    left_part = edge_result[..., :hidden]
    right_part = edge_result[..., hidden:]
    sequence_full_count = alignment_columns.shape[0]
    shard_in = lax.all_gather(right_part, "dap", axis=1, tiled=True)
    outer_sum = (
        jnp.einsum("sia,sjb->ijab", left_part, shard_in, preferred_element_type=jnp.float32)
        / sequence_full_count
    )
    row_count = shard_in.shape[1]
    flat = outer_sum.reshape(res_rows * row_count, hidden * hidden)
    edge_increment = jnp.dot(flat, weight_f32, precision=lax.Precision.HIGHEST).reshape(
        res_rows, row_count, pair_chans
    )
    pair_mid = (edge_matrix.astype(jnp.float32) + edge_increment).astype(jnp.bfloat16)
    tri_normed = standardize_features(pair_mid.astype(jnp.float32)).astype(jnp.bfloat16)
    tri_proj = jnp.dot(
        tri_normed.reshape(-1, pair_chans),
        edges_gate_factor_matrix,
        preferred_element_type=jnp.float32,
    ).reshape(res_rows, width, 3 * pair_chans)
    mask_f = edge_validity.astype(jnp.float32)[..., None]
    side_a = (mask_f * tri_proj[..., :pair_chans]).astype(jnp.bfloat16)
    side_b = (mask_f * tri_proj[..., pair_chans : 2 * pair_chans]).astype(jnp.bfloat16)
    gating = jax.nn.sigmoid(tri_proj[..., 2 * pair_chans :])
    tri_prod = jnp.einsum(
        "ikc,jkc->ijc",
        side_a,
        lax.all_gather(side_b, "dap", axis=0, tiled=True),
        preferred_element_type=jnp.float32,
    )
    prod_normed = standardize_features(tri_prod).astype(jnp.bfloat16)
    tri_update = jnp.dot(
        prod_normed.reshape(-1, pair_chans), cycle_merge_matrix, preferred_element_type=jnp.float32
    ).reshape(res_rows, width, pair_chans)
    pair_output = (pair_mid.astype(jnp.float32) + gating * tri_update).astype(jnp.bfloat16)
    cot_f32 = loss_sensitivity.astype(jnp.float32)
    grad_update = (cot_f32 * gating).astype(jnp.bfloat16)
    grad_normed = jnp.dot(
        grad_update.reshape(-1, pair_chans),
        cycle_merge_matrix.T,
        preferred_element_type=jnp.float32,
    ).reshape(res_rows, width, pair_chans)
    grad_prod = norm_back(tri_prod, grad_normed).astype(jnp.bfloat16)
    grad_part = grad_prod
    grad_a = jnp.einsum(
        "ijc,jkc->ikc",
        grad_part,
        lax.all_gather(side_b, "dap", axis=0, tiled=True),
        preferred_element_type=jnp.float32,
    )
    grad_part = grad_prod
    grad_b = lax.psum_scatter(
        jnp.einsum("ijc,ikc->jkc", grad_part, side_a, preferred_element_type=jnp.float32).astype(
            jnp.bfloat16
        ),
        "dap",
        scatter_dimension=0,
        tiled=True,
    ).astype(jnp.float32)
    grad_gate = cot_f32 * tri_update * gating * (1.0 - gating)
    grad_proj = jnp.concatenate([mask_f * grad_a, mask_f * grad_b, grad_gate], -1).astype(
        jnp.bfloat16
    )
    grad_input = jnp.dot(
        grad_proj.reshape(-1, 3 * pair_chans),
        edges_gate_factor_matrix.T,
        preferred_element_type=jnp.float32,
    ).reshape(res_rows, width, pair_chans)
    pair_gradient = cot_f32 + norm_back(pair_mid.astype(jnp.float32), grad_input)
    return (family_after_heads, pair_output, pair_gradient)


F32 = jnp.float32
BF16 = jnp.bfloat16
NT = (((1,), (1,)), ((), ()))


def dot(a, b):
    return jnp.dot(a, b, preferred_element_type=F32)


def dot_nt(a, b):
    return lax.dot_general(a, b, NT, preferred_element_type=F32)


def iota(shape, dim):
    return lax.broadcasted_iota(jnp.int32, shape, dim)


def pack_kernel(width, edge_ref, weight_ref, loss_ref, mask_ref, send_ref, mask_s):
    rows, chans = edge_ref.shape
    heads = weight_ref.shape[0]
    own = rows // width
    lanes = heads * width
    send_ref[:rows, :] = edge_ref[...]
    send_ref[rows : 2 * rows, :] = loss_ref[...]
    mask_s[...] = jnp.zeros(mask_s.shape, F32)
    mask_s[:own, :] = mask_ref[...].astype(F32)
    eye = (iota((width, width), 0) == iota((width, width), 1)).astype(F32).astype(BF16)
    base = 2 * rows
    send_ref[base : base + width, :] = dot_nt(eye, mask_s[...].astype(BF16)).astype(BF16)
    normed = standardize_features(edge_ref[...].astype(F32)).astype(BF16)
    spread = (iota((heads, lanes), 0) == iota((heads, lanes), 1) // width).astype(F32)
    weight = lax.dot_general(
        weight_ref[...], spread.astype(BF16), (((0,), (0,)), ((), ())), preferred_element_type=F32
    ).astype(BF16)
    every = dot(normed, weight)
    keep = iota((rows, lanes), 0) % width == iota((rows, lanes), 1) % width
    picked = jnp.where(keep, every, 0.0).astype(BF16)
    packed = jnp.zeros((16, 128), F32)
    for t in range(lanes // 128):
        place = iota((16, rows), 0) == 8 * t + iota((16, rows), 1) // width
        packed = packed + dot(
            place.astype(F32).astype(BF16), picked[:, 128 * t : 128 * t + 128]
        )
    send_ref[base + width :, :] = packed.astype(BF16)


def attention_kernel(
    width,
    heads,
    own,
    family_ref,
    all_ref,
    project_ref,
    merge_ref,
    factor_ref,
    family_out_ref,
    send_ref,
    query_s,
    key_s,
    value_s,
    weight_s,
    row_s,
):
    rows, depth = family_ref.shape
    seqs = rows // width
    tiles = depth // 128
    group = 128 // width
    source = family_ref[...].astype(F32)
    normed = standardize_features(source).astype(BF16)
    query_s[...] = dot(normed, project_ref[:, :depth]).astype(BF16)
    key_s[...] = dot(normed, project_ref[:, depth : 2 * depth]).astype(BF16)
    value_s[...] = dot(normed, project_ref[:, 2 * depth : 3 * depth]).astype(BF16)
    gating = jax.nn.sigmoid(dot(normed, project_ref[:, 3 * depth :]))
    same = (iota((128, 128), 0) // width == iota((128, 128), 1) // width).astype(F32).astype(BF16)
    lane_group = iota((rows, 128), 1) // width
    scale = 1.0 / math.sqrt(depth // heads)
    gated = []
    base = all_ref.shape[1] - 16
    biases = jnp.concatenate([all_ref[d, base:, :] for d in range(all_ref.shape[0])], 0)
    for t in range(tiles):
        cols = slice(128 * t, 128 * t + 128)
        row = iota((width, biases.shape[0]), 0)
        take = iota((width, biases.shape[0]), 1) == 16 * (row // own) + 8 * t + row % own
        bias = dot(take.astype(F32).astype(BF16), biases)
        parts = []
        for s in range(seqs):
            span = slice(width * s, width * s + width)
            keys = jnp.concatenate([key_s[span, cols]] * group, 0) * same
            parts.append(dot_nt(query_s[span, cols], keys) * scale + bias)
        logits = jnp.concatenate(parts, 0)
        top = jnp.full(logits.shape, -jnp.inf, F32)
        for h in range(group):
            best = jnp.max(
                jnp.where(lane_group == h, logits, -jnp.inf), axis=-1, keepdims=True
            )
            top = jnp.where(lane_group == h, best, top)
        weight_s[...] = jnp.exp(logits - top).astype(BF16)
        total = dot(weight_s[...], same)
        parts = []
        for s in range(seqs):
            span = slice(width * s, width * s + width)
            values = jnp.concatenate([value_s[span, cols]] * group, 0) * same
            parts.append(dot(weight_s[span, :], values))
        mixed = jnp.concatenate(parts, 0) / total
        gated.append((gating[:, cols] * mixed).astype(BF16))
    after = (source + dot(jnp.concatenate(gated, 1), merge_ref[...])).astype(BF16)
    family_out_ref[...] = after
    ready = standardize_features(after.astype(F32))
    for t in range(tiles):
        row_s[rows * t : rows * (t + 1), :] = ready[:, 128 * t : 128 * t + 128]
    hidden = factor_ref.shape[0] // 2
    placed = jnp.zeros((width // group * seqs, 256), F32)
    for q in range(group):
        picked = jnp.concatenate(
            [
                jnp.concatenate(
                    [
                        row_s[pl.ds(rows * t + group * g + q, seqs, stride=width), :]
                        for g in range(width // group)
                    ],
                    0,
                )
                for t in range(tiles)
            ],
            1,
        ).astype(BF16)
        both = dot_nt(picked, factor_ref[...]).astype(BF16)
        src = iota((2 * hidden, 256), 0)
        dst = iota((2 * hidden, 256), 1)
        goal = src % hidden + hidden * q + 128 * (src // hidden)
        placed = placed + dot(both, (goal == dst).astype(F32).astype(BF16))
    groups = width // group
    for g in range(groups):
        span = slice(seqs * g, seqs * g + seqs)
        send_ref[seqs * g : seqs * (g + 1), :] = placed[span, :128].astype(BF16)
        base = seqs * groups
        send_ref[base + seqs * g : base + seqs * (g + 1), :] = placed[span, 128:].astype(BF16)


def block_transpose(blocks, step):
    lane = iota(blocks[0].shape, 1)
    for shift in (2 * step, step):
        low = lane // shift % 2 == 0
        stride = shift // step
        out = list(blocks)
        for q in range(len(blocks)):
            if q // stride % 2 == 0:
                x, y = blocks[q], blocks[q + stride]
                up = pltpu.roll(y, shift, 1)
                down = pltpu.roll(x, 4 * step - shift, 1)
                out[q] = jnp.where(low, x, up)
                out[q + stride] = jnp.where(low, down, y)
        blocks = out
    return blocks


def pair_kernel(
    axis,
    width,
    own,
    hidden,
    seqs,
    sides_ref,
    all_ref,
    covariance_ref,
    edges_ref,
    cycle_ref,
    out_ref,
    grad_ref,
    turn_s,
    right_s,
    cov_s,
    cov_bf_s,
    mid_s,
    a_s,
    b_s,
    loss_s,
    own_a_s,
    own_b_s,
    tri_s,
):
    me = lax.axis_index(axis)
    n = all_ref.shape[0]
    group = 128 // hidden
    groups = width // group
    pairs = own * width
    chans = 128

    def gathered(first, count):
        return jnp.concatenate([sides_ref[d, first : first + count, :] for d in range(n)], 0)

    for g in range(groups):
        right = gathered(seqs * groups + seqs * g, seqs).astype(F32)
        turn_s[128 * g : 128 * g + 128, :] = right.T
    cov_s[...] = covariance_ref[...].astype(F32)
    for b in range(hidden):
        span = slice(width * b, width * b + width)
        right_s[span, :] = turn_s[pl.ds(b, width, stride=hidden), :].astype(BF16)
        span = slice(hidden * b, hidden * b + hidden)
        cov_bf_s[span, :] = cov_s[pl.ds(b, hidden, stride=hidden), :].astype(BF16)
    for g in range(groups):
        left = gathered(seqs * g, seqs)
        outer = dot(right_s[...], left)
        columns = []
        for p in range(hidden // group):
            first = 128 * p
            columns.append(
                block_transpose(
                    [outer[first + width * q : first + width * (q + 1), :] for q in range(group)],
                    hidden,
                )
            )
        flat = jnp.concatenate(
            [jnp.concatenate([c[i] for c in columns], 1) for i in range(group)], 0
        )
        high = flat.astype(BF16)
        low = (flat - high.astype(F32)).astype(BF16)
        added = (dot(high, cov_bf_s[...]) + dot(low, cov_bf_s[...])) * (1.0 / (seqs * n))
        span = slice(pairs * g, pairs * (g + 1))
        edge = all_ref[g, :pairs, :].astype(F32)
        mid = (edge + added).astype(BF16).astype(F32)
        mid_s[span, :] = mid
        normed = standardize_features(mid).astype(BF16)
        sides = dot(normed, edges_ref[:, : 2 * chans])
        mask = all_ref[g, 2 * pairs : 2 * pairs + width, :].astype(F32)
        keep = jnp.concatenate(
            [jnp.broadcast_to(mask[:, r : r + 1], (width, chans)) for r in range(own)], 0
        )
        a_s[span, :] = (keep * sides[:, :chans]).astype(BF16).astype(F32)
        b_s[span, :] = (keep * sides[:, chans:]).astype(BF16).astype(F32)
        loss_s[span, :] = all_ref[g, pairs : 2 * pairs, :].astype(F32)

    rows = pl.ds(pl.multiple_of(me * pairs, pairs), pairs)

    def rows_and_columns(ref):
        return jnp.concatenate(
            [ref[rows, :]] + [ref[pl.ds(me * own + r, width, stride=width), :] for r in range(own)],
            0,
        )

    mid = rows_and_columns(mid_s)
    loss = rows_and_columns(loss_s)
    own_a_s[...] = a_s[rows, :]
    own_b_s[...] = b_s[rows, :]
    normed = standardize_features(mid).astype(BF16)
    gating = jax.nn.sigmoid(dot(normed, edges_ref[:, 2 * chans :]))

    def row(ref, r):
        return jnp.broadcast_to(ref[r : r + 1, :], (width, chans))

    acc = [jnp.zeros((width, chans), F32) for _ in range(2 * own)]
    for k in range(width):
        b_k = b_s[pl.ds(k, width, stride=width), :]
        a_k = a_s[pl.ds(k, width, stride=width), :]
        for r in range(own):
            acc[r] = acc[r] + row(own_a_s, width * r + k) * b_k
            acc[own + r] = acc[own + r] + row(own_b_s, width * r + k) * a_k
    tri = jnp.concatenate(acc, 0)
    center = tri - jnp.mean(tri, -1, keepdims=True)
    scale_inv = lax.rsqrt(jnp.mean(center * center, -1, keepdims=True) + EPSILON)
    unit = center * scale_inv
    update = dot(unit[:pairs].astype(BF16), cycle_ref[...])
    out_ref[...] = (mid[:pairs] + gating[:pairs] * update).astype(BF16)
    grad_normed = dot_nt((loss * gating).astype(BF16), cycle_ref[...])
    tri_s[...] = (
        (
            scale_inv
            * (
                grad_normed
                - jnp.mean(grad_normed, -1, keepdims=True)
                - unit * jnp.mean(grad_normed * unit, -1, keepdims=True)
            )
        )
        .astype(BF16)
        .astype(F32)
    )
    acc = [jnp.zeros((width, chans), F32) for _ in range(2 * own)]
    for j in range(width):
        span = slice(width * j, width * j + width)
        b_j = b_s[span, :]
        a_j = a_s[span, :]
        for r in range(own):
            acc[r] = acc[r] + row(tri_s, width * r + j) * b_j
            acc[own + r] = acc[own + r] + row(tri_s, pairs + width * r + j) * a_j
    mask = all_ref[me, 2 * pairs : 2 * pairs + width, :].astype(F32)
    keep = jnp.concatenate(
        [jnp.broadcast_to(mask[:, r : r + 1], (width, chans)) for r in range(own)], 0
    )
    gate_own = gating[:pairs]
    grad_gate = loss[:pairs] * update * gate_own * (1.0 - gate_own)
    grad_proj = jnp.concatenate(
        [
            keep * jnp.concatenate(acc[:own], 0),
            keep * jnp.concatenate(acc[own:], 0),
            grad_gate,
        ],
        1,
    ).astype(BF16)
    grad_input = dot_nt(grad_proj, edges_ref[...])
    grad_ref[...] = loss[:pairs] + norm_back(mid[:pairs], grad_input)


def body_resident(
    family_matrix,
    edge_matrix,
    edge_validity,
    query_key_value_gate_matrix,
    logit_offset_matrix,
    heads_merge_matrix,
    left_right_factor_matrix,
    covariance_merge_matrix,
    edges_gate_factor_matrix,
    cycle_merge_matrix,
    loss_sensitivity,
):
    seqs, width, depth = family_matrix.shape
    own, _, chans = edge_matrix.shape
    heads = logit_offset_matrix.shape[1]
    hidden = left_right_factor_matrix.shape[1] // 2
    pairs = own * width
    every = width * width
    edge = edge_matrix.reshape(pairs, chans)
    loss = loss_sensitivity.reshape(pairs, chans)
    vmem = pl.BlockSpec(memory_space=pltpu.VMEM)
    packed = pl.pallas_call(
        functools.partial(pack_kernel, width),
        out_shape=jax.ShapeDtypeStruct((2 * pairs + width + 16, chans), BF16),
        in_specs=[vmem] * 4,
        out_specs=vmem,
        scratch_shapes=[pltpu.VMEM((128, width), F32)],
        name="pack_pairs",
    )(edge, logit_offset_matrix.T, loss, edge_validity)
    packed_all = lax.all_gather(packed, "dap", axis=0, tiled=False)
    family_out, send = pl.pallas_call(
        functools.partial(attention_kernel, width, heads, own),
        out_shape=(
            jax.ShapeDtypeStruct((seqs * width, depth), BF16),
            jax.ShapeDtypeStruct((2 * seqs * width * hidden // 128, 128), BF16),
        ),
        in_specs=[vmem] * 5,
        out_specs=(vmem, vmem),
        scratch_shapes=[pltpu.VMEM((seqs * width, depth), BF16)] * 3
        + [
            pltpu.VMEM((seqs * width, 128), BF16),
            pltpu.VMEM((seqs * width * depth // 128, 128), F32),
        ],
        name="row_attention",
    )(
        family_matrix.reshape(seqs * width, depth),
        packed_all,
        query_key_value_gate_matrix,
        heads_merge_matrix,
        left_right_factor_matrix.T,
    )
    gathered = lax.all_gather(send, "dap", axis=0, tiled=False)
    pair_out, pair_grad = pl.pallas_call(
        functools.partial(pair_kernel, "dap", width, own, hidden, seqs),
        out_shape=(
            jax.ShapeDtypeStruct((pairs, chans), BF16),
            jax.ShapeDtypeStruct((pairs, chans), F32),
        ),
        in_specs=[vmem] * 5,
        out_specs=(vmem, vmem),
        scratch_shapes=[
            pltpu.VMEM((hidden * width, 128), F32),
            pltpu.VMEM((hidden * width, 128), BF16),
            pltpu.VMEM((hidden * hidden, chans), F32),
            pltpu.VMEM((hidden * hidden, chans), BF16),
            pltpu.VMEM((every, chans), F32),
            pltpu.VMEM((every, chans), F32),
            pltpu.VMEM((every, chans), F32),
            pltpu.VMEM((every, chans), F32),
            pltpu.VMEM((pairs, chans), F32),
            pltpu.VMEM((pairs, chans), F32),
            pltpu.VMEM((2 * pairs, chans), F32),
        ],
        name="pair_update",
    )(gathered, packed_all, covariance_merge_matrix, edges_gate_factor_matrix, cycle_merge_matrix)
    return (
        family_out.reshape(seqs, width, depth),
        pair_out.reshape(own, width, chans),
        pair_grad.reshape(own, width, chans),
    )


def fits_resident(dap, family, edge, logit, factor):
    seqs, width, depth = family.shape
    own, _, chans = edge.shape
    return (
        own * dap == width
        and width == 32
        and factor.shape[1] == 64
        and depth == 32 * logit.shape[1]
        and depth % 128 == 0
        and chans == 128
        and own * width == 128
        and seqs % 16 == 0
        and seqs * dap == 128
    )


def body(*args):
    dap = lax.axis_size("dap")
    if fits_resident(dap, args[0], args[1], args[4], args[6]):
        return body_resident(*args)
    return body_general(*args)


def solution(mesh):
    in_specs = (
        P(("dp", "dap"), None, None),
        P(("dp", "dap"), None, None),
        P(("dp", "dap"), None),
        P(),
        P(),
        P(),
        P(),
        P(),
        P(),
        P(),
        P(("dp", "dap"), None, None),
    )
    out_specs = (
        P(("dp", "dap"), None, None),
        P(("dp", "dap"), None, None),
        P(("dp", "dap"), None, None),
    )
    return jax.shard_map(body, mesh=mesh, in_specs=in_specs, out_specs=out_specs, check_vma=False)
```

```python
import functools
import math

import jax
import jax.numpy as jnp
from jax import lax
from jax.experimental import pallas as pl
from jax.experimental.pallas import tpu as pltpu
from jax.sharding import PartitionSpec as P

EPSILON = 1e-05


def standardize_features(values):
    center = values - jnp.mean(values, -1, keepdims=True)
    scale_inv = lax.rsqrt(jnp.mean(center * center, -1, keepdims=True) + EPSILON)
    return center * scale_inv


def norm_back(values, grad_out):
    center = values - jnp.mean(values, -1, keepdims=True)
    scale_inv = lax.rsqrt(jnp.mean(center * center, -1, keepdims=True) + EPSILON)
    standardized_source = center * scale_inv
    return scale_inv * (
        grad_out
        - jnp.mean(grad_out, -1, keepdims=True)
        - standardized_source * jnp.mean(grad_out * standardized_source, -1, keepdims=True)
    )


def lateral_heads_mixing(
    family_shard_slice, logit_offset_whole, query_key_value_gate_matrix, heads_merge_matrix
):
    homolog_number, amino_number, feature_depth = family_shard_slice.shape
    head_count = logit_offset_whole.shape[1]
    head_size = feature_depth // head_count
    standardized_source = standardize_features(family_shard_slice.astype(jnp.float32)).astype(
        jnp.bfloat16
    )
    projected = jnp.dot(
        standardized_source.reshape(-1, feature_depth),
        query_key_value_gate_matrix,
        preferred_element_type=jnp.float32,
    )
    projected = projected.reshape(homolog_number, amino_number, 4 * feature_depth)
    shape_heads = (homolog_number, amino_number, head_count, head_size)
    queries = projected[..., :feature_depth].astype(jnp.bfloat16).reshape(shape_heads)
    key_rows = (
        projected[..., feature_depth : 2 * feature_depth].astype(jnp.bfloat16).reshape(shape_heads)
    )
    value_rows = (
        projected[..., 2 * feature_depth : 3 * feature_depth]
        .astype(jnp.bfloat16)
        .reshape(shape_heads)
    )
    gating = jax.nn.sigmoid(projected[..., 3 * feature_depth :])
    logits = jnp.einsum("sihd,sjhd->sihj", queries, key_rows, preferred_element_type=jnp.float32)
    logits = logits / math.sqrt(head_size) + logit_offset_whole.astype(jnp.float32)[None]
    weights = jax.nn.softmax(logits, axis=-1).astype(jnp.bfloat16)
    mixed = jnp.einsum("sihj,sjhd->sihd", weights, value_rows, preferred_element_type=jnp.float32)
    gated = (gating * mixed.reshape(homolog_number, amino_number, feature_depth)).astype(
        jnp.bfloat16
    )
    edge_increment = jnp.dot(
        gated.reshape(-1, feature_depth), heads_merge_matrix, preferred_element_type=jnp.float32
    )
    return (
        family_shard_slice.astype(jnp.float32)
        + edge_increment.reshape(homolog_number, amino_number, feature_depth)
    ).astype(jnp.bfloat16)


def pair_projection_step(alignment_rows, left_right_factor_matrix):
    standardized_source = standardize_features(alignment_rows.astype(jnp.float32)).astype(
        jnp.bfloat16
    )
    edge_result = jnp.dot(
        standardized_source.reshape(-1, alignment_rows.shape[2]),
        left_right_factor_matrix,
        preferred_element_type=jnp.float32,
    )
    return edge_result.reshape(alignment_rows.shape[0], alignment_rows.shape[1], -1).astype(
        jnp.bfloat16
    )


def body_general(
    family_matrix,
    edge_matrix,
    edge_validity,
    query_key_value_gate_matrix,
    logit_offset_matrix,
    heads_merge_matrix,
    left_right_factor_matrix,
    covariance_merge_matrix,
    edges_gate_factor_matrix,
    cycle_merge_matrix,
    loss_sensitivity,
):
    res_rows, width, pair_chans = edge_matrix.shape
    pair_normed = standardize_features(edge_matrix.astype(jnp.float32)).astype(jnp.bfloat16)
    bias_local = jnp.einsum(
        "ijc,ch->ihj", pair_normed, logit_offset_matrix, preferred_element_type=jnp.float32
    ).astype(jnp.bfloat16)
    logit_offset_whole = lax.all_gather(bias_local, "dap", axis=0, tiled=True)
    homolog_lines = family_matrix.shape[0]
    homolog_subset = math.gcd(homolog_lines, 8)
    batched_lines = family_matrix.reshape(
        homolog_lines // homolog_subset,
        homolog_subset,
        family_matrix.shape[1],
        family_matrix.shape[2],
    )
    family_after_heads = lax.map(
        lambda family_shard_slice: lateral_heads_mixing(
            family_shard_slice, logit_offset_whole, query_key_value_gate_matrix, heads_merge_matrix
        ),
        batched_lines,
    ).reshape(family_matrix.shape)
    hidden = left_right_factor_matrix.shape[1] // 2
    weight_f32 = covariance_merge_matrix.astype(jnp.float32)
    alignment_columns = lax.all_to_all(
        family_after_heads, "dap", split_axis=1, concat_axis=0, tiled=True
    )
    edge_result = pair_projection_step(alignment_columns, left_right_factor_matrix)
    left_part = edge_result[..., :hidden]
    right_part = edge_result[..., hidden:]
    sequence_full_count = alignment_columns.shape[0]
    shard_in = lax.all_gather(right_part, "dap", axis=1, tiled=True)
    outer_sum = (
        jnp.einsum("sia,sjb->ijab", left_part, shard_in, preferred_element_type=jnp.float32)
        / sequence_full_count
    )
    row_count = shard_in.shape[1]
    flat = outer_sum.reshape(res_rows * row_count, hidden * hidden)
    edge_increment = jnp.dot(flat, weight_f32, precision=lax.Precision.HIGHEST).reshape(
        res_rows, row_count, pair_chans
    )
    pair_mid = (edge_matrix.astype(jnp.float32) + edge_increment).astype(jnp.bfloat16)
    tri_normed = standardize_features(pair_mid.astype(jnp.float32)).astype(jnp.bfloat16)
    tri_proj = jnp.dot(
        tri_normed.reshape(-1, pair_chans),
        edges_gate_factor_matrix,
        preferred_element_type=jnp.float32,
    ).reshape(res_rows, width, 3 * pair_chans)
    mask_f = edge_validity.astype(jnp.float32)[..., None]
    side_a = (mask_f * tri_proj[..., :pair_chans]).astype(jnp.bfloat16)
    side_b = (mask_f * tri_proj[..., pair_chans : 2 * pair_chans]).astype(jnp.bfloat16)
    gating = jax.nn.sigmoid(tri_proj[..., 2 * pair_chans :])
    tri_prod = jnp.einsum(
        "ikc,jkc->ijc",
        side_a,
        lax.all_gather(side_b, "dap", axis=0, tiled=True),
        preferred_element_type=jnp.float32,
    )
    prod_normed = standardize_features(tri_prod).astype(jnp.bfloat16)
    tri_update = jnp.dot(
        prod_normed.reshape(-1, pair_chans), cycle_merge_matrix, preferred_element_type=jnp.float32
    ).reshape(res_rows, width, pair_chans)
    pair_output = (pair_mid.astype(jnp.float32) + gating * tri_update).astype(jnp.bfloat16)
    cot_f32 = loss_sensitivity.astype(jnp.float32)
    grad_update = (cot_f32 * gating).astype(jnp.bfloat16)
    grad_normed = jnp.dot(
        grad_update.reshape(-1, pair_chans),
        cycle_merge_matrix.T,
        preferred_element_type=jnp.float32,
    ).reshape(res_rows, width, pair_chans)
    grad_prod = norm_back(tri_prod, grad_normed).astype(jnp.bfloat16)
    grad_part = grad_prod
    grad_a = jnp.einsum(
        "ijc,jkc->ikc",
        grad_part,
        lax.all_gather(side_b, "dap", axis=0, tiled=True),
        preferred_element_type=jnp.float32,
    )
    grad_part = grad_prod
    grad_b = lax.psum_scatter(
        jnp.einsum("ijc,ikc->jkc", grad_part, side_a, preferred_element_type=jnp.float32).astype(
            jnp.bfloat16
        ),
        "dap",
        scatter_dimension=0,
        tiled=True,
    ).astype(jnp.float32)
    grad_gate = cot_f32 * tri_update * gating * (1.0 - gating)
    grad_proj = jnp.concatenate([mask_f * grad_a, mask_f * grad_b, grad_gate], -1).astype(
        jnp.bfloat16
    )
    grad_input = jnp.dot(
        grad_proj.reshape(-1, 3 * pair_chans),
        edges_gate_factor_matrix.T,
        preferred_element_type=jnp.float32,
    ).reshape(res_rows, width, pair_chans)
    pair_gradient = cot_f32 + norm_back(pair_mid.astype(jnp.float32), grad_input)
    return (family_after_heads, pair_output, pair_gradient)


F32 = jnp.float32
BF16 = jnp.bfloat16
NT = (((1,), (1,)), ((), ()))


def dot(a, b):
    return jnp.dot(a, b, preferred_element_type=F32)


def dot_nt(a, b):
    return lax.dot_general(a, b, NT, preferred_element_type=F32)


def iota(shape, dim):
    return lax.broadcasted_iota(jnp.int32, shape, dim)


def pack_kernel(width, edge_ref, weight_ref, loss_ref, mask_ref, send_ref, mask_s):
    rows, chans = edge_ref.shape
    heads = weight_ref.shape[0]
    own = rows // width
    lanes = heads * width
    send_ref[:rows, :] = edge_ref[...]
    send_ref[rows : 2 * rows, :] = loss_ref[...]
    mask_s[...] = jnp.zeros(mask_s.shape, F32)
    mask_s[:own, :] = mask_ref[...].astype(F32)
    eye = (iota((width, width), 0) == iota((width, width), 1)).astype(F32).astype(BF16)
    base = 2 * rows
    send_ref[base : base + width, :] = dot_nt(eye, mask_s[...].astype(BF16)).astype(BF16)
    normed = standardize_features(edge_ref[...].astype(F32)).astype(BF16)
    spread = (iota((heads, lanes), 0) == iota((heads, lanes), 1) // width).astype(F32)
    weight = lax.dot_general(
        weight_ref[...], spread.astype(BF16), (((0,), (0,)), ((), ())), preferred_element_type=F32
    ).astype(BF16)
    every = dot(normed, weight)
    keep = iota((rows, lanes), 0) % width == iota((rows, lanes), 1) % width
    picked = jnp.where(keep, every, 0.0).astype(BF16)
    packed = jnp.zeros((16, 128), F32)
    for t in range(lanes // 128):
        place = iota((16, rows), 0) == 8 * t + iota((16, rows), 1) // width
        packed = packed + dot(
            place.astype(F32).astype(BF16), picked[:, 128 * t : 128 * t + 128]
        )
    send_ref[base + width :, :] = packed.astype(BF16)


def attention_kernel(
    width,
    heads,
    own,
    family_ref,
    all_ref,
    project_ref,
    merge_ref,
    factor_ref,
    family_out_ref,
    send_ref,
    query_s,
    key_s,
    value_s,
    weight_s,
    row_s,
    turn_s,
    line_s,
):
    rows, depth = family_ref.shape
    seqs = rows // width
    tiles = depth // 128
    group = 128 // width
    source = family_ref[...].astype(F32)
    normed = standardize_features(source).astype(BF16)
    query_s[...] = dot(normed, project_ref[:, :depth]).astype(BF16)
    key_s[...] = dot(normed, project_ref[:, depth : 2 * depth]).astype(BF16)
    value_s[...] = dot(normed, project_ref[:, 2 * depth : 3 * depth]).astype(BF16)
    gating = jax.nn.sigmoid(dot(normed, project_ref[:, 3 * depth :]))
    same = (iota((128, 128), 0) // width == iota((128, 128), 1) // width).astype(F32).astype(BF16)
    lane_group = iota((rows, 128), 1) // width
    scale = 1.0 / math.sqrt(depth // heads)
    gated = []
    base = all_ref.shape[1] - 16
    biases = jnp.concatenate([all_ref[d, base:, :] for d in range(all_ref.shape[0])], 0)
    for t in range(tiles):
        cols = slice(128 * t, 128 * t + 128)
        row = iota((width, biases.shape[0]), 0)
        take = iota((width, biases.shape[0]), 1) == 16 * (row // own) + 8 * t + row % own
        bias = dot(take.astype(F32).astype(BF16), biases)
        parts = []
        for s in range(seqs):
            span = slice(width * s, width * s + width)
            keys = jnp.concatenate([key_s[span, cols]] * group, 0) * same
            parts.append(dot_nt(query_s[span, cols], keys) * scale + bias)
        logits = jnp.concatenate(parts, 0)
        top = jnp.full(logits.shape, -jnp.inf, F32)
        for h in range(group):
            best = jnp.max(
                jnp.where(lane_group == h, logits, -jnp.inf), axis=-1, keepdims=True
            )
            top = jnp.where(lane_group == h, best, top)
        weight_s[...] = jnp.exp(logits - top).astype(BF16)
        total = dot(weight_s[...], same)
        parts = []
        for s in range(seqs):
            span = slice(width * s, width * s + width)
            values = jnp.concatenate([value_s[span, cols]] * group, 0) * same
            parts.append(dot(weight_s[span, :], values))
        mixed = jnp.concatenate(parts, 0) / total
        gated.append((gating[:, cols] * mixed).astype(BF16))
    after = (source + dot(jnp.concatenate(gated, 1), merge_ref[...])).astype(BF16)
    family_out_ref[...] = after
    ready = standardize_features(after.astype(F32)).astype(BF16)
    hidden = factor_ref.shape[0] // 2
    groups = width // group
    row_s[:, : 2 * hidden] = dot_nt(ready, factor_ref[...])
    placed = jnp.zeros((groups * seqs, 128), F32)
    for q in range(group):
        picked = jnp.concatenate(
            [row_s[pl.ds(group * g + q, seqs, stride=width), :] for g in range(groups)], 0
        )[:, :hidden].astype(BF16)
        here = iota((hidden, 128), 0) + hidden * q == iota((hidden, 128), 1)
        placed = placed + dot(picked, here.astype(F32).astype(BF16))
    for g in range(groups):
        send_ref[seqs * g : seqs * (g + 1), :] = placed[seqs * g : seqs * (g + 1), :].astype(BF16)
    turned = dot_nt(factor_ref[hidden : 2 * hidden, :], ready)
    for k in range(rows // 128):
        turn_s[hidden * k : hidden * (k + 1), :] = turned[:, 128 * k : 128 * k + 128]
    chunks = hidden // group
    for k in range(rows // 128):
        blocks = [
            turn_s[pl.ds(hidden * k + q, chunks, stride=group), :] for q in range(group)
        ]
        for p, block in enumerate(block_transpose(blocks, width)):
            first = chunks * (group * k + p)
            line_s[first : first + chunks, :] = block
    base = seqs * groups
    for g in range(chunks):
        send_ref[base + seqs * g : base + seqs * (g + 1), :] = line_s[
            pl.ds(g, seqs, stride=chunks), :
        ].astype(BF16)


def block_transpose(blocks, step):
    lane = iota(blocks[0].shape, 1)
    for shift in (2 * step, step):
        low = lane // shift % 2 == 0
        stride = shift // step
        out = list(blocks)
        for q in range(len(blocks)):
            if q // stride % 2 == 0:
                x, y = blocks[q], blocks[q + stride]
                up = pltpu.roll(y, shift, 1)
                down = pltpu.roll(x, 4 * step - shift, 1)
                out[q] = jnp.where(low, x, up)
                out[q + stride] = jnp.where(low, down, y)
        blocks = out
    return blocks


def average(values, weights):
    high = values.astype(BF16)
    low = (values - high.astype(F32)).astype(BF16)
    return dot(jnp.concatenate([high, low], 1), weights)


def center_and_scale(values, weights):
    center = values - average(values, weights)
    return center, lax.rsqrt(average(center * center, weights) + EPSILON)


def merge_rows(parts):
    row = iota(parts[0].shape, 0)
    step = 1
    while len(parts) > 1:
        low = row // step % 2 == 0
        parts = [
            jnp.where(low, x, y) + pltpu.roll(jnp.where(low, y, x), step, 0)
            for x, y in zip(parts[::2], parts[1::2])
        ]
        step *= 2
    return parts[0]


def pair_kernel(
    axis,
    width,
    own,
    hidden,
    seqs,
    sides_ref,
    all_ref,
    covariance_ref,
    edges_ref,
    cycle_ref,
    out_ref,
    grad_ref,
    right_s,
    cov_s,
    cov_bf_s,
    flat_s,
    mid_s,
    unit_s,
    scale_s,
    gate_s,
    a_s,
    b_s,
    loss_s,
    tri_s,
):
    me = lax.axis_index(axis)
    n = all_ref.shape[0]
    group = 128 // hidden
    groups = width // group
    chunks = hidden // group
    pairs = own * width
    chans = 128
    total = seqs * n

    def gathered(first):
        return jnp.concatenate([sides_ref[d, first : first + seqs, :] for d in range(n)], 0)

    eye = (iota((128, 128), 0) == iota((128, 128), 1)).astype(F32).astype(BF16)
    for g in range(chunks):
        turned = dot_nt(eye, gathered(seqs * (groups + g))).astype(BF16)
        for q in range(group):
            right_s[width * g : width * (g + 1), total * q : total * (q + 1)] = turned[
                width * q : width * (q + 1), :
            ]
    cov_s[...] = covariance_ref[...].astype(F32)
    for b in range(hidden):
        span = slice(hidden * b, hidden * b + hidden)
        cov_bf_s[span, :] = cov_s[pl.ds(b, hidden, stride=hidden), :].astype(BF16)
    weights = jnp.full((2 * chans, chans), 1.0 / chans, BF16)
    block = iota((total, 128), 1) // hidden
    for g in range(groups):
        left = gathered(seqs * g).astype(F32)
        rolled = [left] + [pltpu.roll(left, hidden * d, 1) for d in range(1, group)]
        for half in range(group // 2):
            columns = []
            for i in (2 * half, 2 * half + 1):
                columns.append(
                    jnp.concatenate(
                        [
                            jnp.where(block == q, rolled[(q - i) % group], 0.0).astype(BF16)
                            for q in range(group)
                        ],
                        0,
                    )
                )
            outer = dot(right_s[...], jnp.concatenate(columns, 1)).astype(BF16)
            for k in range(2):
                i = group * g + 2 * half + k
                for c in range(chunks):
                    flat_s[width * i : width * (i + 1), 128 * c : 128 * c + 128] = outer[
                        width * c : width * (c + 1), 128 * k : 128 * k + 128
                    ]
    part = n * pairs // 2
    spans = [slice(part * h, part * (h + 1)) for h in range(2)]
    added = [dot(flat_s[span, :], cov_bf_s[...]) for span in spans]
    mids = []
    for h, span in enumerate(spans):
        devices = range(n // 2 * h, n // 2 * (h + 1))
        edge = jnp.concatenate([all_ref[d, :pairs, :] for d in devices], 0).astype(F32)
        mids.append((edge + added[h] * (1.0 / total)).astype(BF16))
        mid_s[span, :] = mids[h].astype(F32)
    centers = [mid.astype(F32) - dot(mid, weights[:chans]) for mid in mids]
    scales = [lax.rsqrt(average(c * c, weights) + EPSILON) for c in centers]
    units = [c * scale for c, scale in zip(centers, scales)]
    sides = [dot(unit.astype(BF16), edges_ref[...]) for unit in units]
    for h, span in enumerate(spans):
        scale_s[span, :] = scales[h]
        unit_s[span, :] = units[h]
        gate_s[span, :] = sides[h][:, 2 * chans :]
        for d in range(n // 2):
            g = n // 2 * h + d
            mask = all_ref[g, 2 * pairs : 2 * pairs + width, :].astype(F32)
            keep = jnp.concatenate(
                [jnp.broadcast_to(mask[:, r : r + 1], (width, chans)) for r in range(own)], 0
            )
            here = slice(pairs * d, pairs * (d + 1))
            there = slice(pairs * g, pairs * (g + 1))
            a_s[there, :] = (keep * sides[h][here, :chans]).astype(BF16).astype(F32)
            b_s[there, :] = (keep * sides[h][here, chans : 2 * chans]).astype(BF16).astype(F32)
            loss_s[there, :] = all_ref[g, pairs : 2 * pairs, :].astype(F32)

    rows = pl.ds(pl.multiple_of(me * pairs, pairs), pairs)

    def rows_and_columns(ref):
        return jnp.concatenate(
            [ref[rows, :]] + [ref[pl.ds(me * own + r, width, stride=width), :] for r in range(own)],
            0,
        )

    mid = mid_s[rows, :]
    loss = rows_and_columns(loss_s)
    gating = jax.nn.sigmoid(rows_and_columns(gate_s))
    tri = []
    for fixed, moving in ((a_s, b_s), (b_s, a_s)):
        held = fixed[rows, :]
        for r in range(own):
            mine = [held[width * r + 8 * v : width * r + 8 * v + 8] for v in range(width // 8)]
            for j in range(0, width, 8):
                parts = []
                for jj in range(j, j + 8):
                    prods = [
                        mine[v] * moving[width * jj + 8 * v : width * jj + 8 * v + 8, :]
                        for v in range(width // 8)
                    ]
                    parts.append(functools.reduce(jnp.add, prods))
                tri.append(merge_rows(parts))
    tri = jnp.concatenate(tri, 0)
    center, scale_inv = center_and_scale(tri, weights)
    unit = center * scale_inv
    update = dot(unit[:pairs].astype(BF16), cycle_ref[...])
    out_ref[...] = (mid + gating[:pairs] * update).astype(BF16)
    grad_normed = dot_nt((loss * gating).astype(BF16), cycle_ref[...])
    tri_s[...] = (
        (
            scale_inv
            * (
                grad_normed
                - average(grad_normed, weights)
                - unit * average(grad_normed * unit, weights)
            )
        )
        .astype(BF16)
        .astype(F32)
    )

    def row(ref, r):
        return jnp.broadcast_to(ref[r : r + 1, :], (width, chans))

    acc = [jnp.zeros((width, chans), F32) for _ in range(2 * own)]
    for j in range(width):
        span = slice(width * j, width * j + width)
        b_j = b_s[span, :]
        a_j = a_s[span, :]
        for r in range(own):
            acc[r] = acc[r] + row(tri_s, width * r + j) * b_j
            acc[own + r] = acc[own + r] + row(tri_s, pairs + width * r + j) * a_j
    mask = all_ref[me, 2 * pairs : 2 * pairs + width, :].astype(F32)
    keep = jnp.concatenate(
        [jnp.broadcast_to(mask[:, r : r + 1], (width, chans)) for r in range(own)], 0
    )
    gate_own = gating[:pairs]
    grad_gate = loss[:pairs] * update * gate_own * (1.0 - gate_own)
    grad_proj = jnp.concatenate(
        [
            keep * jnp.concatenate(acc[:own], 0),
            keep * jnp.concatenate(acc[own:], 0),
            grad_gate,
        ],
        1,
    ).astype(BF16)
    grad_input = dot_nt(grad_proj, edges_ref[...])
    scale_inv = scale_s[rows, :]
    unit = unit_s[rows, :]
    grad_ref[...] = loss[:pairs] + scale_inv * (
        grad_input - average(grad_input, weights) - unit * average(grad_input * unit, weights)
    )


def body_resident(
    family_matrix,
    edge_matrix,
    edge_validity,
    query_key_value_gate_matrix,
    logit_offset_matrix,
    heads_merge_matrix,
    left_right_factor_matrix,
    covariance_merge_matrix,
    edges_gate_factor_matrix,
    cycle_merge_matrix,
    loss_sensitivity,
):
    seqs, width, depth = family_matrix.shape
    own, _, chans = edge_matrix.shape
    heads = logit_offset_matrix.shape[1]
    hidden = left_right_factor_matrix.shape[1] // 2
    pairs = own * width
    every = width * width
    edge = edge_matrix.reshape(pairs, chans)
    loss = loss_sensitivity.reshape(pairs, chans)
    vmem = pl.BlockSpec(memory_space=pltpu.VMEM)
    packed = pl.pallas_call(
        functools.partial(pack_kernel, width),
        out_shape=jax.ShapeDtypeStruct((2 * pairs + width + 16, chans), BF16),
        in_specs=[vmem] * 4,
        out_specs=vmem,
        scratch_shapes=[pltpu.VMEM((128, width), F32)],
        name="pack_pairs",
    )(edge, logit_offset_matrix.T, loss, edge_validity)
    packed_all = lax.all_gather(packed, "dap", axis=0, tiled=False)
    family_out, send = pl.pallas_call(
        functools.partial(attention_kernel, width, heads, own),
        out_shape=(
            jax.ShapeDtypeStruct((seqs * width, depth), BF16),
            jax.ShapeDtypeStruct((2 * seqs * width * hidden // 128, 128), BF16),
        ),
        in_specs=[vmem] * 5,
        out_specs=(vmem, vmem),
        scratch_shapes=[pltpu.VMEM((seqs * width, depth), BF16)] * 3
        + [
            pltpu.VMEM((seqs * width, 128), BF16),
            pltpu.VMEM((seqs * width, 128), F32),
            pltpu.VMEM((seqs * width * hidden // 128, 128), F32),
            pltpu.VMEM((seqs * width * hidden // 128, 128), F32),
        ],
        compiler_params=pltpu.CompilerParams(vmem_limit_bytes=16 << 20),
        name="row_attention",
    )(
        family_matrix.reshape(seqs * width, depth),
        packed_all,
        query_key_value_gate_matrix,
        heads_merge_matrix,
        left_right_factor_matrix.T,
    )
    gathered = lax.all_gather(send, "dap", axis=0, tiled=False)
    pair_out, pair_grad = pl.pallas_call(
        functools.partial(pair_kernel, "dap", width, own, hidden, seqs),
        out_shape=(
            jax.ShapeDtypeStruct((pairs, chans), BF16),
            jax.ShapeDtypeStruct((pairs, chans), F32),
        ),
        in_specs=[vmem] * 5,
        out_specs=(vmem, vmem),
        scratch_shapes=[
            pltpu.VMEM((width * hidden * hidden // 128, 128 // hidden * 128), BF16),
            pltpu.VMEM((hidden * hidden, chans), F32),
            pltpu.VMEM((hidden * hidden, chans), BF16),
            pltpu.VMEM((every, hidden * hidden), BF16),
            pltpu.VMEM((every, chans), F32),
            pltpu.VMEM((every, chans), F32),
            pltpu.VMEM((every, chans), F32),
            pltpu.VMEM((every, chans), F32),
            pltpu.VMEM((every, chans), F32),
            pltpu.VMEM((every, chans), F32),
            pltpu.VMEM((every, chans), F32),
            pltpu.VMEM((2 * pairs, chans), F32),
        ],
        compiler_params=pltpu.CompilerParams(vmem_limit_bytes=16 << 20),
        name="pair_update",
    )(gathered, packed_all, covariance_merge_matrix, edges_gate_factor_matrix, cycle_merge_matrix)
    return (
        family_out.reshape(seqs, width, depth),
        pair_out.reshape(own, width, chans),
        pair_grad.reshape(own, width, chans),
    )


def fits_resident(dap, family, edge, logit, factor):
    seqs, width, depth = family.shape
    own, _, chans = edge.shape
    return (
        own * dap == width
        and width == 32
        and factor.shape[1] == 64
        and depth == 32 * logit.shape[1]
        and depth % 128 == 0
        and chans == 128
        and own * width == 128
        and seqs % 16 == 0
        and seqs * dap == 128
    )


def body(*args):
    dap = lax.axis_size("dap")
    if fits_resident(dap, args[0], args[1], args[4], args[6]):
        return body_resident(*args)
    return body_general(*args)


def solution(mesh):
    in_specs = (
        P(("dp", "dap"), None, None),
        P(("dp", "dap"), None, None),
        P(("dp", "dap"), None),
        P(),
        P(),
        P(),
        P(),
        P(),
        P(),
        P(),
        P(("dp", "dap"), None, None),
    )
    out_specs = (
        P(("dp", "dap"), None, None),
        P(("dp", "dap"), None, None),
        P(("dp", "dap"), None, None),
    )
    return jax.shard_map(body, mesh=mesh, in_specs=in_specs, out_specs=out_specs, check_vma=False)
```

```python
import functools
import math

import jax
import jax.numpy as jnp
from jax import lax
from jax.experimental import pallas as pl
from jax.experimental.pallas import tpu as pltpu
from jax.sharding import PartitionSpec as P

EPSILON = 1e-05


def standardize_features(values):
    center = values - jnp.mean(values, -1, keepdims=True)
    scale_inv = lax.rsqrt(jnp.mean(center * center, -1, keepdims=True) + EPSILON)
    return center * scale_inv


def norm_back(values, grad_out):
    center = values - jnp.mean(values, -1, keepdims=True)
    scale_inv = lax.rsqrt(jnp.mean(center * center, -1, keepdims=True) + EPSILON)
    standardized_source = center * scale_inv
    return scale_inv * (
        grad_out
        - jnp.mean(grad_out, -1, keepdims=True)
        - standardized_source * jnp.mean(grad_out * standardized_source, -1, keepdims=True)
    )


def lateral_heads_mixing(
    family_shard_slice, logit_offset_whole, query_key_value_gate_matrix, heads_merge_matrix
):
    homolog_number, amino_number, feature_depth = family_shard_slice.shape
    head_count = logit_offset_whole.shape[1]
    head_size = feature_depth // head_count
    standardized_source = standardize_features(family_shard_slice.astype(jnp.float32)).astype(
        jnp.bfloat16
    )
    projected = jnp.dot(
        standardized_source.reshape(-1, feature_depth),
        query_key_value_gate_matrix,
        preferred_element_type=jnp.float32,
    )
    projected = projected.reshape(homolog_number, amino_number, 4 * feature_depth)
    shape_heads = (homolog_number, amino_number, head_count, head_size)
    queries = projected[..., :feature_depth].astype(jnp.bfloat16).reshape(shape_heads)
    key_rows = (
        projected[..., feature_depth : 2 * feature_depth].astype(jnp.bfloat16).reshape(shape_heads)
    )
    value_rows = (
        projected[..., 2 * feature_depth : 3 * feature_depth]
        .astype(jnp.bfloat16)
        .reshape(shape_heads)
    )
    gating = jax.nn.sigmoid(projected[..., 3 * feature_depth :])
    logits = jnp.einsum("sihd,sjhd->sihj", queries, key_rows, preferred_element_type=jnp.float32)
    logits = logits / math.sqrt(head_size) + logit_offset_whole.astype(jnp.float32)[None]
    weights = jax.nn.softmax(logits, axis=-1).astype(jnp.bfloat16)
    mixed = jnp.einsum("sihj,sjhd->sihd", weights, value_rows, preferred_element_type=jnp.float32)
    gated = (gating * mixed.reshape(homolog_number, amino_number, feature_depth)).astype(
        jnp.bfloat16
    )
    edge_increment = jnp.dot(
        gated.reshape(-1, feature_depth), heads_merge_matrix, preferred_element_type=jnp.float32
    )
    return (
        family_shard_slice.astype(jnp.float32)
        + edge_increment.reshape(homolog_number, amino_number, feature_depth)
    ).astype(jnp.bfloat16)


def pair_projection_step(alignment_rows, left_right_factor_matrix):
    standardized_source = standardize_features(alignment_rows.astype(jnp.float32)).astype(
        jnp.bfloat16
    )
    edge_result = jnp.dot(
        standardized_source.reshape(-1, alignment_rows.shape[2]),
        left_right_factor_matrix,
        preferred_element_type=jnp.float32,
    )
    return edge_result.reshape(alignment_rows.shape[0], alignment_rows.shape[1], -1).astype(
        jnp.bfloat16
    )


def body_general(
    family_matrix,
    edge_matrix,
    edge_validity,
    query_key_value_gate_matrix,
    logit_offset_matrix,
    heads_merge_matrix,
    left_right_factor_matrix,
    covariance_merge_matrix,
    edges_gate_factor_matrix,
    cycle_merge_matrix,
    loss_sensitivity,
):
    res_rows, width, pair_chans = edge_matrix.shape
    pair_normed = standardize_features(edge_matrix.astype(jnp.float32)).astype(jnp.bfloat16)
    bias_local = jnp.einsum(
        "ijc,ch->ihj", pair_normed, logit_offset_matrix, preferred_element_type=jnp.float32
    ).astype(jnp.bfloat16)
    logit_offset_whole = lax.all_gather(bias_local, "dap", axis=0, tiled=True)
    homolog_lines = family_matrix.shape[0]
    homolog_subset = math.gcd(homolog_lines, 8)
    batched_lines = family_matrix.reshape(
        homolog_lines // homolog_subset,
        homolog_subset,
        family_matrix.shape[1],
        family_matrix.shape[2],
    )
    family_after_heads = lax.map(
        lambda family_shard_slice: lateral_heads_mixing(
            family_shard_slice, logit_offset_whole, query_key_value_gate_matrix, heads_merge_matrix
        ),
        batched_lines,
    ).reshape(family_matrix.shape)
    hidden = left_right_factor_matrix.shape[1] // 2
    weight_f32 = covariance_merge_matrix.astype(jnp.float32)
    alignment_columns = lax.all_to_all(
        family_after_heads, "dap", split_axis=1, concat_axis=0, tiled=True
    )
    edge_result = pair_projection_step(alignment_columns, left_right_factor_matrix)
    left_part = edge_result[..., :hidden]
    right_part = edge_result[..., hidden:]
    sequence_full_count = alignment_columns.shape[0]
    shard_in = lax.all_gather(right_part, "dap", axis=1, tiled=True)
    outer_sum = (
        jnp.einsum("sia,sjb->ijab", left_part, shard_in, preferred_element_type=jnp.float32)
        / sequence_full_count
    )
    row_count = shard_in.shape[1]
    flat = outer_sum.reshape(res_rows * row_count, hidden * hidden)
    edge_increment = jnp.dot(flat, weight_f32, precision=lax.Precision.HIGHEST).reshape(
        res_rows, row_count, pair_chans
    )
    pair_mid = (edge_matrix.astype(jnp.float32) + edge_increment).astype(jnp.bfloat16)
    tri_normed = standardize_features(pair_mid.astype(jnp.float32)).astype(jnp.bfloat16)
    tri_proj = jnp.dot(
        tri_normed.reshape(-1, pair_chans),
        edges_gate_factor_matrix,
        preferred_element_type=jnp.float32,
    ).reshape(res_rows, width, 3 * pair_chans)
    mask_f = edge_validity.astype(jnp.float32)[..., None]
    side_a = (mask_f * tri_proj[..., :pair_chans]).astype(jnp.bfloat16)
    side_b = (mask_f * tri_proj[..., pair_chans : 2 * pair_chans]).astype(jnp.bfloat16)
    gating = jax.nn.sigmoid(tri_proj[..., 2 * pair_chans :])
    tri_prod = jnp.einsum(
        "ikc,jkc->ijc",
        side_a,
        lax.all_gather(side_b, "dap", axis=0, tiled=True),
        preferred_element_type=jnp.float32,
    )
    prod_normed = standardize_features(tri_prod).astype(jnp.bfloat16)
    tri_update = jnp.dot(
        prod_normed.reshape(-1, pair_chans), cycle_merge_matrix, preferred_element_type=jnp.float32
    ).reshape(res_rows, width, pair_chans)
    pair_output = (pair_mid.astype(jnp.float32) + gating * tri_update).astype(jnp.bfloat16)
    cot_f32 = loss_sensitivity.astype(jnp.float32)
    grad_update = (cot_f32 * gating).astype(jnp.bfloat16)
    grad_normed = jnp.dot(
        grad_update.reshape(-1, pair_chans),
        cycle_merge_matrix.T,
        preferred_element_type=jnp.float32,
    ).reshape(res_rows, width, pair_chans)
    grad_prod = norm_back(tri_prod, grad_normed).astype(jnp.bfloat16)
    grad_part = grad_prod
    grad_a = jnp.einsum(
        "ijc,jkc->ikc",
        grad_part,
        lax.all_gather(side_b, "dap", axis=0, tiled=True),
        preferred_element_type=jnp.float32,
    )
    grad_part = grad_prod
    grad_b = lax.psum_scatter(
        jnp.einsum("ijc,ikc->jkc", grad_part, side_a, preferred_element_type=jnp.float32).astype(
            jnp.bfloat16
        ),
        "dap",
        scatter_dimension=0,
        tiled=True,
    ).astype(jnp.float32)
    grad_gate = cot_f32 * tri_update * gating * (1.0 - gating)
    grad_proj = jnp.concatenate([mask_f * grad_a, mask_f * grad_b, grad_gate], -1).astype(
        jnp.bfloat16
    )
    grad_input = jnp.dot(
        grad_proj.reshape(-1, 3 * pair_chans),
        edges_gate_factor_matrix.T,
        preferred_element_type=jnp.float32,
    ).reshape(res_rows, width, pair_chans)
    pair_gradient = cot_f32 + norm_back(pair_mid.astype(jnp.float32), grad_input)
    return (family_after_heads, pair_output, pair_gradient)


F32 = jnp.float32
BF16 = jnp.bfloat16
NT = (((1,), (1,)), ((), ()))


def dot(a, b):
    return jnp.dot(a, b, preferred_element_type=F32)


def dot_nt(a, b):
    return lax.dot_general(a, b, NT, preferred_element_type=F32)


def iota(shape, dim):
    return lax.broadcasted_iota(jnp.int32, shape, dim)


def pack_kernel(
    width, edge_ref, weight_ref, loss_ref, mask_ref, send_ref, edge_s, weight_s, loss_s, mask_s,
    tile_s, sems
):
    copies = [
        pltpu.make_async_copy(source, target, sems.at[k])
        for k, (source, target) in enumerate(
            (
                (edge_ref, edge_s),
                (weight_ref, weight_s),
                (loss_ref, loss_s),
                (mask_ref, mask_s),
            )
        )
    ]
    for copy in copies:
        copy.start()
    for copy in copies:
        copy.wait()
    rows, chans = edge_s.shape
    heads = weight_s.shape[0]
    own = rows // width
    lanes = heads * width
    peers = width // own
    tile_s[...] = jnp.zeros(tile_s.shape, F32)
    tile_s[2 * own : 3 * own, :width] = mask_s[...].astype(F32)
    normed = standardize_features(edge_s[...].astype(F32)).astype(BF16)
    spread = (iota((heads, lanes), 0) == iota((heads, lanes), 1) // width).astype(F32)
    weight = lax.dot_general(
        weight_s[...], spread.astype(BF16), (((0,), (0,)), ((), ())), preferred_element_type=F32
    ).astype(BF16)
    every = dot(normed, weight)
    keep = iota((rows, lanes), 0) % width == iota((rows, lanes), 1) % width
    picked = jnp.where(keep, every, 0.0).astype(BF16)
    packed = tile_s[...]
    for t in range(lanes // 128):
        place = iota((16, rows), 0) == own * t + iota((16, rows), 1) // width
        packed = packed + dot(
            place.astype(F32).astype(BF16), picked[:, 128 * t : 128 * t + 128]
        )
    packed = packed.astype(BF16)
    goal = iota((rows, rows), 0)
    source = goal % own * width + goal // (own * own) * own + goal // own % own
    place = (source == iota((rows, rows), 1)).astype(F32).astype(BF16)
    losses = dot(place, loss_s[...]).astype(BF16)
    for e in range(peers):
        send_ref[32 * e : 32 * e + 16, :] = packed
        send_ref[32 * e + 16 : 32 * e + 32, :] = losses[16 * e : 16 * e + 16]


def project_kernel(
    width,
    heads,
    hidden,
    family_ref,
    project_ref,
    covariance_ref,
    logits_ref,
    value_ref,
    gating_ref,
    cov_ref,
    query_s,
    key_s,
    cov_s,
):
    rows, depth = family_ref.shape
    seqs = rows // width
    group = 128 // width
    normed = standardize_features(family_ref[...].astype(F32)).astype(BF16)
    query_s[...] = dot(normed, project_ref[:, :depth]).astype(BF16)
    key_s[...] = dot(normed, project_ref[:, depth : 2 * depth]).astype(BF16)
    value_ref[...] = dot(normed, project_ref[:, 2 * depth : 3 * depth]).astype(BF16)
    gating_ref[...] = jax.nn.sigmoid(dot(normed, project_ref[:, 3 * depth :]))
    same = (iota((128, 128), 0) // width == iota((128, 128), 1) // width).astype(F32).astype(BF16)
    scale = 1.0 / math.sqrt(depth // heads)
    for t in range(depth // 128):
        cols = slice(128 * t, 128 * t + 128)
        for s in range(seqs):
            span = slice(width * s, width * s + width)
            keys = jnp.concatenate([key_s[span, cols]] * group, 0) * same
            logits_ref[span, cols] = dot_nt(query_s[span, cols], keys) * scale
    cov_s[...] = covariance_ref[...].astype(F32)
    for b in range(hidden):
        span = slice(hidden * b, hidden * b + hidden)
        cov_ref[span, :] = cov_s[pl.ds(b, hidden, stride=hidden), :].astype(BF16)


def attention_kernel(
    width,
    own,
    family_ref,
    got_ref,
    logits_ref,
    value_ref,
    gating_ref,
    merge_ref,
    factor_ref,
    edge_ref,
    family_out_ref,
    send_ref,
    after_s,
    weight_s,
    row_s,
    turn_s,
    line_s,
    sem,
):
    rows, depth = family_ref.shape
    seqs = rows // width
    tiles = depth // 128
    group = 128 // width
    same = (iota((128, 128), 0) // width == iota((128, 128), 1) // width).astype(F32).astype(BF16)
    lane_group = iota((rows, 128), 1) // width
    biases = jnp.concatenate([got_ref[d, :16, :] for d in range(got_ref.shape[0])], 0)
    gated = []
    for t in range(tiles):
        cols = slice(128 * t, 128 * t + 128)
        row = iota((width, biases.shape[0]), 0)
        take = iota((width, biases.shape[0]), 1) == 16 * (row // own) + own * t + row % own
        bias = dot(take.astype(F32).astype(BF16), biases)
        logits = jnp.concatenate(
            [logits_ref[width * s : width * (s + 1), cols] + bias for s in range(seqs)], 0
        )
        top = jnp.full(logits.shape, -jnp.inf, F32)
        for h in range(group):
            best = jnp.max(
                jnp.where(lane_group == h, logits, -jnp.inf), axis=-1, keepdims=True
            )
            top = jnp.where(lane_group == h, best, top)
        weight_s[:, cols] = jnp.exp(logits - top).astype(BF16)
        total = dot(weight_s[:, cols], same)
        parts = []
        for s in range(seqs):
            span = slice(width * s, width * s + width)
            values = jnp.concatenate([value_ref[span, cols]] * group, 0) * same
            parts.append(dot(weight_s[span, cols], values))
        mixed = jnp.concatenate(parts, 0) / total
        gated.append((gating_ref[:, cols] * mixed).astype(BF16))
    after = (
        family_ref[...].astype(F32) + dot(jnp.concatenate(gated, 1), merge_ref[...])
    ).astype(BF16)
    after_s[...] = after
    leave = pltpu.make_async_copy(after_s, family_out_ref, sem)
    leave.start()
    ready = standardize_features(after.astype(F32)).astype(BF16)
    hidden = factor_ref.shape[0] // 2
    groups = width // group
    row_s[:, : 2 * hidden] = dot_nt(ready, factor_ref[...])
    placed = jnp.zeros((groups * seqs, 128), F32)
    for q in range(group):
        picked = jnp.concatenate(
            [row_s[pl.ds(group * g + q, seqs, stride=width), :] for g in range(groups)], 0
        )[:, :hidden].astype(BF16)
        here = iota((hidden, 128), 0) + hidden * q == iota((hidden, 128), 1)
        placed = placed + dot(picked, here.astype(F32).astype(BF16))
    for g in range(groups):
        send_ref[seqs * g : seqs * (g + 1), :] = placed[seqs * g : seqs * (g + 1), :].astype(BF16)
    turned = dot_nt(factor_ref[hidden : 2 * hidden, :], ready)
    for k in range(rows // 128):
        turn_s[hidden * k : hidden * (k + 1), :] = turned[:, 128 * k : 128 * k + 128]
    chunks = hidden // group
    for k in range(rows // 128):
        blocks = [
            turn_s[pl.ds(hidden * k + q, chunks, stride=group), :] for q in range(group)
        ]
        for p, block in enumerate(block_transpose(blocks, width)):
            first = chunks * (group * k + p)
            line_s[first : first + chunks, :] = block
    base = seqs * groups
    for g in range(chunks):
        send_ref[base + seqs * g : base + seqs * (g + 1), :] = line_s[
            pl.ds(g, seqs, stride=chunks), :
        ].astype(BF16)
    send_ref[2 * base :, :] = edge_ref[...]
    leave.wait()


def block_transpose(blocks, step):
    lane = iota(blocks[0].shape, 1)
    for shift in (2 * step, step):
        low = lane // shift % 2 == 0
        stride = shift // step
        out = list(blocks)
        for q in range(len(blocks)):
            if q // stride % 2 == 0:
                x, y = blocks[q], blocks[q + stride]
                up = pltpu.roll(y, shift, 1)
                down = pltpu.roll(x, 4 * step - shift, 1)
                out[q] = jnp.where(low, x, up)
                out[q + stride] = jnp.where(low, down, y)
        blocks = out
    return blocks


def average(values, weights):
    high = values.astype(BF16)
    low = (values - high.astype(F32)).astype(BF16)
    return dot(jnp.concatenate([high, low], 1), weights)


def center_and_scale(values, weights):
    center = values - average(values, weights)
    return center, lax.rsqrt(average(center * center, weights) + EPSILON)


def merge_rows(parts):
    row = iota(parts[0].shape, 0)
    step = 1
    while len(parts) > 1:
        low = row // step % 2 == 0
        parts = [
            jnp.where(low, x, y) + pltpu.roll(jnp.where(low, y, x), step, 0)
            for x, y in zip(parts[::2], parts[1::2])
        ]
        step *= 2
    return parts[0]


def pair_kernel(
    axis,
    width,
    own,
    hidden,
    seqs,
    sides_ref,
    got_ref,
    own_loss_ref,
    covariance_ref,
    edges_ref,
    cycle_ref,
    out_ref,
    grad_ref,
    right_s,
    flat_s,
    mid_s,
    unit_s,
    scale_s,
    gate_s,
    a_s,
    b_s,
    tri_s,
):
    me = lax.axis_index(axis)
    n = sides_ref.shape[0]
    group = 128 // hidden
    groups = width // group
    chunks = hidden // group
    pairs = own * width
    chans = 128
    total = seqs * n
    base = 2 * seqs * groups

    def gathered(first):
        return jnp.concatenate([sides_ref[d, first : first + seqs, :] for d in range(n)], 0)

    eye = (iota((128, 128), 0) == iota((128, 128), 1)).astype(F32).astype(BF16)
    for g in range(chunks):
        turned = dot_nt(eye, gathered(seqs * (groups + g))).astype(BF16)
        for q in range(group):
            right_s[width * g : width * (g + 1), total * q : total * (q + 1)] = turned[
                width * q : width * (q + 1), :
            ]
    weights = jnp.full((2 * chans, chans), 1.0 / chans, BF16)
    block = iota((total, 128), 1) // hidden
    for g in range(groups):
        left = gathered(seqs * g).astype(F32)
        rolled = [left] + [pltpu.roll(left, hidden * d, 1) for d in range(1, group)]
        for half in range(group // 2):
            columns = []
            for i in (2 * half, 2 * half + 1):
                columns.append(
                    jnp.concatenate(
                        [
                            jnp.where(block == q, rolled[(q - i) % group], 0.0).astype(BF16)
                            for q in range(group)
                        ],
                        0,
                    )
                )
            outer = dot(right_s[...], jnp.concatenate(columns, 1)).astype(BF16)
            for k in range(2):
                i = group * g + 2 * half + k
                for c in range(chunks):
                    flat_s[width * i : width * (i + 1), 128 * c : 128 * c + 128] = outer[
                        width * c : width * (c + 1), 128 * k : 128 * k + 128
                    ]
    part = n * pairs // 2
    spans = [slice(part * h, part * (h + 1)) for h in range(2)]
    tiles = jnp.concatenate([got_ref[d, :16, :] for d in range(n)], 0)
    pick = (iota((width, 128), 0) == iota((width, 128), 1)).astype(F32).astype(BF16)
    masks = dot_nt(pick, tiles)

    def kept(columns, first):
        return jnp.concatenate(
            [
                jnp.broadcast_to(columns[:, first + r : first + r + 1], (width, chans))
                for r in range(own)
            ],
            0,
        )

    added = [dot(flat_s[span, :], covariance_ref[...]) for span in spans]
    mids = []
    for h, span in enumerate(spans):
        devices = range(n // 2 * h, n // 2 * (h + 1))
        edge = jnp.concatenate([sides_ref[d, base:, :] for d in devices], 0).astype(F32)
        mids.append((edge + added[h] * (1.0 / total)).astype(BF16))
        mid_s[span, :] = mids[h].astype(F32)
    centers = [mid.astype(F32) - dot(mid, weights[:chans]) for mid in mids]
    scales = [lax.rsqrt(average(c * c, weights) + EPSILON) for c in centers]
    units = [c * scale for c, scale in zip(centers, scales)]
    sides = [dot(unit.astype(BF16), edges_ref[...]) for unit in units]
    for h, span in enumerate(spans):
        scale_s[span, :] = scales[h]
        unit_s[span, :] = units[h]
        gate_s[span, :] = sides[h][:, 2 * chans :]
        for d in range(n // 2):
            g = n // 2 * h + d
            keep = kept(masks, 16 * g + 2 * own)
            here = slice(pairs * d, pairs * (d + 1))
            there = slice(pairs * g, pairs * (g + 1))
            a_s[there, :] = (keep * sides[h][here, :chans]).astype(BF16).astype(F32)
            b_s[there, :] = (keep * sides[h][here, chans : 2 * chans]).astype(BF16).astype(F32)

    rows = pl.ds(pl.multiple_of(me * pairs, pairs), pairs)

    def rows_and_columns(ref):
        return jnp.concatenate(
            [ref[rows, :]] + [ref[pl.ds(me * own + r, width, stride=width), :] for r in range(own)],
            0,
        )

    mid = mid_s[rows, :]
    losses = jnp.concatenate([got_ref[d, 16:, :] for d in range(n)], 0)
    goal = iota((pairs, pairs), 0)
    source = goal % width // own * 16 + goal // width * own + goal % own
    place = (source == iota((pairs, pairs), 1)).astype(F32).astype(BF16)
    loss = jnp.concatenate([own_loss_ref[...].astype(F32), dot(place, losses)], 0)
    gating = jax.nn.sigmoid(rows_and_columns(gate_s))
    tri = []
    for fixed, moving in ((a_s, b_s), (b_s, a_s)):
        held = fixed[rows, :]
        for r in range(own):
            mine = [held[width * r + 8 * v : width * r + 8 * v + 8] for v in range(width // 8)]
            for j in range(0, width, 8):
                parts = []
                for jj in range(j, j + 8):
                    prods = [
                        mine[v] * moving[width * jj + 8 * v : width * jj + 8 * v + 8, :]
                        for v in range(width // 8)
                    ]
                    parts.append(functools.reduce(jnp.add, prods))
                tri.append(merge_rows(parts))
    tri = jnp.concatenate(tri, 0)
    center, scale_inv = center_and_scale(tri, weights)
    unit = center * scale_inv
    update = dot(unit[:pairs].astype(BF16), cycle_ref[...])
    out_ref[...] = (mid + gating[:pairs] * update).astype(BF16)
    grad_normed = dot_nt((loss * gating).astype(BF16), cycle_ref[...])
    tri_s[...] = (
        (
            scale_inv
            * (
                grad_normed
                - average(grad_normed, weights)
                - unit * average(grad_normed * unit, weights)
            )
        )
        .astype(BF16)
        .astype(F32)
    )

    def row(ref, r):
        return jnp.broadcast_to(ref[r : r + 1, :], (width, chans))

    acc = [jnp.zeros((width, chans), F32) for _ in range(2 * own)]
    for j in range(width):
        span = slice(width * j, width * j + width)
        b_j = b_s[span, :]
        a_j = a_s[span, :]
        for r in range(own):
            acc[r] = acc[r] + row(tri_s, width * r + j) * b_j
            acc[own + r] = acc[own + r] + row(tri_s, pairs + width * r + j) * a_j
    keep = kept(dot_nt(pick, got_ref[me, :16, :]), 2 * own)
    gate_own = gating[:pairs]
    grad_gate = loss[:pairs] * update * gate_own * (1.0 - gate_own)
    grad_proj = jnp.concatenate(
        [
            keep * jnp.concatenate(acc[:own], 0),
            keep * jnp.concatenate(acc[own:], 0),
            grad_gate,
        ],
        1,
    ).astype(BF16)
    grad_input = dot_nt(grad_proj, edges_ref[...])
    scale_inv = scale_s[rows, :]
    unit = unit_s[rows, :]
    grad_ref[...] = loss[:pairs] + scale_inv * (
        grad_input - average(grad_input, weights) - unit * average(grad_input * unit, weights)
    )


def body_resident(
    family_matrix,
    edge_matrix,
    edge_validity,
    query_key_value_gate_matrix,
    logit_offset_matrix,
    heads_merge_matrix,
    left_right_factor_matrix,
    covariance_merge_matrix,
    edges_gate_factor_matrix,
    cycle_merge_matrix,
    loss_sensitivity,
):
    seqs, width, depth = family_matrix.shape
    own, _, chans = edge_matrix.shape
    heads = logit_offset_matrix.shape[1]
    hidden = left_right_factor_matrix.shape[1] // 2
    pairs = own * width
    every = width * width
    edge = edge_matrix.reshape(pairs, chans)
    loss = loss_sensitivity.reshape(pairs, chans)
    vmem = pl.BlockSpec(memory_space=pltpu.VMEM)
    hbm = pl.BlockSpec(memory_space=pltpu.HBM)
    family = family_matrix.reshape(seqs * width, depth)
    factor = left_right_factor_matrix.T
    sided = 2 * seqs * width * hidden // 128
    peers = width // own
    packed = pl.pallas_call(
        functools.partial(pack_kernel, width),
        out_shape=jax.ShapeDtypeStruct((32 * peers, chans), BF16),
        in_specs=[hbm] * 4,
        out_specs=vmem,
        scratch_shapes=[
            pltpu.VMEM((pairs, chans), BF16),
            pltpu.VMEM((heads, chans), BF16),
            pltpu.VMEM((pairs, chans), BF16),
            pltpu.VMEM((own, width), jnp.int32),
            pltpu.VMEM((16, 128), F32),
            pltpu.SemaphoreType.DMA((4,)),
        ],
        name="pack_pairs",
    )(edge, logit_offset_matrix.T, loss, edge_validity)
    got = lax.all_to_all(packed, "dap", split_axis=0, concat_axis=0, tiled=True)
    got = got.reshape(peers, 32, chans)
    logits, value, gating, covariance = pl.pallas_call(
        functools.partial(project_kernel, width, heads, hidden),
        out_shape=(
            jax.ShapeDtypeStruct((seqs * width, depth), F32),
            jax.ShapeDtypeStruct((seqs * width, depth), BF16),
            jax.ShapeDtypeStruct((seqs * width, depth), F32),
            jax.ShapeDtypeStruct((hidden * hidden, chans), BF16),
        ),
        in_specs=[vmem] * 3,
        out_specs=(vmem,) * 4,
        scratch_shapes=[pltpu.VMEM((seqs * width, depth), BF16)] * 2
        + [pltpu.VMEM((hidden * hidden, chans), F32)],
        compiler_params=pltpu.CompilerParams(vmem_limit_bytes=16 << 20),
        cost_estimate=pl.CostEstimate(
            flops=16 * seqs * width * depth * depth,
            bytes_accessed=32 * seqs * width * depth,
            transcendentals=seqs * width * depth,
        ),
        name="project_family",
    )(family, query_key_value_gate_matrix, covariance_merge_matrix)
    family_out, send = pl.pallas_call(
        functools.partial(attention_kernel, width, own),
        out_shape=(
            jax.ShapeDtypeStruct((seqs * width, depth), BF16),
            jax.ShapeDtypeStruct((sided + pairs, 128), BF16),
        ),
        in_specs=[vmem] * 8,
        out_specs=(hbm, vmem),
        scratch_shapes=[
            pltpu.VMEM((seqs * width, depth), BF16),
            pltpu.VMEM((seqs * width, depth), BF16),
            pltpu.VMEM((seqs * width, 128), F32),
            pltpu.VMEM((seqs * width * hidden // 128, 128), F32),
            pltpu.VMEM((seqs * width * hidden // 128, 128), F32),
            pltpu.SemaphoreType.DMA(()),
        ],
        compiler_params=pltpu.CompilerParams(vmem_limit_bytes=16 << 20),
        name="row_attention",
    )(family, got, logits, value, gating, heads_merge_matrix, factor, edge)
    gathered = lax.all_gather(send, "dap", axis=0, tiled=False)
    pair_out, pair_grad = pl.pallas_call(
        functools.partial(pair_kernel, "dap", width, own, hidden, seqs),
        out_shape=(
            jax.ShapeDtypeStruct((pairs, chans), BF16),
            jax.ShapeDtypeStruct((pairs, chans), F32),
        ),
        in_specs=[vmem] * 6,
        out_specs=(vmem, vmem),
        scratch_shapes=[
            pltpu.VMEM((width * hidden * hidden // 128, 128 // hidden * 128), BF16),
            pltpu.VMEM((every, hidden * hidden), BF16),
            pltpu.VMEM((every, chans), F32),
            pltpu.VMEM((every, chans), F32),
            pltpu.VMEM((every, chans), F32),
            pltpu.VMEM((every, chans), F32),
            pltpu.VMEM((every, chans), F32),
            pltpu.VMEM((every, chans), F32),
            pltpu.VMEM((2 * pairs, chans), F32),
        ],
        compiler_params=pltpu.CompilerParams(vmem_limit_bytes=16 << 20),
        name="pair_update",
    )(gathered, got, loss, covariance, edges_gate_factor_matrix, cycle_merge_matrix)
    return (
        family_out.reshape(seqs, width, depth),
        pair_out.reshape(own, width, chans),
        pair_grad.reshape(own, width, chans),
    )


def fits_resident(dap, family, edge, logit, factor):
    seqs, width, depth = family.shape
    own, _, chans = edge.shape
    return (
        own * dap == width
        and width == 32
        and factor.shape[1] == 64
        and depth == 32 * logit.shape[1]
        and depth % 128 == 0
        and chans == 128
        and own * width == 128
        and seqs % 16 == 0
        and seqs * dap == 128
    )


def body(*args):
    dap = lax.axis_size("dap")
    if fits_resident(dap, args[0], args[1], args[4], args[6]):
        return body_resident(*args)
    return body_general(*args)


def solution(mesh):
    in_specs = (
        P(("dp", "dap"), None, None),
        P(("dp", "dap"), None, None),
        P(("dp", "dap"), None),
        P(),
        P(),
        P(),
        P(),
        P(),
        P(),
        P(),
        P(("dp", "dap"), None, None),
    )
    out_specs = (
        P(("dp", "dap"), None, None),
        P(("dp", "dap"), None, None),
        P(("dp", "dap"), None, None),
    )
    return jax.shard_map(body, mesh=mesh, in_specs=in_specs, out_specs=out_specs, check_vma=False)
```

```python
import functools
import math

import jax
import jax.numpy as jnp
from jax import lax
from jax.experimental import pallas as pl
from jax.experimental.pallas import tpu as pltpu
from jax.sharding import PartitionSpec as P

EPSILON = 1e-05


def standardize_features(values):
    center = values - jnp.mean(values, -1, keepdims=True)
    scale_inv = lax.rsqrt(jnp.mean(center * center, -1, keepdims=True) + EPSILON)
    return center * scale_inv


def norm_back(values, grad_out):
    center = values - jnp.mean(values, -1, keepdims=True)
    scale_inv = lax.rsqrt(jnp.mean(center * center, -1, keepdims=True) + EPSILON)
    standardized_source = center * scale_inv
    return scale_inv * (
        grad_out
        - jnp.mean(grad_out, -1, keepdims=True)
        - standardized_source * jnp.mean(grad_out * standardized_source, -1, keepdims=True)
    )


def lateral_heads_mixing(
    family_shard_slice, logit_offset_whole, query_key_value_gate_matrix, heads_merge_matrix
):
    homolog_number, amino_number, feature_depth = family_shard_slice.shape
    head_count = logit_offset_whole.shape[1]
    head_size = feature_depth // head_count
    standardized_source = standardize_features(family_shard_slice.astype(jnp.float32)).astype(
        jnp.bfloat16
    )
    projected = jnp.dot(
        standardized_source.reshape(-1, feature_depth),
        query_key_value_gate_matrix,
        preferred_element_type=jnp.float32,
    )
    projected = projected.reshape(homolog_number, amino_number, 4 * feature_depth)
    shape_heads = (homolog_number, amino_number, head_count, head_size)
    queries = projected[..., :feature_depth].astype(jnp.bfloat16).reshape(shape_heads)
    key_rows = (
        projected[..., feature_depth : 2 * feature_depth].astype(jnp.bfloat16).reshape(shape_heads)
    )
    value_rows = (
        projected[..., 2 * feature_depth : 3 * feature_depth]
        .astype(jnp.bfloat16)
        .reshape(shape_heads)
    )
    gating = jax.nn.sigmoid(projected[..., 3 * feature_depth :])
    logits = jnp.einsum("sihd,sjhd->sihj", queries, key_rows, preferred_element_type=jnp.float32)
    logits = logits / math.sqrt(head_size) + logit_offset_whole.astype(jnp.float32)[None]
    weights = jax.nn.softmax(logits, axis=-1).astype(jnp.bfloat16)
    mixed = jnp.einsum("sihj,sjhd->sihd", weights, value_rows, preferred_element_type=jnp.float32)
    gated = (gating * mixed.reshape(homolog_number, amino_number, feature_depth)).astype(
        jnp.bfloat16
    )
    edge_increment = jnp.dot(
        gated.reshape(-1, feature_depth), heads_merge_matrix, preferred_element_type=jnp.float32
    )
    return (
        family_shard_slice.astype(jnp.float32)
        + edge_increment.reshape(homolog_number, amino_number, feature_depth)
    ).astype(jnp.bfloat16)


def pair_projection_step(alignment_rows, left_right_factor_matrix):
    standardized_source = standardize_features(alignment_rows.astype(jnp.float32)).astype(
        jnp.bfloat16
    )
    edge_result = jnp.dot(
        standardized_source.reshape(-1, alignment_rows.shape[2]),
        left_right_factor_matrix,
        preferred_element_type=jnp.float32,
    )
    return edge_result.reshape(alignment_rows.shape[0], alignment_rows.shape[1], -1).astype(
        jnp.bfloat16
    )


def body_general(
    family_matrix,
    edge_matrix,
    edge_validity,
    query_key_value_gate_matrix,
    logit_offset_matrix,
    heads_merge_matrix,
    left_right_factor_matrix,
    covariance_merge_matrix,
    edges_gate_factor_matrix,
    cycle_merge_matrix,
    loss_sensitivity,
):
    res_rows, width, pair_chans = edge_matrix.shape
    pair_normed = standardize_features(edge_matrix.astype(jnp.float32)).astype(jnp.bfloat16)
    bias_local = jnp.einsum(
        "ijc,ch->ihj", pair_normed, logit_offset_matrix, preferred_element_type=jnp.float32
    ).astype(jnp.bfloat16)
    logit_offset_whole = lax.all_gather(bias_local, "dap", axis=0, tiled=True)
    homolog_lines = family_matrix.shape[0]
    homolog_subset = math.gcd(homolog_lines, 8)
    batched_lines = family_matrix.reshape(
        homolog_lines // homolog_subset,
        homolog_subset,
        family_matrix.shape[1],
        family_matrix.shape[2],
    )
    family_after_heads = lax.map(
        lambda family_shard_slice: lateral_heads_mixing(
            family_shard_slice, logit_offset_whole, query_key_value_gate_matrix, heads_merge_matrix
        ),
        batched_lines,
    ).reshape(family_matrix.shape)
    hidden = left_right_factor_matrix.shape[1] // 2
    weight_f32 = covariance_merge_matrix.astype(jnp.float32)
    alignment_columns = lax.all_to_all(
        family_after_heads, "dap", split_axis=1, concat_axis=0, tiled=True
    )
    edge_result = pair_projection_step(alignment_columns, left_right_factor_matrix)
    left_part = edge_result[..., :hidden]
    right_part = edge_result[..., hidden:]
    sequence_full_count = alignment_columns.shape[0]
    shard_in = lax.all_gather(right_part, "dap", axis=1, tiled=True)
    outer_sum = (
        jnp.einsum("sia,sjb->ijab", left_part, shard_in, preferred_element_type=jnp.float32)
        / sequence_full_count
    )
    row_count = shard_in.shape[1]
    flat = outer_sum.reshape(res_rows * row_count, hidden * hidden)
    edge_increment = jnp.dot(flat, weight_f32, precision=lax.Precision.HIGHEST).reshape(
        res_rows, row_count, pair_chans
    )
    pair_mid = (edge_matrix.astype(jnp.float32) + edge_increment).astype(jnp.bfloat16)
    tri_normed = standardize_features(pair_mid.astype(jnp.float32)).astype(jnp.bfloat16)
    tri_proj = jnp.dot(
        tri_normed.reshape(-1, pair_chans),
        edges_gate_factor_matrix,
        preferred_element_type=jnp.float32,
    ).reshape(res_rows, width, 3 * pair_chans)
    mask_f = edge_validity.astype(jnp.float32)[..., None]
    side_a = (mask_f * tri_proj[..., :pair_chans]).astype(jnp.bfloat16)
    side_b = (mask_f * tri_proj[..., pair_chans : 2 * pair_chans]).astype(jnp.bfloat16)
    gating = jax.nn.sigmoid(tri_proj[..., 2 * pair_chans :])
    tri_prod = jnp.einsum(
        "ikc,jkc->ijc",
        side_a,
        lax.all_gather(side_b, "dap", axis=0, tiled=True),
        preferred_element_type=jnp.float32,
    )
    prod_normed = standardize_features(tri_prod).astype(jnp.bfloat16)
    tri_update = jnp.dot(
        prod_normed.reshape(-1, pair_chans), cycle_merge_matrix, preferred_element_type=jnp.float32
    ).reshape(res_rows, width, pair_chans)
    pair_output = (pair_mid.astype(jnp.float32) + gating * tri_update).astype(jnp.bfloat16)
    cot_f32 = loss_sensitivity.astype(jnp.float32)
    grad_update = (cot_f32 * gating).astype(jnp.bfloat16)
    grad_normed = jnp.dot(
        grad_update.reshape(-1, pair_chans),
        cycle_merge_matrix.T,
        preferred_element_type=jnp.float32,
    ).reshape(res_rows, width, pair_chans)
    grad_prod = norm_back(tri_prod, grad_normed).astype(jnp.bfloat16)
    grad_part = grad_prod
    grad_a = jnp.einsum(
        "ijc,jkc->ikc",
        grad_part,
        lax.all_gather(side_b, "dap", axis=0, tiled=True),
        preferred_element_type=jnp.float32,
    )
    grad_part = grad_prod
    grad_b = lax.psum_scatter(
        jnp.einsum("ijc,ikc->jkc", grad_part, side_a, preferred_element_type=jnp.float32).astype(
            jnp.bfloat16
        ),
        "dap",
        scatter_dimension=0,
        tiled=True,
    ).astype(jnp.float32)
    grad_gate = cot_f32 * tri_update * gating * (1.0 - gating)
    grad_proj = jnp.concatenate([mask_f * grad_a, mask_f * grad_b, grad_gate], -1).astype(
        jnp.bfloat16
    )
    grad_input = jnp.dot(
        grad_proj.reshape(-1, 3 * pair_chans),
        edges_gate_factor_matrix.T,
        preferred_element_type=jnp.float32,
    ).reshape(res_rows, width, pair_chans)
    pair_gradient = cot_f32 + norm_back(pair_mid.astype(jnp.float32), grad_input)
    return (family_after_heads, pair_output, pair_gradient)


F32 = jnp.float32
BF16 = jnp.bfloat16
NT = (((1,), (1,)), ((), ()))
PARTS = 2


def dot(a, b):
    return jnp.dot(a, b, preferred_element_type=F32)


def dot_nt(a, b):
    return lax.dot_general(a, b, NT, preferred_element_type=F32)


def iota(shape, dim):
    return lax.broadcasted_iota(jnp.int32, shape, dim)


def pack_kernel(
    width, edge_ref, weight_ref, loss_ref, mask_ref, send_ref, edge_s, weight_s, loss_s, mask_s,
    tile_s, sems
):
    copies = [
        pltpu.make_async_copy(source, target, sems.at[k])
        for k, (source, target) in enumerate(
            (
                (edge_ref, edge_s),
                (weight_ref, weight_s),
                (loss_ref, loss_s),
                (mask_ref, mask_s),
            )
        )
    ]
    for copy in copies:
        copy.start()
    for copy in copies:
        copy.wait()
    rows, chans = edge_s.shape
    heads = weight_s.shape[0]
    own = rows // width
    lanes = heads * width
    peers = width // own
    tile_s[...] = jnp.zeros(tile_s.shape, F32)
    tile_s[2 * own : 3 * own, :width] = mask_s[...].astype(F32)
    normed = standardize_features(edge_s[...].astype(F32)).astype(BF16)
    spread = (iota((heads, lanes), 0) == iota((heads, lanes), 1) // width).astype(F32)
    weight = lax.dot_general(
        weight_s[...], spread.astype(BF16), (((0,), (0,)), ((), ())), preferred_element_type=F32
    ).astype(BF16)
    every = dot(normed, weight)
    keep = iota((rows, lanes), 0) % width == iota((rows, lanes), 1) % width
    picked = jnp.where(keep, every, 0.0).astype(BF16)
    packed = tile_s[...]
    for t in range(lanes // 128):
        place = iota((16, rows), 0) == own * t + iota((16, rows), 1) // width
        packed = packed + dot(
            place.astype(F32).astype(BF16), picked[:, 128 * t : 128 * t + 128]
        )
    packed = packed.astype(BF16)
    goal = iota((rows, rows), 0)
    source = goal % own * width + goal // (own * own) * own + goal // own % own
    place = (source == iota((rows, rows), 1)).astype(F32).astype(BF16)
    losses = dot(place, loss_s[...]).astype(BF16)
    for e in range(peers):
        send_ref[32 * e : 32 * e + 16, :] = packed
        send_ref[32 * e + 16 : 32 * e + 32, :] = losses[16 * e : 16 * e + 16]


def project_kernel(
    width,
    heads,
    hidden,
    family_ref,
    project_ref,
    covariance_ref,
    logits_ref,
    value_ref,
    gating_ref,
    cov_ref,
    query_s,
    key_s,
    value_s,
    cov_s,
):
    rows, depth = family_ref.shape
    seqs = rows // width
    group = 128 // width
    normed = standardize_features(family_ref[...].astype(F32)).astype(BF16)
    query_s[...] = dot(normed, project_ref[:, :depth]).astype(BF16)
    key_s[...] = dot(normed, project_ref[:, depth : 2 * depth]).astype(BF16)
    value_s[...] = dot(normed, project_ref[:, 2 * depth : 3 * depth]).astype(BF16)
    gating_ref[...] = jax.nn.sigmoid(dot(normed, project_ref[:, 3 * depth :]))
    same = (iota((128, 128), 0) // width == iota((128, 128), 1) // width).astype(F32).astype(BF16)
    scale = 1.0 / math.sqrt(depth // heads)
    for t in range(depth // 128):
        cols = slice(128 * t, 128 * t + 128)
        for s in range(seqs):
            span = slice(width * s, width * s + width)
            keys = jnp.concatenate([key_s[span, cols]] * group, 0) * same
            logits_ref[span, cols] = dot_nt(query_s[span, cols], keys) * scale
            values = jnp.concatenate([value_s[span, cols]] * group, 0) * same
            value_ref[128 * s : 128 * (s + 1), cols] = values
    cov_s[...] = covariance_ref[...].astype(F32)
    for b in range(hidden):
        rows_b = cov_s[pl.ds(b, hidden, stride=hidden), :].astype(BF16)
        cov_ref[0, hidden * b : hidden * (b + 1), :] = rows_b
        swapped = b ^ (group // 2)
        cov_ref[1, hidden * swapped : hidden * (swapped + 1), :] = rows_b


def attention_kernel(
    width,
    own,
    family_ref,
    got_ref,
    logits_ref,
    value_ref,
    gating_ref,
    merge_ref,
    factor_ref,
    edge_ref,
    family_out_ref,
    send_ref,
    after_s,
    weight_s,
    row_s,
    turn_s,
    line_s,
    sem,
):
    rows, depth = family_ref.shape
    seqs = rows // width
    tiles = depth // 128
    group = 128 // width
    biases = jnp.concatenate([got_ref[d, :16, :] for d in range(got_ref.shape[0])], 0)
    gated = []
    for t in range(tiles):
        cols = slice(128 * t, 128 * t + 128)
        row = iota((width, biases.shape[0]), 0)
        take = iota((width, biases.shape[0]), 1) == 16 * (row // own) + own * t + row % own
        bias = dot(take.astype(F32).astype(BF16), biases)
        for k in range(rows // 128):
            span = slice(128 * k, 128 * (k + 1))
            flipped = (logits_ref[span, cols] + jnp.concatenate([bias] * group, 0)).T
            parts = []
            for h in range(group):
                some = flipped[width * h : width * (h + 1)]
                raised = jnp.exp(some - jnp.max(some, 0, keepdims=True))
                parts.append(raised * (1.0 / jnp.sum(raised, 0, keepdims=True)))
            weight_s[span, cols] = jnp.concatenate(parts, 0).astype(BF16).T
    for t in range(tiles):
        cols = slice(128 * t, 128 * t + 128)
        mixed = jnp.concatenate(
            [
                dot(weight_s[width * s : width * (s + 1), cols], value_ref[128 * s : 128 * (s + 1), cols])
                for s in range(seqs)
            ],
            0,
        )
        gated.append((gating_ref[:, cols] * mixed).astype(BF16))
    after = (
        family_ref[...].astype(F32) + dot(jnp.concatenate(gated, 1), merge_ref[...])
    ).astype(BF16)
    after_s[...] = after
    leave = pltpu.make_async_copy(after_s, family_out_ref, sem)
    leave.start()
    ready = standardize_features(after.astype(F32)).astype(BF16)
    hidden = factor_ref.shape[0] // 2
    groups = width // group
    row_s[:, : 2 * hidden] = dot_nt(ready, factor_ref[...])
    placed = jnp.zeros((groups * seqs, 128), F32)
    for q in range(group):
        picked = jnp.concatenate(
            [row_s[pl.ds(group * g + q, seqs, stride=width), :] for g in range(groups)], 0
        )[:, :hidden].astype(BF16)
        here = iota((hidden, 128), 0) + hidden * q == iota((hidden, 128), 1)
        placed = placed + dot(picked, here.astype(F32).astype(BF16))
    for g in range(groups):
        send_ref[seqs * g : seqs * (g + 1), :] = placed[seqs * g : seqs * (g + 1), :].astype(BF16)
    turned = dot_nt(factor_ref[hidden : 2 * hidden, :], ready)
    for k in range(rows // 128):
        turn_s[hidden * k : hidden * (k + 1), :] = turned[:, 128 * k : 128 * k + 128]
    chunks = hidden // group
    for k in range(rows // 128):
        blocks = [
            turn_s[pl.ds(hidden * k + q, chunks, stride=group), :] for q in range(group)
        ]
        for p, block in enumerate(block_transpose(blocks, width)):
            first = chunks * (group * k + p)
            line_s[first : first + chunks, :] = block
    base = seqs * groups
    for g in range(chunks):
        send_ref[base + seqs * g : base + seqs * (g + 1), :] = line_s[
            pl.ds(g, seqs, stride=chunks), :
        ].astype(BF16)
    send_ref[2 * base :, :] = edge_ref[...]
    leave.wait()


def block_transpose(blocks, step):
    lane = iota(blocks[0].shape, 1)
    for shift in (2 * step, step):
        low = lane // shift % 2 == 0
        stride = shift // step
        out = list(blocks)
        for q in range(len(blocks)):
            if q // stride % 2 == 0:
                x, y = blocks[q], blocks[q + stride]
                up = pltpu.roll(y, shift, 1)
                down = pltpu.roll(x, 4 * step - shift, 1)
                out[q] = jnp.where(low, x, up)
                out[q + stride] = jnp.where(low, down, y)
        blocks = out
    return blocks


def mean(values):
    return jnp.mean(values, -1, keepdims=True)


def merge_rows(parts):
    row = iota(parts[0].shape, 0)
    step = 1
    while len(parts) > 1:
        low = row // step % 2 == 0
        parts = [
            jnp.where(low, x, y) + pltpu.roll(jnp.where(low, y, x), step, 0)
            for x, y in zip(parts[::2], parts[1::2])
        ]
        step *= 2
    return parts[0]


def pair_kernel(
    axis,
    width,
    own,
    hidden,
    seqs,
    sides_ref,
    got_ref,
    own_loss_ref,
    covariance_ref,
    edges_ref,
    cycle_ref,
    out_ref,
    grad_ref,
    right_s,
    flat_s,
    mid_s,
    unit_s,
    scale_s,
    a_s,
    b_s,
    tri_s,
):
    me = lax.axis_index(axis)
    n = sides_ref.shape[0]
    every = width * width
    group = 128 // hidden
    groups = width // group
    chunks = hidden // group
    pairs = own * width
    chans = 128
    total = seqs * n
    base = 2 * seqs * groups

    def gathered(first):
        return jnp.concatenate([sides_ref[d, first : first + seqs, :] for d in range(n)], 0)

    eye = (iota((128, 128), 0) == iota((128, 128), 1)).astype(F32).astype(BF16)
    for g in range(chunks):
        turned = dot_nt(eye, gathered(seqs * (groups + g))).astype(BF16)
        for q in range(group):
            right_s[width * g : width * (g + 1), total * q : total * (q + 1)] = turned[
                width * q : width * (q + 1), :
            ]
    block = iota((total, 128), 1) // hidden
    low_half = iota((width * chunks, 128), 1) < 64
    zero = jnp.zeros((total, 128), BF16)
    for g in range(groups):
        left = gathered(seqs * g)
        wide = left.astype(F32)
        rolled = [left] + [
            pltpu.roll(wide, hidden * d, 1).astype(BF16) for d in range(1, group)
        ]

        def placed(first, second, lane):
            return jnp.where(
                block == lane,
                rolled[(lane - first) % group],
                jnp.where(block == lane + 2, rolled[(lane + 2 - second) % group], zero),
            )

        halves = []
        for h in range(2):
            columns = []
            for even in range(0, group, 2):
                first, second = (even, even + 1) if h == 0 else (even + 1, even)
                columns.append(
                    jnp.concatenate([placed(first, second, lane) for lane in range(2)], 0)
                )
            halves.append(
                dot(
                    right_s[:, 2 * total * h : 2 * total * (h + 1)],
                    jnp.concatenate(columns, 1),
                ).astype(BF16)
            )
        for e in range(group // 2):
            x, y = (half[:, 128 * e : 128 * e + 128] for half in halves)
            for odd, outer in enumerate(
                (jnp.where(low_half, x, y), jnp.where(low_half, y, x))
            ):
                first = every // 2 * odd + width * (group // 2 * g + e)
                for c in range(chunks):
                    flat_s[first : first + width, 128 * c : 128 * c + 128] = outer[
                        width * c : width * (c + 1)
                    ]
    tiles = jnp.concatenate([got_ref[d, :16, :] for d in range(n)], 0)
    pick = (iota((width, 128), 0) == iota((width, 128), 1)).astype(F32).astype(BF16)
    masks = dot_nt(pick, tiles)

    def kept(columns, first):
        return jnp.concatenate(
            [
                jnp.broadcast_to(columns[:, first + r : first + r + 1], (width, chans))
                for r in range(own)
            ],
            0,
        )

    count = width // PARTS
    lists = [
        [2 * (count * (p // 2) + k) + p % 2 for k in range(count)] for p in range(PARTS)
    ]
    centered = jnp.where(
        iota((chans, chans), 0) == iota((chans, chans), 1), 1.0 - 1.0 / chans, -1.0 / chans
    ).astype(BF16)
    added = [
        dot(
            flat_s[
                every // 2 * (p % 2) + width * count * (p // 2) : every // 2 * (p % 2)
                + width * count * (p // 2 + 1),
                :,
            ],
            covariance_ref[p % 2],
        )
        for p in range(PARTS)
    ]
    mids = []
    for p, residues in enumerate(lists):
        edge = jnp.concatenate(
            [
                sides_ref[i // own, base + width * (i % own) : base + width * (i % own + 1), :]
                for i in residues
            ],
            0,
        ).astype(F32)
        mids.append((edge + added[p] * (1.0 / total)).astype(BF16))
    centers = [dot(mid, centered) for mid in mids]
    scales = [lax.rsqrt(mean(c * c) + EPSILON) for c in centers]
    units = [c * scale for c, scale in zip(centers, scales)]
    sides = [dot(unit.astype(BF16), edges_ref[:, : 2 * chans]) for unit in units]
    for p, residues in enumerate(lists):
        for k, i in enumerate(residues):
            here = slice(width * k, width * (k + 1))
            there = slice(width * i, width * (i + 1))
            mid_s[there, :] = mids[p][here].astype(F32)
            scale_s[there, :] = jnp.broadcast_to(scales[p][here], (width, chans))
            unit_s[there, :] = units[p][here]
            lane = 16 * (i // own) + 2 * own + i % own
            keep = jnp.broadcast_to(masks[:, lane : lane + 1], (width, chans))
            a_s[there, :] = (keep * sides[p][here, :chans]).astype(BF16).astype(F32)
            b_s[there, :] = (keep * sides[p][here, chans:]).astype(BF16).astype(F32)

    rows = pl.ds(pl.multiple_of(me * pairs, pairs), pairs)

    def rows_and_columns(ref):
        return jnp.concatenate(
            [ref[rows, :]] + [ref[pl.ds(me * own + r, width, stride=width), :] for r in range(own)],
            0,
        )

    mid = mid_s[rows, :]
    losses = jnp.concatenate([got_ref[d, 16:, :] for d in range(n)], 0)
    goal = iota((pairs, pairs), 0)
    source = goal % width // own * 16 + goal // width * own + goal % own
    place = (source == iota((pairs, pairs), 1)).astype(F32).astype(BF16)
    loss = jnp.concatenate([own_loss_ref[...].astype(F32), dot(place, losses)], 0)
    gating = jax.nn.sigmoid(
        dot(rows_and_columns(unit_s).astype(BF16), edges_ref[:, 2 * chans :])
    )
    tri = []
    for fixed, moving in ((a_s, b_s), (b_s, a_s)):
        held = fixed[rows, :]
        for r in range(own):
            mine = [held[width * r + 8 * v : width * r + 8 * v + 8] for v in range(width // 8)]
            for j in range(0, width, 8):
                parts = []
                for jj in range(j, j + 8):
                    prods = [
                        mine[v] * moving[width * jj + 8 * v : width * jj + 8 * v + 8, :]
                        for v in range(width // 8)
                    ]
                    parts.append(functools.reduce(jnp.add, prods))
                tri.append(merge_rows(parts))
    tri = jnp.concatenate(tri, 0)
    center = tri - mean(tri)
    scale_inv = lax.rsqrt(mean(center * center) + EPSILON)
    unit = center * scale_inv
    update = dot(unit[:pairs].astype(BF16), cycle_ref[...])
    out_ref[...] = (mid + gating[:pairs] * update).astype(BF16)
    grad_normed = dot_nt((loss * gating).astype(BF16), cycle_ref[...])
    tri_s[...] = (
        (
            scale_inv
            * (
                grad_normed - mean(grad_normed) - unit * mean(grad_normed * unit)
            )
        )
        .astype(BF16)
        .astype(F32)
    )

    def row(ref, r):
        return jnp.broadcast_to(ref[r : r + 1, :], (width, chans))

    acc = [jnp.zeros((width, chans), F32) for _ in range(2 * own)]
    for j in range(width):
        span = slice(width * j, width * j + width)
        b_j = b_s[span, :]
        a_j = a_s[span, :]
        for r in range(own):
            acc[r] = acc[r] + row(tri_s, width * r + j) * b_j
            acc[own + r] = acc[own + r] + row(tri_s, pairs + width * r + j) * a_j
    keep = kept(dot_nt(pick, got_ref[me, :16, :]), 2 * own)
    gate_own = gating[:pairs]
    grad_gate = loss[:pairs] * update * gate_own * (1.0 - gate_own)
    grad_proj = jnp.concatenate(
        [
            keep * jnp.concatenate(acc[:own], 0),
            keep * jnp.concatenate(acc[own:], 0),
            grad_gate,
        ],
        1,
    ).astype(BF16)
    grad_input = dot_nt(grad_proj, edges_ref[...])
    scale_inv = scale_s[rows, :]
    unit = unit_s[rows, :]
    grad_ref[...] = loss[:pairs] + scale_inv * (
        grad_input - mean(grad_input) - unit * mean(grad_input * unit)
    )


def body_resident(
    family_matrix,
    edge_matrix,
    edge_validity,
    query_key_value_gate_matrix,
    logit_offset_matrix,
    heads_merge_matrix,
    left_right_factor_matrix,
    covariance_merge_matrix,
    edges_gate_factor_matrix,
    cycle_merge_matrix,
    loss_sensitivity,
):
    seqs, width, depth = family_matrix.shape
    own, _, chans = edge_matrix.shape
    heads = logit_offset_matrix.shape[1]
    hidden = left_right_factor_matrix.shape[1] // 2
    pairs = own * width
    every = width * width
    edge = edge_matrix.reshape(pairs, chans)
    loss = loss_sensitivity.reshape(pairs, chans)
    vmem = pl.BlockSpec(memory_space=pltpu.VMEM)
    hbm = pl.BlockSpec(memory_space=pltpu.HBM)
    family = family_matrix.reshape(seqs * width, depth)
    factor = left_right_factor_matrix.T
    sided = 2 * seqs * width * hidden // 128
    peers = width // own
    packed = pl.pallas_call(
        functools.partial(pack_kernel, width),
        out_shape=jax.ShapeDtypeStruct((32 * peers, chans), BF16),
        in_specs=[hbm] * 4,
        out_specs=vmem,
        scratch_shapes=[
            pltpu.VMEM((pairs, chans), BF16),
            pltpu.VMEM((heads, chans), BF16),
            pltpu.VMEM((pairs, chans), BF16),
            pltpu.VMEM((own, width), jnp.int32),
            pltpu.VMEM((16, 128), F32),
            pltpu.SemaphoreType.DMA((4,)),
        ],
        name="pack_pairs",
    )(edge, logit_offset_matrix.T, loss, edge_validity)
    got = lax.all_to_all(packed, "dap", split_axis=0, concat_axis=0, tiled=True)
    got = got.reshape(peers, 32, chans)
    logits, value, gating, covariance = pl.pallas_call(
        functools.partial(project_kernel, width, heads, hidden),
        out_shape=(
            jax.ShapeDtypeStruct((seqs * width, depth), F32),
            jax.ShapeDtypeStruct((seqs * 128, depth), BF16),
            jax.ShapeDtypeStruct((seqs * width, depth), F32),
            jax.ShapeDtypeStruct((2, hidden * hidden, chans), BF16),
        ),
        in_specs=[vmem] * 3,
        out_specs=(vmem,) * 4,
        scratch_shapes=[pltpu.VMEM((seqs * width, depth), BF16)] * 3
        + [pltpu.VMEM((hidden * hidden, chans), F32)],
        compiler_params=pltpu.CompilerParams(vmem_limit_bytes=16 << 20),
        cost_estimate=pl.CostEstimate(
            flops=16 * seqs * width * depth * depth,
            bytes_accessed=32 * seqs * width * depth,
            transcendentals=seqs * width * depth,
        ),
        name="project_family",
    )(family, query_key_value_gate_matrix, covariance_merge_matrix)
    family_out, send = pl.pallas_call(
        functools.partial(attention_kernel, width, own),
        out_shape=(
            jax.ShapeDtypeStruct((seqs * width, depth), BF16),
            jax.ShapeDtypeStruct((sided + pairs, 128), BF16),
        ),
        in_specs=[vmem] * 8,
        out_specs=(hbm, vmem),
        scratch_shapes=[
            pltpu.VMEM((seqs * width, depth), BF16),
            pltpu.VMEM((seqs * width, depth), BF16),
            pltpu.VMEM((seqs * width, 128), F32),
            pltpu.VMEM((seqs * width * hidden // 128, 128), F32),
            pltpu.VMEM((seqs * width * hidden // 128, 128), F32),
            pltpu.SemaphoreType.DMA(()),
        ],
        compiler_params=pltpu.CompilerParams(vmem_limit_bytes=16 << 20),
        name="row_attention",
    )(family, got, logits, value, gating, heads_merge_matrix, factor, edge)
    gathered = lax.all_gather(send, "dap", axis=0, tiled=False)
    pair_out, pair_grad = pl.pallas_call(
        functools.partial(pair_kernel, "dap", width, own, hidden, seqs),
        out_shape=(
            jax.ShapeDtypeStruct((pairs, chans), BF16),
            jax.ShapeDtypeStruct((pairs, chans), F32),
        ),
        in_specs=[vmem] * 6,
        out_specs=(vmem, vmem),
        scratch_shapes=[
            pltpu.VMEM((width * hidden * hidden // 128, 128 // hidden * 128), BF16),
            pltpu.VMEM((every, hidden * hidden), BF16),
            pltpu.VMEM((every, chans), F32),
            pltpu.VMEM((every, chans), F32),
            pltpu.VMEM((every, chans), F32),
            pltpu.VMEM((every, chans), F32),
            pltpu.VMEM((every, chans), F32),
            pltpu.VMEM((2 * pairs, chans), F32),
        ],
        compiler_params=pltpu.CompilerParams(vmem_limit_bytes=16 << 20),
        name="pair_update",
    )(gathered, got, loss, covariance, edges_gate_factor_matrix, cycle_merge_matrix)
    return (
        family_out.reshape(seqs, width, depth),
        pair_out.reshape(own, width, chans),
        pair_grad.reshape(own, width, chans),
    )


def fits_resident(dap, family, edge, logit, factor):
    seqs, width, depth = family.shape
    own, _, chans = edge.shape
    return (
        own * dap == width
        and width == 32
        and factor.shape[1] == 64
        and depth == 32 * logit.shape[1]
        and depth % 128 == 0
        and chans == 128
        and own * width == 128
        and seqs % 16 == 0
        and seqs * dap == 128
    )


def body(*args):
    dap = lax.axis_size("dap")
    if fits_resident(dap, args[0], args[1], args[4], args[6]):
        return body_resident(*args)
    return body_general(*args)


def solution(mesh):
    in_specs = (
        P(("dp", "dap"), None, None),
        P(("dp", "dap"), None, None),
        P(("dp", "dap"), None),
        P(),
        P(),
        P(),
        P(),
        P(),
        P(),
        P(),
        P(("dp", "dap"), None, None),
    )
    out_specs = (
        P(("dp", "dap"), None, None),
        P(("dp", "dap"), None, None),
        P(("dp", "dap"), None, None),
    )
    return jax.shard_map(body, mesh=mesh, in_specs=in_specs, out_specs=out_specs, check_vma=False)
```

```python
import functools
import math

import jax
import jax.numpy as jnp
from jax import lax
from jax.experimental import pallas as pl
from jax.experimental.pallas import tpu as pltpu
from jax.sharding import PartitionSpec as P

EPSILON = 1e-05


def standardize_features(values):
    center = values - jnp.mean(values, -1, keepdims=True)
    scale_inv = lax.rsqrt(jnp.mean(center * center, -1, keepdims=True) + EPSILON)
    return center * scale_inv


def norm_back(values, grad_out):
    center = values - jnp.mean(values, -1, keepdims=True)
    scale_inv = lax.rsqrt(jnp.mean(center * center, -1, keepdims=True) + EPSILON)
    standardized_source = center * scale_inv
    return scale_inv * (
        grad_out
        - jnp.mean(grad_out, -1, keepdims=True)
        - standardized_source * jnp.mean(grad_out * standardized_source, -1, keepdims=True)
    )


def lateral_heads_mixing(
    family_shard_slice, logit_offset_whole, query_key_value_gate_matrix, heads_merge_matrix
):
    homolog_number, amino_number, feature_depth = family_shard_slice.shape
    head_count = logit_offset_whole.shape[1]
    head_size = feature_depth // head_count
    standardized_source = standardize_features(family_shard_slice.astype(jnp.float32)).astype(
        jnp.bfloat16
    )
    projected = jnp.dot(
        standardized_source.reshape(-1, feature_depth),
        query_key_value_gate_matrix,
        preferred_element_type=jnp.float32,
    )
    projected = projected.reshape(homolog_number, amino_number, 4 * feature_depth)
    shape_heads = (homolog_number, amino_number, head_count, head_size)
    queries = projected[..., :feature_depth].astype(jnp.bfloat16).reshape(shape_heads)
    key_rows = (
        projected[..., feature_depth : 2 * feature_depth].astype(jnp.bfloat16).reshape(shape_heads)
    )
    value_rows = (
        projected[..., 2 * feature_depth : 3 * feature_depth]
        .astype(jnp.bfloat16)
        .reshape(shape_heads)
    )
    gating = jax.nn.sigmoid(projected[..., 3 * feature_depth :])
    logits = jnp.einsum("sihd,sjhd->sihj", queries, key_rows, preferred_element_type=jnp.float32)
    logits = logits / math.sqrt(head_size) + logit_offset_whole.astype(jnp.float32)[None]
    weights = jax.nn.softmax(logits, axis=-1).astype(jnp.bfloat16)
    mixed = jnp.einsum("sihj,sjhd->sihd", weights, value_rows, preferred_element_type=jnp.float32)
    gated = (gating * mixed.reshape(homolog_number, amino_number, feature_depth)).astype(
        jnp.bfloat16
    )
    edge_increment = jnp.dot(
        gated.reshape(-1, feature_depth), heads_merge_matrix, preferred_element_type=jnp.float32
    )
    return (
        family_shard_slice.astype(jnp.float32)
        + edge_increment.reshape(homolog_number, amino_number, feature_depth)
    ).astype(jnp.bfloat16)


def pair_projection_step(alignment_rows, left_right_factor_matrix):
    standardized_source = standardize_features(alignment_rows.astype(jnp.float32)).astype(
        jnp.bfloat16
    )
    edge_result = jnp.dot(
        standardized_source.reshape(-1, alignment_rows.shape[2]),
        left_right_factor_matrix,
        preferred_element_type=jnp.float32,
    )
    return edge_result.reshape(alignment_rows.shape[0], alignment_rows.shape[1], -1).astype(
        jnp.bfloat16
    )


def body_general(
    family_matrix,
    edge_matrix,
    edge_validity,
    query_key_value_gate_matrix,
    logit_offset_matrix,
    heads_merge_matrix,
    left_right_factor_matrix,
    covariance_merge_matrix,
    edges_gate_factor_matrix,
    cycle_merge_matrix,
    loss_sensitivity,
):
    res_rows, width, pair_chans = edge_matrix.shape
    pair_normed = standardize_features(edge_matrix.astype(jnp.float32)).astype(jnp.bfloat16)
    bias_local = jnp.einsum(
        "ijc,ch->ihj", pair_normed, logit_offset_matrix, preferred_element_type=jnp.float32
    ).astype(jnp.bfloat16)
    logit_offset_whole = lax.all_gather(bias_local, "dap", axis=0, tiled=True)
    homolog_lines = family_matrix.shape[0]
    homolog_subset = math.gcd(homolog_lines, 8)
    batched_lines = family_matrix.reshape(
        homolog_lines // homolog_subset,
        homolog_subset,
        family_matrix.shape[1],
        family_matrix.shape[2],
    )
    family_after_heads = lax.map(
        lambda family_shard_slice: lateral_heads_mixing(
            family_shard_slice, logit_offset_whole, query_key_value_gate_matrix, heads_merge_matrix
        ),
        batched_lines,
    ).reshape(family_matrix.shape)
    hidden = left_right_factor_matrix.shape[1] // 2
    weight_f32 = covariance_merge_matrix.astype(jnp.float32)
    alignment_columns = lax.all_to_all(
        family_after_heads, "dap", split_axis=1, concat_axis=0, tiled=True
    )
    edge_result = pair_projection_step(alignment_columns, left_right_factor_matrix)
    left_part = edge_result[..., :hidden]
    right_part = edge_result[..., hidden:]
    sequence_full_count = alignment_columns.shape[0]
    shard_in = lax.all_gather(right_part, "dap", axis=1, tiled=True)
    outer_sum = (
        jnp.einsum("sia,sjb->ijab", left_part, shard_in, preferred_element_type=jnp.float32)
        / sequence_full_count
    )
    row_count = shard_in.shape[1]
    flat = outer_sum.reshape(res_rows * row_count, hidden * hidden)
    edge_increment = jnp.dot(flat, weight_f32, precision=lax.Precision.HIGHEST).reshape(
        res_rows, row_count, pair_chans
    )
    pair_mid = (edge_matrix.astype(jnp.float32) + edge_increment).astype(jnp.bfloat16)
    tri_normed = standardize_features(pair_mid.astype(jnp.float32)).astype(jnp.bfloat16)
    tri_proj = jnp.dot(
        tri_normed.reshape(-1, pair_chans),
        edges_gate_factor_matrix,
        preferred_element_type=jnp.float32,
    ).reshape(res_rows, width, 3 * pair_chans)
    mask_f = edge_validity.astype(jnp.float32)[..., None]
    side_a = (mask_f * tri_proj[..., :pair_chans]).astype(jnp.bfloat16)
    side_b = (mask_f * tri_proj[..., pair_chans : 2 * pair_chans]).astype(jnp.bfloat16)
    gating = jax.nn.sigmoid(tri_proj[..., 2 * pair_chans :])
    tri_prod = jnp.einsum(
        "ikc,jkc->ijc",
        side_a,
        lax.all_gather(side_b, "dap", axis=0, tiled=True),
        preferred_element_type=jnp.float32,
    )
    prod_normed = standardize_features(tri_prod).astype(jnp.bfloat16)
    tri_update = jnp.dot(
        prod_normed.reshape(-1, pair_chans), cycle_merge_matrix, preferred_element_type=jnp.float32
    ).reshape(res_rows, width, pair_chans)
    pair_output = (pair_mid.astype(jnp.float32) + gating * tri_update).astype(jnp.bfloat16)
    cot_f32 = loss_sensitivity.astype(jnp.float32)
    grad_update = (cot_f32 * gating).astype(jnp.bfloat16)
    grad_normed = jnp.dot(
        grad_update.reshape(-1, pair_chans),
        cycle_merge_matrix.T,
        preferred_element_type=jnp.float32,
    ).reshape(res_rows, width, pair_chans)
    grad_prod = norm_back(tri_prod, grad_normed).astype(jnp.bfloat16)
    grad_part = grad_prod
    grad_a = jnp.einsum(
        "ijc,jkc->ikc",
        grad_part,
        lax.all_gather(side_b, "dap", axis=0, tiled=True),
        preferred_element_type=jnp.float32,
    )
    grad_part = grad_prod
    grad_b = lax.psum_scatter(
        jnp.einsum("ijc,ikc->jkc", grad_part, side_a, preferred_element_type=jnp.float32).astype(
            jnp.bfloat16
        ),
        "dap",
        scatter_dimension=0,
        tiled=True,
    ).astype(jnp.float32)
    grad_gate = cot_f32 * tri_update * gating * (1.0 - gating)
    grad_proj = jnp.concatenate([mask_f * grad_a, mask_f * grad_b, grad_gate], -1).astype(
        jnp.bfloat16
    )
    grad_input = jnp.dot(
        grad_proj.reshape(-1, 3 * pair_chans),
        edges_gate_factor_matrix.T,
        preferred_element_type=jnp.float32,
    ).reshape(res_rows, width, pair_chans)
    pair_gradient = cot_f32 + norm_back(pair_mid.astype(jnp.float32), grad_input)
    return (family_after_heads, pair_output, pair_gradient)


F32 = jnp.float32
BF16 = jnp.bfloat16
NT = (((1,), (1,)), ((), ()))
PARTS = 2


def dot(a, b):
    return jnp.dot(a, b, preferred_element_type=F32)


def dot_nt(a, b):
    return lax.dot_general(a, b, NT, preferred_element_type=F32)


def iota(shape, dim):
    return lax.broadcasted_iota(jnp.int32, shape, dim)


def pack_kernel(
    width, edge_ref, weight_ref, loss_ref, mask_ref, send_ref, edge_s, weight_s, loss_s, mask_s,
    tile_s, sems
):
    copies = [
        pltpu.make_async_copy(source, target, sems.at[k])
        for k, (source, target) in enumerate(
            (
                (edge_ref, edge_s),
                (weight_ref, weight_s),
                (loss_ref, loss_s),
                (mask_ref, mask_s),
            )
        )
    ]
    for copy in copies:
        copy.start()
    rows, chans = edge_s.shape
    heads = weight_s.shape[0]
    own = rows // width
    lanes = heads * width
    peers = width // own
    spread = (iota((heads, lanes), 0) == iota((heads, lanes), 1) // width).astype(F32)
    keep = iota((width, lanes), 0) == iota((width, lanes), 1) % width
    goal = iota((rows, rows), 0)
    source = goal % own * width + goal // (own * own) * own + goal // own % own
    place = (source == iota((rows, rows), 1)).astype(F32).astype(BF16)
    tile_s[...] = jnp.zeros(tile_s.shape, F32)
    for copy in copies:
        copy.wait()
    weight = lax.dot_general(
        weight_s[...], spread.astype(BF16), (((0,), (0,)), ((), ())), preferred_element_type=F32
    ).astype(BF16)
    column = dot(jnp.ones((8, chans), BF16), weight)[:1]
    every = dot(edge_s[...], weight)
    edge = edge_s[...].astype(F32)
    middle = jnp.mean(edge, -1, keepdims=True)
    center = edge - middle
    scale = lax.rsqrt(jnp.mean(center * center, -1, keepdims=True) + EPSILON)
    bias = scale * (every - middle * column)
    losses = dot(place, loss_s[...]).astype(BF16)
    tile_s[2 * own : 3 * own, :width] = mask_s[...].astype(F32)
    packed = tile_s[...]
    for r in range(own):
        picked = jnp.where(keep, bias[width * r : width * (r + 1)], 0.0)
        total = jnp.sum(picked, 0, keepdims=True)
        for t in range(lanes // 128):
            packed = jnp.where(
                iota((16, 128), 0) == own * t + r, total[:, 128 * t : 128 * t + 128], packed
            )
    packed = packed.astype(BF16)
    for e in range(peers):
        send_ref[32 * e : 32 * e + 16, :] = packed
        send_ref[32 * e + 16 : 32 * e + 32, :] = losses[16 * e : 16 * e + 16]


def project_kernel(
    width,
    heads,
    hidden,
    family_ref,
    project_hbm,
    covariance_hbm,
    logits_ref,
    value_ref,
    gating_ref,
    cov_ref,
    project_ref,
    covariance_ref,
    sems,
    query_s,
    key_s,
    value_s,
    logits_s,
    cov_s,
):
    copies = [
        pltpu.make_async_copy(project_hbm, project_ref, sems.at[0]),
        pltpu.make_async_copy(covariance_hbm, covariance_ref, sems.at[1]),
    ]
    for copy in copies:
        copy.start()
    rows, depth = family_ref.shape
    seqs = rows // width
    group = 128 // width
    normed = standardize_features(family_ref[...].astype(F32)).astype(BF16)
    copies[0].wait()
    query_s[...] = dot(normed, project_ref[:, :depth]).astype(BF16)
    key_s[...] = dot(normed, project_ref[:, depth : 2 * depth]).astype(BF16)
    value_s[...] = dot(normed, project_ref[:, 2 * depth : 3 * depth]).astype(BF16)
    gating_ref[...] = jax.nn.sigmoid(dot(normed, project_ref[:, 3 * depth :]))
    same = (iota((128, 128), 0) // width == iota((128, 128), 1) // width).astype(F32).astype(BF16)
    scale = 1.0 / math.sqrt(depth // heads)
    for t in range(depth // 128):
        cols = slice(128 * t, 128 * t + 128)
        for s in range(seqs):
            span = slice(width * s, width * s + width)
            keys = jnp.concatenate([key_s[span, cols]] * group, 0) * same
            logits_s[span, :] = dot_nt(query_s[span, cols], keys) * scale
            values = jnp.concatenate([value_s[span, cols]] * group, 0) * same
            value_ref[128 * s : 128 * (s + 1), cols] = values
        for k in range(rows // 128):
            span = slice(128 * k, 128 * (k + 1))
            logits_ref[span, cols] = logits_s[span, :].T
    copies[1].wait()
    cov_s[...] = covariance_ref[...].astype(F32)
    for b in range(hidden):
        rows_b = cov_s[pl.ds(b, hidden, stride=hidden), :].astype(BF16)
        cov_ref[0, hidden * b : hidden * (b + 1), :] = rows_b
        swapped = b ^ (group // 2)
        cov_ref[1, hidden * swapped : hidden * (swapped + 1), :] = rows_b


def attention_kernel(
    width,
    own,
    family_ref,
    got_ref,
    logits_ref,
    value_ref,
    gating_ref,
    merge_ref,
    factor_ref,
    edge_ref,
    family_out_ref,
    send_ref,
    after_s,
    weight_s,
    row_s,
    turn_s,
    line_s,
    sem,
):
    rows, depth = family_ref.shape
    seqs = rows // width
    tiles = depth // 128
    group = 128 // width
    biases = jnp.concatenate([got_ref[d, :16, :] for d in range(got_ref.shape[0])], 0)
    gated = []
    for t in range(tiles):
        cols = slice(128 * t, 128 * t + 128)
        row = iota((128, biases.shape[0]), 0) % width
        take = iota((128, biases.shape[0]), 1) == 16 * (row // own) + own * t + row % own
        bias = dot(take.astype(F32).astype(BF16), biases).T
        for k in range(rows // 128):
            span = slice(128 * k, 128 * (k + 1))
            flipped = logits_ref[span, cols] + bias
            parts = []
            for h in range(group):
                some = flipped[width * h : width * (h + 1)]
                raised = jnp.exp(some - jnp.max(some, 0, keepdims=True))
                parts.append(raised * (1.0 / jnp.sum(raised, 0, keepdims=True)))
            weight_s[span, cols] = jnp.concatenate(parts, 0).astype(BF16).T
    for t in range(tiles):
        cols = slice(128 * t, 128 * t + 128)
        mixed = jnp.concatenate(
            [
                dot(weight_s[width * s : width * (s + 1), cols], value_ref[128 * s : 128 * (s + 1), cols])
                for s in range(seqs)
            ],
            0,
        )
        gated.append((gating_ref[:, cols] * mixed).astype(BF16))
    after = (
        family_ref[...].astype(F32) + dot(jnp.concatenate(gated, 1), merge_ref[...])
    ).astype(BF16)
    after_s[...] = after
    leave = pltpu.make_async_copy(after_s, family_out_ref, sem)
    leave.start()
    ready = standardize_features(after.astype(F32)).astype(BF16)
    hidden = factor_ref.shape[0] // 2
    groups = width // group
    row_s[:, : 2 * hidden] = dot_nt(ready, factor_ref[...])
    placed = jnp.zeros((groups * seqs, 128), F32)
    for q in range(group):
        picked = jnp.concatenate(
            [row_s[pl.ds(group * g + q, seqs, stride=width), :] for g in range(groups)], 0
        )[:, :hidden].astype(BF16)
        here = iota((hidden, 128), 0) + hidden * q == iota((hidden, 128), 1)
        placed = placed + dot(picked, here.astype(F32).astype(BF16))
    for g in range(groups):
        send_ref[seqs * g : seqs * (g + 1), :] = placed[seqs * g : seqs * (g + 1), :].astype(BF16)
    turned = dot_nt(factor_ref[hidden : 2 * hidden, :], ready)
    for k in range(rows // 128):
        turn_s[hidden * k : hidden * (k + 1), :] = turned[:, 128 * k : 128 * k + 128]
    chunks = hidden // group
    for k in range(rows // 128):
        blocks = [
            turn_s[pl.ds(hidden * k + q, chunks, stride=group), :] for q in range(group)
        ]
        for p, block in enumerate(block_transpose(blocks, width)):
            first = chunks * (group * k + p)
            line_s[first : first + chunks, :] = block
    base = seqs * groups
    for g in range(chunks):
        send_ref[base + seqs * g : base + seqs * (g + 1), :] = line_s[
            pl.ds(g, seqs, stride=chunks), :
        ].astype(BF16)
    send_ref[2 * base :, :] = edge_ref[...]
    leave.wait()


def block_transpose(blocks, step):
    lane = iota(blocks[0].shape, 1)
    for shift in (2 * step, step):
        low = lane // shift % 2 == 0
        stride = shift // step
        out = list(blocks)
        for q in range(len(blocks)):
            if q // stride % 2 == 0:
                x, y = blocks[q], blocks[q + stride]
                up = pltpu.roll(y, shift, 1)
                down = pltpu.roll(x, 4 * step - shift, 1)
                out[q] = jnp.where(low, x, up)
                out[q + stride] = jnp.where(low, down, y)
        blocks = out
    return blocks


def mean(values):
    return jnp.mean(values, -1, keepdims=True)


def merge_rows(parts):
    row = iota(parts[0].shape, 0)
    step = 1
    while len(parts) > 1:
        low = row // step % 2 == 0
        parts = [
            jnp.where(low, x, y) + pltpu.roll(jnp.where(low, y, x), step, 0)
            for x, y in zip(parts[::2], parts[1::2])
        ]
        step *= 2
    return parts[0]


def pair_kernel(
    axis,
    width,
    own,
    hidden,
    seqs,
    sides_ref,
    got_ref,
    own_loss_ref,
    covariance_ref,
    edges_ref,
    cycle_ref,
    out_ref,
    grad_ref,
    right_s,
    flat_s,
    mid_s,
    unit_s,
    scale_s,
    a_s,
    b_s,
    tri_s,
):
    me = lax.axis_index(axis)
    n = sides_ref.shape[0]
    every = width * width
    group = 128 // hidden
    groups = width // group
    chunks = hidden // group
    pairs = own * width
    chans = 128
    total = seqs * n
    base = 2 * seqs * groups

    def gathered(first):
        return jnp.concatenate([sides_ref[d, first : first + seqs, :] for d in range(n)], 0)

    eye = (iota((128, 128), 0) == iota((128, 128), 1)).astype(F32).astype(BF16)
    for g in range(chunks):
        turned = dot_nt(eye, gathered(seqs * (groups + g))).astype(BF16)
        for q in range(group):
            right_s[width * g : width * (g + 1), total * q : total * (q + 1)] = turned[
                width * q : width * (q + 1), :
            ]
    block = iota((total, 128), 1) // hidden
    low_half = iota((width * chunks, 128), 1) < 64
    zero = jnp.zeros((total, 128), BF16)
    for g in range(groups):
        left = gathered(seqs * g)
        wide = left.astype(F32)
        rolled = [left] + [
            pltpu.roll(wide, hidden * d, 1).astype(BF16) for d in range(1, group)
        ]

        def placed(first, second, lane):
            return jnp.where(
                block == lane,
                rolled[(lane - first) % group],
                jnp.where(block == lane + 2, rolled[(lane + 2 - second) % group], zero),
            )

        halves = []
        for h in range(2):
            columns = []
            for even in range(0, group, 2):
                first, second = (even, even + 1) if h == 0 else (even + 1, even)
                columns.append(
                    jnp.concatenate([placed(first, second, lane) for lane in range(2)], 0)
                )
            halves.append(
                dot(
                    right_s[:, 2 * total * h : 2 * total * (h + 1)],
                    jnp.concatenate(columns, 1),
                ).astype(BF16)
            )
        for e in range(group // 2):
            x, y = (half[:, 128 * e : 128 * e + 128] for half in halves)
            for odd, outer in enumerate(
                (jnp.where(low_half, x, y), jnp.where(low_half, y, x))
            ):
                first = every // 2 * odd + width * (group // 2 * g + e)
                for c in range(chunks):
                    flat_s[first : first + width, 128 * c : 128 * c + 128] = outer[
                        width * c : width * (c + 1)
                    ]
    tiles = jnp.concatenate([got_ref[d, :16, :] for d in range(n)], 0)
    pick = (iota((width, 128), 0) == iota((width, 128), 1)).astype(F32).astype(BF16)
    masks = dot_nt(pick, tiles)

    def kept(columns, first):
        return jnp.concatenate(
            [
                jnp.broadcast_to(columns[:, first + r : first + r + 1], (width, chans))
                for r in range(own)
            ],
            0,
        )

    count = width // PARTS
    lists = [
        [2 * (count * (p // 2) + k) + p % 2 for k in range(count)] for p in range(PARTS)
    ]
    centered = jnp.where(
        iota((chans, chans), 0) == iota((chans, chans), 1), 1.0 - 1.0 / chans, -1.0 / chans
    ).astype(BF16)
    added = [
        dot(
            flat_s[
                every // 2 * (p % 2) + width * count * (p // 2) : every // 2 * (p % 2)
                + width * count * (p // 2 + 1),
                :,
            ],
            covariance_ref[p % 2],
        )
        for p in range(PARTS)
    ]
    mids = []
    for p, residues in enumerate(lists):
        edge = jnp.concatenate(
            [
                sides_ref[i // own, base + width * (i % own) : base + width * (i % own + 1), :]
                for i in residues
            ],
            0,
        ).astype(F32)
        mids.append((edge + added[p] * (1.0 / total)).astype(BF16))
    centers = [dot(mid, centered) for mid in mids]
    scales = [lax.rsqrt(mean(c * c) + EPSILON) for c in centers]
    units = [c * scale for c, scale in zip(centers, scales)]
    sides = [dot(unit.astype(BF16), edges_ref[:, : 2 * chans]) for unit in units]
    for p, residues in enumerate(lists):
        for k, i in enumerate(residues):
            here = slice(width * k, width * (k + 1))
            there = slice(width * i, width * (i + 1))
            mid_s[there, :] = mids[p][here].astype(F32)
            scale_s[there, :] = jnp.broadcast_to(scales[p][here], (width, chans))
            unit_s[there, :] = units[p][here]
            lane = 16 * (i // own) + 2 * own + i % own
            keep = jnp.broadcast_to(masks[:, lane : lane + 1], (width, chans))
            a_s[there, :] = (keep * sides[p][here, :chans]).astype(BF16).astype(F32)
            b_s[there, :] = (keep * sides[p][here, chans:]).astype(BF16).astype(F32)

    rows = pl.ds(pl.multiple_of(me * pairs, pairs), pairs)

    def rows_and_columns(ref):
        return jnp.concatenate(
            [ref[rows, :]] + [ref[pl.ds(me * own + r, width, stride=width), :] for r in range(own)],
            0,
        )

    mid = mid_s[rows, :]
    losses = jnp.concatenate([got_ref[d, 16:, :] for d in range(n)], 0)
    goal = iota((pairs, pairs), 0)
    source = goal % width // own * 16 + goal // width * own + goal % own
    place = (source == iota((pairs, pairs), 1)).astype(F32).astype(BF16)
    loss = jnp.concatenate([own_loss_ref[...].astype(F32), dot(place, losses)], 0)
    gating = jax.nn.sigmoid(
        dot(rows_and_columns(unit_s).astype(BF16), edges_ref[:, 2 * chans :])
    )
    tri = []
    for fixed, moving in ((a_s, b_s), (b_s, a_s)):
        held = fixed[rows, :]
        for r in range(own):
            mine = [held[width * r + 8 * v : width * r + 8 * v + 8] for v in range(width // 8)]
            for j in range(0, width, 8):
                parts = []
                for jj in range(j, j + 8):
                    prods = [
                        mine[v] * moving[width * jj + 8 * v : width * jj + 8 * v + 8, :]
                        for v in range(width // 8)
                    ]
                    parts.append(functools.reduce(jnp.add, prods))
                tri.append(merge_rows(parts))
    tri = jnp.concatenate(tri, 0)
    center = tri - mean(tri)
    scale_inv = lax.rsqrt(mean(center * center) + EPSILON)
    unit = center * scale_inv
    update = dot(unit[:pairs].astype(BF16), cycle_ref[...])
    out_ref[...] = (mid + gating[:pairs] * update).astype(BF16)
    grad_normed = dot_nt((loss * gating).astype(BF16), cycle_ref[...])
    tri_s[...] = (
        (
            scale_inv
            * (
                grad_normed - mean(grad_normed) - unit * mean(grad_normed * unit)
            )
        )
        .astype(BF16)
        .astype(F32)
    )

    acc = []
    for first, ref in ((0, b_s), (own, a_s)):
        sums = [[jnp.zeros((8, chans), F32) for _ in range(width // 8)] for _ in range(own)]
        for j in range(width):
            parts = [ref[width * j + 8 * v : width * j + 8 * v + 8, :] for v in range(width // 8)]
            for r in range(own):
                at = width * (first + r) + j
                row = jnp.broadcast_to(tri_s[at : at + 1, :], (8, chans))
                sums[r] = [old + row * part for old, part in zip(sums[r], parts)]
        acc += [jnp.concatenate(vregs, 0) for vregs in sums]
    keep = kept(dot_nt(pick, got_ref[me, :16, :]), 2 * own)
    gate_own = gating[:pairs]
    grad_gate = loss[:pairs] * update * gate_own * (1.0 - gate_own)
    grad_proj = jnp.concatenate(
        [
            keep * jnp.concatenate(acc[:own], 0),
            keep * jnp.concatenate(acc[own:], 0),
            grad_gate,
        ],
        1,
    ).astype(BF16)
    grad_input = dot_nt(grad_proj, edges_ref[...])
    scale_inv = scale_s[rows, :]
    unit = unit_s[rows, :]
    grad_ref[...] = loss[:pairs] + scale_inv * (
        grad_input - mean(grad_input) - unit * mean(grad_input * unit)
    )


def body_resident(
    family_matrix,
    edge_matrix,
    edge_validity,
    query_key_value_gate_matrix,
    logit_offset_matrix,
    heads_merge_matrix,
    left_right_factor_matrix,
    covariance_merge_matrix,
    edges_gate_factor_matrix,
    cycle_merge_matrix,
    loss_sensitivity,
):
    seqs, width, depth = family_matrix.shape
    own, _, chans = edge_matrix.shape
    heads = logit_offset_matrix.shape[1]
    hidden = left_right_factor_matrix.shape[1] // 2
    pairs = own * width
    every = width * width
    edge = edge_matrix.reshape(pairs, chans)
    loss = loss_sensitivity.reshape(pairs, chans)
    vmem = pl.BlockSpec(memory_space=pltpu.VMEM)
    hbm = pl.BlockSpec(memory_space=pltpu.HBM)
    family = family_matrix.reshape(seqs * width, depth)
    factor = left_right_factor_matrix.T
    sided = 2 * seqs * width * hidden // 128
    peers = width // own
    packed = pl.pallas_call(
        functools.partial(pack_kernel, width),
        out_shape=jax.ShapeDtypeStruct((32 * peers, chans), BF16),
        in_specs=[hbm] * 4,
        out_specs=vmem,
        scratch_shapes=[
            pltpu.VMEM((pairs, chans), BF16),
            pltpu.VMEM((heads, chans), BF16),
            pltpu.VMEM((pairs, chans), BF16),
            pltpu.VMEM((own, width), jnp.int32),
            pltpu.VMEM((16, 128), F32),
            pltpu.SemaphoreType.DMA((4,)),
        ],
        name="pack_pairs",
    )(edge, logit_offset_matrix.T, loss, edge_validity)
    got = lax.all_to_all(packed, "dap", split_axis=0, concat_axis=0, tiled=True)
    got = got.reshape(peers, 32, chans)
    logits, value, gating, covariance = pl.pallas_call(
        functools.partial(project_kernel, width, heads, hidden),
        out_shape=(
            jax.ShapeDtypeStruct((seqs * width, depth), F32),
            jax.ShapeDtypeStruct((seqs * 128, depth), BF16),
            jax.ShapeDtypeStruct((seqs * width, depth), F32),
            jax.ShapeDtypeStruct((2, hidden * hidden, chans), BF16),
        ),
        in_specs=[vmem, hbm, hbm],
        out_specs=(vmem,) * 4,
        scratch_shapes=[
            pltpu.VMEM(query_key_value_gate_matrix.shape, BF16),
            pltpu.VMEM(covariance_merge_matrix.shape, BF16),
            pltpu.SemaphoreType.DMA((2,)),
        ]
        + [pltpu.VMEM((seqs * width, depth), BF16)] * 3
        + [pltpu.VMEM((seqs * width, 128), F32)]
        + [pltpu.VMEM((hidden * hidden, chans), F32)],
        compiler_params=pltpu.CompilerParams(vmem_limit_bytes=16 << 20),
        cost_estimate=pl.CostEstimate(
            flops=16 * seqs * width * depth * depth,
            bytes_accessed=32 * seqs * width * depth,
            transcendentals=seqs * width * depth,
        ),
        name="project_family",
    )(
        family,
        pltpu.with_memory_space_constraint(query_key_value_gate_matrix, pltpu.HBM),
        pltpu.with_memory_space_constraint(covariance_merge_matrix, pltpu.HBM),
    )
    family_out, send = pl.pallas_call(
        functools.partial(attention_kernel, width, own),
        out_shape=(
            jax.ShapeDtypeStruct((seqs * width, depth), BF16),
            jax.ShapeDtypeStruct((sided + pairs, 128), BF16),
        ),
        in_specs=[vmem] * 8,
        out_specs=(hbm, vmem),
        scratch_shapes=[
            pltpu.VMEM((seqs * width, depth), BF16),
            pltpu.VMEM((seqs * width, depth), BF16),
            pltpu.VMEM((seqs * width, 128), F32),
            pltpu.VMEM((seqs * width * hidden // 128, 128), F32),
            pltpu.VMEM((seqs * width * hidden // 128, 128), F32),
            pltpu.SemaphoreType.DMA(()),
        ],
        compiler_params=pltpu.CompilerParams(vmem_limit_bytes=16 << 20),
        name="row_attention",
    )(family, got, logits, value, gating, heads_merge_matrix, factor, edge)
    gathered = lax.all_gather(send, "dap", axis=0, tiled=False)
    pair_out, pair_grad = pl.pallas_call(
        functools.partial(pair_kernel, "dap", width, own, hidden, seqs),
        out_shape=(
            jax.ShapeDtypeStruct((pairs, chans), BF16),
            jax.ShapeDtypeStruct((pairs, chans), F32),
        ),
        in_specs=[vmem] * 6,
        out_specs=(vmem, vmem),
        scratch_shapes=[
            pltpu.VMEM((width * hidden * hidden // 128, 128 // hidden * 128), BF16),
            pltpu.VMEM((every, hidden * hidden), BF16),
            pltpu.VMEM((every, chans), F32),
            pltpu.VMEM((every, chans), F32),
            pltpu.VMEM((every, chans), F32),
            pltpu.VMEM((every, chans), F32),
            pltpu.VMEM((every, chans), F32),
            pltpu.VMEM((2 * pairs, chans), F32),
        ],
        compiler_params=pltpu.CompilerParams(vmem_limit_bytes=16 << 20),
        name="pair_update",
    )(gathered, got, loss, covariance, edges_gate_factor_matrix, cycle_merge_matrix)
    return (
        family_out.reshape(seqs, width, depth),
        pair_out.reshape(own, width, chans),
        pair_grad.reshape(own, width, chans),
    )


def fits_resident(dap, family, edge, logit, factor):
    seqs, width, depth = family.shape
    own, _, chans = edge.shape
    return (
        own * dap == width
        and width == 32
        and factor.shape[1] == 64
        and depth == 32 * logit.shape[1]
        and depth % 128 == 0
        and chans == 128
        and own * width == 128
        and seqs % 16 == 0
        and seqs * dap == 128
    )


def body(*args):
    dap = lax.axis_size("dap")
    if fits_resident(dap, args[0], args[1], args[4], args[6]):
        return body_resident(*args)
    return body_general(*args)


def solution(mesh):
    in_specs = (
        P(("dp", "dap"), None, None),
        P(("dp", "dap"), None, None),
        P(("dp", "dap"), None),
        P(),
        P(),
        P(),
        P(),
        P(),
        P(),
        P(),
        P(("dp", "dap"), None, None),
    )
    out_specs = (
        P(("dp", "dap"), None, None),
        P(("dp", "dap"), None, None),
        P(("dp", "dap"), None, None),
    )
    return jax.shard_map(body, mesh=mesh, in_specs=in_specs, out_specs=out_specs, check_vma=False)
```

```python
import functools
import math

import jax
import jax.numpy as jnp
from jax import lax
from jax.experimental import pallas as pl
from jax.experimental.pallas import tpu as pltpu
from jax.sharding import PartitionSpec as P

EPSILON = 1e-05


def standardize_features(values):
    center = values - jnp.mean(values, -1, keepdims=True)
    scale_inv = lax.rsqrt(jnp.mean(center * center, -1, keepdims=True) + EPSILON)
    return center * scale_inv


def norm_back(values, grad_out):
    center = values - jnp.mean(values, -1, keepdims=True)
    scale_inv = lax.rsqrt(jnp.mean(center * center, -1, keepdims=True) + EPSILON)
    standardized_source = center * scale_inv
    return scale_inv * (
        grad_out
        - jnp.mean(grad_out, -1, keepdims=True)
        - standardized_source * jnp.mean(grad_out * standardized_source, -1, keepdims=True)
    )


def lateral_heads_mixing(
    family_shard_slice, logit_offset_whole, query_key_value_gate_matrix, heads_merge_matrix
):
    homolog_number, amino_number, feature_depth = family_shard_slice.shape
    head_count = logit_offset_whole.shape[1]
    head_size = feature_depth // head_count
    standardized_source = standardize_features(family_shard_slice.astype(jnp.float32)).astype(
        jnp.bfloat16
    )
    projected = jnp.dot(
        standardized_source.reshape(-1, feature_depth),
        query_key_value_gate_matrix,
        preferred_element_type=jnp.float32,
    )
    projected = projected.reshape(homolog_number, amino_number, 4 * feature_depth)
    shape_heads = (homolog_number, amino_number, head_count, head_size)
    queries = projected[..., :feature_depth].astype(jnp.bfloat16).reshape(shape_heads)
    key_rows = (
        projected[..., feature_depth : 2 * feature_depth].astype(jnp.bfloat16).reshape(shape_heads)
    )
    value_rows = (
        projected[..., 2 * feature_depth : 3 * feature_depth]
        .astype(jnp.bfloat16)
        .reshape(shape_heads)
    )
    gating = jax.nn.sigmoid(projected[..., 3 * feature_depth :])
    logits = jnp.einsum("sihd,sjhd->sihj", queries, key_rows, preferred_element_type=jnp.float32)
    logits = logits / math.sqrt(head_size) + logit_offset_whole.astype(jnp.float32)[None]
    weights = jax.nn.softmax(logits, axis=-1).astype(jnp.bfloat16)
    mixed = jnp.einsum("sihj,sjhd->sihd", weights, value_rows, preferred_element_type=jnp.float32)
    gated = (gating * mixed.reshape(homolog_number, amino_number, feature_depth)).astype(
        jnp.bfloat16
    )
    edge_increment = jnp.dot(
        gated.reshape(-1, feature_depth), heads_merge_matrix, preferred_element_type=jnp.float32
    )
    return (
        family_shard_slice.astype(jnp.float32)
        + edge_increment.reshape(homolog_number, amino_number, feature_depth)
    ).astype(jnp.bfloat16)


def pair_projection_step(alignment_rows, left_right_factor_matrix):
    standardized_source = standardize_features(alignment_rows.astype(jnp.float32)).astype(
        jnp.bfloat16
    )
    edge_result = jnp.dot(
        standardized_source.reshape(-1, alignment_rows.shape[2]),
        left_right_factor_matrix,
        preferred_element_type=jnp.float32,
    )
    return edge_result.reshape(alignment_rows.shape[0], alignment_rows.shape[1], -1).astype(
        jnp.bfloat16
    )


def body_general(
    family_matrix,
    edge_matrix,
    edge_validity,
    query_key_value_gate_matrix,
    logit_offset_matrix,
    heads_merge_matrix,
    left_right_factor_matrix,
    covariance_merge_matrix,
    edges_gate_factor_matrix,
    cycle_merge_matrix,
    loss_sensitivity,
):
    res_rows, width, pair_chans = edge_matrix.shape
    pair_normed = standardize_features(edge_matrix.astype(jnp.float32)).astype(jnp.bfloat16)
    bias_local = jnp.einsum(
        "ijc,ch->ihj", pair_normed, logit_offset_matrix, preferred_element_type=jnp.float32
    ).astype(jnp.bfloat16)
    logit_offset_whole = lax.all_gather(bias_local, "dap", axis=0, tiled=True)
    homolog_lines = family_matrix.shape[0]
    homolog_subset = math.gcd(homolog_lines, 8)
    batched_lines = family_matrix.reshape(
        homolog_lines // homolog_subset,
        homolog_subset,
        family_matrix.shape[1],
        family_matrix.shape[2],
    )
    family_after_heads = lax.map(
        lambda family_shard_slice: lateral_heads_mixing(
            family_shard_slice, logit_offset_whole, query_key_value_gate_matrix, heads_merge_matrix
        ),
        batched_lines,
    ).reshape(family_matrix.shape)
    hidden = left_right_factor_matrix.shape[1] // 2
    weight_f32 = covariance_merge_matrix.astype(jnp.float32)
    alignment_columns = lax.all_to_all(
        family_after_heads, "dap", split_axis=1, concat_axis=0, tiled=True
    )
    edge_result = pair_projection_step(alignment_columns, left_right_factor_matrix)
    left_part = edge_result[..., :hidden]
    right_part = edge_result[..., hidden:]
    sequence_full_count = alignment_columns.shape[0]
    shard_in = lax.all_gather(right_part, "dap", axis=1, tiled=True)
    outer_sum = (
        jnp.einsum("sia,sjb->ijab", left_part, shard_in, preferred_element_type=jnp.float32)
        / sequence_full_count
    )
    row_count = shard_in.shape[1]
    flat = outer_sum.reshape(res_rows * row_count, hidden * hidden)
    edge_increment = jnp.dot(flat, weight_f32, precision=lax.Precision.HIGHEST).reshape(
        res_rows, row_count, pair_chans
    )
    pair_mid = (edge_matrix.astype(jnp.float32) + edge_increment).astype(jnp.bfloat16)
    tri_normed = standardize_features(pair_mid.astype(jnp.float32)).astype(jnp.bfloat16)
    tri_proj = jnp.dot(
        tri_normed.reshape(-1, pair_chans),
        edges_gate_factor_matrix,
        preferred_element_type=jnp.float32,
    ).reshape(res_rows, width, 3 * pair_chans)
    mask_f = edge_validity.astype(jnp.float32)[..., None]
    side_a = (mask_f * tri_proj[..., :pair_chans]).astype(jnp.bfloat16)
    side_b = (mask_f * tri_proj[..., pair_chans : 2 * pair_chans]).astype(jnp.bfloat16)
    gating = jax.nn.sigmoid(tri_proj[..., 2 * pair_chans :])
    tri_prod = jnp.einsum(
        "ikc,jkc->ijc",
        side_a,
        lax.all_gather(side_b, "dap", axis=0, tiled=True),
        preferred_element_type=jnp.float32,
    )
    prod_normed = standardize_features(tri_prod).astype(jnp.bfloat16)
    tri_update = jnp.dot(
        prod_normed.reshape(-1, pair_chans), cycle_merge_matrix, preferred_element_type=jnp.float32
    ).reshape(res_rows, width, pair_chans)
    pair_output = (pair_mid.astype(jnp.float32) + gating * tri_update).astype(jnp.bfloat16)
    cot_f32 = loss_sensitivity.astype(jnp.float32)
    grad_update = (cot_f32 * gating).astype(jnp.bfloat16)
    grad_normed = jnp.dot(
        grad_update.reshape(-1, pair_chans),
        cycle_merge_matrix.T,
        preferred_element_type=jnp.float32,
    ).reshape(res_rows, width, pair_chans)
    grad_prod = norm_back(tri_prod, grad_normed).astype(jnp.bfloat16)
    grad_part = grad_prod
    grad_a = jnp.einsum(
        "ijc,jkc->ikc",
        grad_part,
        lax.all_gather(side_b, "dap", axis=0, tiled=True),
        preferred_element_type=jnp.float32,
    )
    grad_part = grad_prod
    grad_b = lax.psum_scatter(
        jnp.einsum("ijc,ikc->jkc", grad_part, side_a, preferred_element_type=jnp.float32).astype(
            jnp.bfloat16
        ),
        "dap",
        scatter_dimension=0,
        tiled=True,
    ).astype(jnp.float32)
    grad_gate = cot_f32 * tri_update * gating * (1.0 - gating)
    grad_proj = jnp.concatenate([mask_f * grad_a, mask_f * grad_b, grad_gate], -1).astype(
        jnp.bfloat16
    )
    grad_input = jnp.dot(
        grad_proj.reshape(-1, 3 * pair_chans),
        edges_gate_factor_matrix.T,
        preferred_element_type=jnp.float32,
    ).reshape(res_rows, width, pair_chans)
    pair_gradient = cot_f32 + norm_back(pair_mid.astype(jnp.float32), grad_input)
    return (family_after_heads, pair_output, pair_gradient)


F32 = jnp.float32
BF16 = jnp.bfloat16
NT = (((1,), (1,)), ((), ()))
PARTS = 2


def dot(a, b):
    return jnp.dot(a, b, preferred_element_type=F32)


def dot_nt(a, b):
    return lax.dot_general(a, b, NT, preferred_element_type=F32)


def iota(shape, dim):
    return lax.broadcasted_iota(jnp.int32, shape, dim)


def pack_kernel(
    width, edge_ref, weight_ref, loss_ref, mask_ref, send_ref, edge_s, weight_s, loss_s, mask_s,
    tile_s, sems
):
    copies = [
        pltpu.make_async_copy(source, target, sems.at[k])
        for k, (source, target) in enumerate(
            (
                (edge_ref, edge_s),
                (weight_ref, weight_s),
                (loss_ref, loss_s),
                (mask_ref, mask_s),
            )
        )
    ]
    for copy in copies:
        copy.start()
    rows, chans = edge_s.shape
    heads = weight_s.shape[0]
    own = rows // width
    lanes = heads * width
    peers = width // own
    spread = (iota((heads, lanes), 0) == iota((heads, lanes), 1) // width).astype(F32)
    keep = iota((width, lanes), 0) == iota((width, lanes), 1) % width
    goal = iota((rows, rows), 0)
    source = goal % own * width + goal // (own * own) * own + goal // own % own
    place = (source == iota((rows, rows), 1)).astype(F32).astype(BF16)
    tile_s[...] = jnp.zeros(tile_s.shape, F32)
    for copy in copies:
        copy.wait()
    weight = lax.dot_general(
        weight_s[...], spread.astype(BF16), (((0,), (0,)), ((), ())), preferred_element_type=F32
    ).astype(BF16)
    column = dot(jnp.ones((8, chans), BF16), weight)[:1]
    every = dot(edge_s[...], weight)
    edge = edge_s[...].astype(F32)
    middle = jnp.mean(edge, -1, keepdims=True)
    center = edge - middle
    scale = lax.rsqrt(jnp.mean(center * center, -1, keepdims=True) + EPSILON)
    bias = scale * (every - middle * column)
    losses = dot(place, loss_s[...]).astype(BF16)
    tile_s[2 * own : 3 * own, :width] = mask_s[...].astype(F32)
    packed = tile_s[...]
    for r in range(own):
        picked = jnp.where(keep, bias[width * r : width * (r + 1)], 0.0)
        total = jnp.sum(picked, 0, keepdims=True)
        for t in range(lanes // 128):
            packed = jnp.where(
                iota((16, 128), 0) == own * t + r, total[:, 128 * t : 128 * t + 128], packed
            )
    packed = packed.astype(BF16)
    for e in range(peers):
        send_ref[32 * e : 32 * e + 16, :] = packed
        send_ref[32 * e + 16 : 32 * e + 32, :] = losses[16 * e : 16 * e + 16]


def project_kernel(
    width,
    heads,
    hidden,
    family_ref,
    project_hbm,
    covariance_hbm,
    logits_ref,
    value_ref,
    gating_ref,
    cov_ref,
    project_ref,
    covariance_ref,
    sems,
    query_s,
    key_s,
    value_s,
    logits_s,
    cov_s,
):
    copies = [
        pltpu.make_async_copy(project_hbm, project_ref, sems.at[0]),
        pltpu.make_async_copy(covariance_hbm, covariance_ref, sems.at[1]),
    ]
    for copy in copies:
        copy.start()
    rows, depth = family_ref.shape
    seqs = rows // width
    group = 128 // width
    normed = standardize_features(family_ref[...].astype(F32)).astype(BF16)
    copies[0].wait()
    query_s[...] = dot(normed, project_ref[:, :depth]).astype(BF16)
    key_s[...] = dot(normed, project_ref[:, depth : 2 * depth]).astype(BF16)
    value_s[...] = dot(normed, project_ref[:, 2 * depth : 3 * depth]).astype(BF16)
    gating_ref[...] = jax.nn.sigmoid(dot(normed, project_ref[:, 3 * depth :]))
    same = (iota((128, 128), 0) // width == iota((128, 128), 1) // width).astype(F32).astype(BF16)
    scale = 1.0 / math.sqrt(depth // heads)
    for t in range(depth // 128):
        cols = slice(128 * t, 128 * t + 128)
        for s in range(seqs):
            span = slice(width * s, width * s + width)
            keys = jnp.concatenate([key_s[span, cols]] * group, 0) * same
            logits_s[span, :] = dot_nt(query_s[span, cols], keys) * scale
            values = jnp.concatenate([value_s[span, cols]] * group, 0) * same
            value_ref[128 * s : 128 * (s + 1), cols] = values
        for k in range(rows // 128):
            span = slice(128 * k, 128 * (k + 1))
            logits_ref[span, cols] = logits_s[span, :].T
    copies[1].wait()
    cov_s[...] = covariance_ref[...].astype(F32)
    for b in range(hidden):
        rows_b = cov_s[pl.ds(b, hidden, stride=hidden), :].astype(BF16)
        cov_ref[0, hidden * b : hidden * (b + 1), :] = rows_b
        swapped = b ^ (group // 2)
        cov_ref[1, hidden * swapped : hidden * (swapped + 1), :] = rows_b


def attention_kernel(
    width,
    own,
    family_ref,
    got_ref,
    logits_ref,
    value_ref,
    gating_ref,
    merge_ref,
    factor_ref,
    edge_ref,
    family_out_ref,
    send_ref,
    after_s,
    weight_s,
    row_s,
    turn_s,
    line_s,
    sem,
):
    rows, depth = family_ref.shape
    seqs = rows // width
    tiles = depth // 128
    group = 128 // width
    biases = jnp.concatenate([got_ref[d, :16, :] for d in range(got_ref.shape[0])], 0)
    gated = []
    for t in range(tiles):
        cols = slice(128 * t, 128 * t + 128)
        row = iota((128, biases.shape[0]), 0) % width
        take = iota((128, biases.shape[0]), 1) == 16 * (row // own) + own * t + row % own
        bias = dot(take.astype(F32).astype(BF16), biases).T
        for k in range(rows // 128):
            span = slice(128 * k, 128 * (k + 1))
            flipped = logits_ref[span, cols] + bias
            parts = []
            for h in range(group):
                some = flipped[width * h : width * (h + 1)]
                raised = jnp.exp(some - jnp.max(some, 0, keepdims=True))
                parts.append(raised * (1.0 / jnp.sum(raised, 0, keepdims=True)))
            weight_s[span, cols] = jnp.concatenate(parts, 0).astype(BF16).T
    for t in range(tiles):
        cols = slice(128 * t, 128 * t + 128)
        mixed = jnp.concatenate(
            [
                dot(weight_s[width * s : width * (s + 1), cols], value_ref[128 * s : 128 * (s + 1), cols])
                for s in range(seqs)
            ],
            0,
        )
        gated.append((gating_ref[:, cols] * mixed).astype(BF16))
    after = (
        family_ref[...].astype(F32) + dot(jnp.concatenate(gated, 1), merge_ref[...])
    ).astype(BF16)
    after_s[...] = after
    leave = pltpu.make_async_copy(after_s, family_out_ref, sem)
    leave.start()
    ready = standardize_features(after.astype(F32)).astype(BF16)
    hidden = factor_ref.shape[0] // 2
    groups = width // group
    row_s[:, : 2 * hidden] = dot_nt(ready, factor_ref[...])
    placed = jnp.zeros((groups * seqs, 128), F32)
    for q in range(group):
        picked = jnp.concatenate(
            [row_s[pl.ds(group * g + q, seqs, stride=width), :] for g in range(groups)], 0
        )[:, :hidden].astype(BF16)
        here = iota((hidden, 128), 0) + hidden * q == iota((hidden, 128), 1)
        placed = placed + dot(picked, here.astype(F32).astype(BF16))
    for g in range(groups):
        send_ref[seqs * g : seqs * (g + 1), :] = placed[seqs * g : seqs * (g + 1), :].astype(BF16)
    turned = dot_nt(factor_ref[hidden : 2 * hidden, :], ready)
    for k in range(rows // 128):
        turn_s[hidden * k : hidden * (k + 1), :] = turned[:, 128 * k : 128 * k + 128]
    chunks = hidden // group
    for k in range(rows // 128):
        blocks = [
            turn_s[pl.ds(hidden * k + q, chunks, stride=group), :] for q in range(group)
        ]
        for p, block in enumerate(block_transpose(blocks, width)):
            first = chunks * (group * k + p)
            line_s[first : first + chunks, :] = block
    base = seqs * groups
    for g in range(chunks):
        send_ref[base + seqs * g : base + seqs * (g + 1), :] = line_s[
            pl.ds(g, seqs, stride=chunks), :
        ].astype(BF16)
    send_ref[2 * base :, :] = edge_ref[...]
    leave.wait()


def block_transpose(blocks, step):
    lane = iota(blocks[0].shape, 1)
    for shift in (2 * step, step):
        low = lane // shift % 2 == 0
        stride = shift // step
        out = list(blocks)
        for q in range(len(blocks)):
            if q // stride % 2 == 0:
                x, y = blocks[q], blocks[q + stride]
                up = pltpu.roll(y, shift, 1)
                down = pltpu.roll(x, 4 * step - shift, 1)
                out[q] = jnp.where(low, x, up)
                out[q + stride] = jnp.where(low, down, y)
        blocks = out
    return blocks


def mean(values):
    return jnp.mean(values, -1, keepdims=True)


def merge_rows(parts):
    row = iota(parts[0].shape, 0)
    step = 1
    while len(parts) > 1:
        low = row // step % 2 == 0
        parts = [
            jnp.where(low, x, y) + pltpu.roll(jnp.where(low, y, x), step, 0)
            for x, y in zip(parts[::2], parts[1::2])
        ]
        step *= 2
    return parts[0]


def pair_kernel(
    axis,
    width,
    own,
    hidden,
    seqs,
    sides_ref,
    got_ref,
    own_loss_ref,
    covariance_ref,
    edges_ref,
    cycle_ref,
    out_ref,
    grad_ref,
    right_s,
    flat_s,
    mid_s,
    unit_s,
    scale_s,
    a_s,
    b_s,
    tri_s,
):
    me = lax.axis_index(axis)
    n = sides_ref.shape[0]
    every = width * width
    group = 128 // hidden
    groups = width // group
    chunks = hidden // group
    pairs = own * width
    chans = 128
    total = seqs * n
    base = 2 * seqs * groups

    def gathered(first):
        return jnp.concatenate([sides_ref[d, first : first + seqs, :] for d in range(n)], 0)

    for g in range(chunks):
        turned = gathered(seqs * (groups + g)).T
        for q in range(group):
            right_s[width * g : width * (g + 1), total * q : total * (q + 1)] = turned[
                width * q : width * (q + 1), :
            ]
    block = iota((total, 128), 1) // hidden
    low_half = iota((width * chunks, 128), 1) < 64
    zero = jnp.zeros((total, 128), BF16)
    for g in range(groups):
        left = gathered(seqs * g)
        wide = left.astype(F32)
        rolled = [left] + [
            pltpu.roll(wide, hidden * d, 1).astype(BF16) for d in range(1, group)
        ]

        def placed(first, second, lane):
            return jnp.where(
                block == lane,
                rolled[(lane - first) % group],
                jnp.where(block == lane + 2, rolled[(lane + 2 - second) % group], zero),
            )

        halves = []
        for h in range(2):
            columns = []
            for even in range(0, group, 2):
                first, second = (even, even + 1) if h == 0 else (even + 1, even)
                columns.append(
                    jnp.concatenate([placed(first, second, lane) for lane in range(2)], 0)
                )
            halves.append(
                dot(
                    right_s[:, 2 * total * h : 2 * total * (h + 1)],
                    jnp.concatenate(columns, 1),
                ).astype(BF16)
            )
        for e in range(group // 2):
            x, y = (half[:, 128 * e : 128 * e + 128] for half in halves)
            for odd, outer in enumerate(
                (jnp.where(low_half, x, y), jnp.where(low_half, y, x))
            ):
                first = every // 2 * odd + width * (group // 2 * g + e)
                for c in range(chunks):
                    flat_s[first : first + width, 128 * c : 128 * c + 128] = outer[
                        width * c : width * (c + 1)
                    ]
    tiles = jnp.concatenate([got_ref[d, :16, :] for d in range(n)], 0)
    pick = (iota((width, 128), 0) == iota((width, 128), 1)).astype(F32).astype(BF16)
    masks = dot_nt(pick, tiles)

    def kept(columns, first):
        return jnp.concatenate(
            [
                jnp.broadcast_to(columns[:, first + r : first + r + 1], (width, chans))
                for r in range(own)
            ],
            0,
        )

    count = width // PARTS
    lists = [
        [2 * (count * (p // 2) + k) + p % 2 for k in range(count)] for p in range(PARTS)
    ]
    centered = jnp.where(
        iota((chans, chans), 0) == iota((chans, chans), 1), 1.0 - 1.0 / chans, -1.0 / chans
    ).astype(BF16)
    added = [
        dot(
            flat_s[
                every // 2 * (p % 2) + width * count * (p // 2) : every // 2 * (p % 2)
                + width * count * (p // 2 + 1),
                :,
            ],
            covariance_ref[p % 2],
        )
        for p in range(PARTS)
    ]
    mids = []
    for p, residues in enumerate(lists):
        edge = jnp.concatenate(
            [
                sides_ref[i // own, base + width * (i % own) : base + width * (i % own + 1), :]
                for i in residues
            ],
            0,
        ).astype(F32)
        mids.append((edge + added[p] * (1.0 / total)).astype(BF16))
    centers = [dot(mid, centered) for mid in mids]
    scales = [lax.rsqrt(mean(c * c) + EPSILON) for c in centers]
    units = [c * scale for c, scale in zip(centers, scales)]
    sides = [dot(unit.astype(BF16), edges_ref[:, : 2 * chans]) for unit in units]
    for p, residues in enumerate(lists):
        for k, i in enumerate(residues):
            here = slice(width * k, width * (k + 1))
            there = slice(width * i, width * (i + 1))
            mid_s[there, :] = mids[p][here].astype(F32)
            scale_s[there, :] = jnp.broadcast_to(scales[p][here], (width, chans))
            unit_s[there, :] = units[p][here]
            lane = 16 * (i // own) + 2 * own + i % own
            keep = jnp.broadcast_to(masks[:, lane : lane + 1], (width, chans))
            a_s[there, :] = (keep * sides[p][here, :chans]).astype(BF16).astype(F32)
            b_s[there, :] = (keep * sides[p][here, chans:]).astype(BF16).astype(F32)

    rows = pl.ds(pl.multiple_of(me * pairs, pairs), pairs)

    def rows_and_columns(ref):
        return jnp.concatenate(
            [ref[rows, :]] + [ref[pl.ds(me * own + r, width, stride=width), :] for r in range(own)],
            0,
        )

    mid = mid_s[rows, :]
    losses = jnp.concatenate([got_ref[d, 16:, :] for d in range(n)], 0)
    goal = iota((pairs, pairs), 0)
    source = goal % width // own * 16 + goal // width * own + goal % own
    place = (source == iota((pairs, pairs), 1)).astype(F32).astype(BF16)
    loss = jnp.concatenate([own_loss_ref[...].astype(F32), dot(place, losses)], 0)
    gating = jax.nn.sigmoid(
        dot(rows_and_columns(unit_s).astype(BF16), edges_ref[:, 2 * chans :])
    )
    tri = []
    for fixed, moving in ((a_s, b_s), (b_s, a_s)):
        held = fixed[rows, :]
        for r in range(own):
            mine = [held[width * r + 8 * v : width * r + 8 * v + 8] for v in range(width // 8)]
            for j in range(0, width, 8):
                parts = []
                for jj in range(j, j + 8):
                    prods = [
                        mine[v] * moving[width * jj + 8 * v : width * jj + 8 * v + 8, :]
                        for v in range(width // 8)
                    ]
                    parts.append(functools.reduce(jnp.add, prods))
                tri.append(merge_rows(parts))
    tri = jnp.concatenate(tri, 0)
    center = tri - mean(tri)
    scale_inv = lax.rsqrt(mean(center * center) + EPSILON)
    unit = center * scale_inv
    update = dot(unit[:pairs].astype(BF16), cycle_ref[...])
    out_ref[...] = (mid + gating[:pairs] * update).astype(BF16)
    grad_normed = dot_nt((loss * gating).astype(BF16), cycle_ref[...])
    tri_s[...] = (
        (
            scale_inv
            * (
                grad_normed - mean(grad_normed) - unit * mean(grad_normed * unit)
            )
        )
        .astype(BF16)
        .astype(F32)
    )

    acc = []
    for first, ref in ((0, b_s), (own, a_s)):
        sums = [[jnp.zeros((8, chans), F32) for _ in range(width // 8)] for _ in range(own)]
        for j in range(width):
            parts = [ref[width * j + 8 * v : width * j + 8 * v + 8, :] for v in range(width // 8)]
            for r in range(own):
                at = width * (first + r) + j
                row = jnp.broadcast_to(tri_s[at : at + 1, :], (8, chans))
                sums[r] = [old + row * part for old, part in zip(sums[r], parts)]
        acc += [jnp.concatenate(vregs, 0) for vregs in sums]
    keep = kept(dot_nt(pick, got_ref[me, :16, :]), 2 * own)
    gate_own = gating[:pairs]
    grad_gate = loss[:pairs] * update * gate_own * (1.0 - gate_own)
    grad_proj = jnp.concatenate(
        [
            keep * jnp.concatenate(acc[:own], 0),
            keep * jnp.concatenate(acc[own:], 0),
            grad_gate,
        ],
        1,
    ).astype(BF16)
    grad_input = dot_nt(grad_proj, edges_ref[...])
    scale_inv = scale_s[rows, :]
    unit = unit_s[rows, :]
    grad_ref[...] = loss[:pairs] + scale_inv * (
        grad_input - mean(grad_input) - unit * mean(grad_input * unit)
    )


def body_resident(
    family_matrix,
    edge_matrix,
    edge_validity,
    query_key_value_gate_matrix,
    logit_offset_matrix,
    heads_merge_matrix,
    left_right_factor_matrix,
    covariance_merge_matrix,
    edges_gate_factor_matrix,
    cycle_merge_matrix,
    loss_sensitivity,
):
    seqs, width, depth = family_matrix.shape
    own, _, chans = edge_matrix.shape
    heads = logit_offset_matrix.shape[1]
    hidden = left_right_factor_matrix.shape[1] // 2
    pairs = own * width
    every = width * width
    edge = edge_matrix.reshape(pairs, chans)
    loss = loss_sensitivity.reshape(pairs, chans)
    vmem = pl.BlockSpec(memory_space=pltpu.VMEM)
    hbm = pl.BlockSpec(memory_space=pltpu.HBM)
    family = family_matrix.reshape(seqs * width, depth)
    factor = left_right_factor_matrix.T
    sided = 2 * seqs * width * hidden // 128
    peers = width // own
    packed = pl.pallas_call(
        functools.partial(pack_kernel, width),
        out_shape=jax.ShapeDtypeStruct((32 * peers, chans), BF16),
        in_specs=[hbm] * 4,
        out_specs=vmem,
        scratch_shapes=[
            pltpu.VMEM((pairs, chans), BF16),
            pltpu.VMEM((heads, chans), BF16),
            pltpu.VMEM((pairs, chans), BF16),
            pltpu.VMEM((own, width), jnp.int32),
            pltpu.VMEM((16, 128), F32),
            pltpu.SemaphoreType.DMA((4,)),
        ],
        name="pack_pairs",
    )(edge, logit_offset_matrix.T, loss, edge_validity)
    got = lax.all_to_all(packed, "dap", split_axis=0, concat_axis=0, tiled=True)
    got = got.reshape(peers, 32, chans)
    logits, value, gating, covariance = pl.pallas_call(
        functools.partial(project_kernel, width, heads, hidden),
        out_shape=(
            jax.ShapeDtypeStruct((seqs * width, depth), F32),
            jax.ShapeDtypeStruct((seqs * 128, depth), BF16),
            jax.ShapeDtypeStruct((seqs * width, depth), F32),
            jax.ShapeDtypeStruct((2, hidden * hidden, chans), BF16),
        ),
        in_specs=[vmem, hbm, hbm],
        out_specs=(vmem,) * 4,
        scratch_shapes=[
            pltpu.VMEM(query_key_value_gate_matrix.shape, BF16),
            pltpu.VMEM(covariance_merge_matrix.shape, BF16),
            pltpu.SemaphoreType.DMA((2,)),
        ]
        + [pltpu.VMEM((seqs * width, depth), BF16)] * 3
        + [pltpu.VMEM((seqs * width, 128), F32)]
        + [pltpu.VMEM((hidden * hidden, chans), F32)],
        compiler_params=pltpu.CompilerParams(vmem_limit_bytes=16 << 20),
        cost_estimate=pl.CostEstimate(
            flops=16 * seqs * width * depth * depth,
            bytes_accessed=32 * seqs * width * depth,
            transcendentals=seqs * width * depth,
        ),
        name="project_family",
    )(
        family,
        pltpu.with_memory_space_constraint(query_key_value_gate_matrix, pltpu.HBM),
        pltpu.with_memory_space_constraint(covariance_merge_matrix, pltpu.HBM),
    )
    family_out, send = pl.pallas_call(
        functools.partial(attention_kernel, width, own),
        out_shape=(
            jax.ShapeDtypeStruct((seqs * width, depth), BF16),
            jax.ShapeDtypeStruct((sided + pairs, 128), BF16),
        ),
        in_specs=[vmem] * 8,
        out_specs=(hbm, vmem),
        scratch_shapes=[
            pltpu.VMEM((seqs * width, depth), BF16),
            pltpu.VMEM((seqs * width, depth), BF16),
            pltpu.VMEM((seqs * width, 128), F32),
            pltpu.VMEM((seqs * width * hidden // 128, 128), F32),
            pltpu.VMEM((seqs * width * hidden // 128, 128), F32),
            pltpu.SemaphoreType.DMA(()),
        ],
        compiler_params=pltpu.CompilerParams(vmem_limit_bytes=16 << 20),
        name="row_attention",
    )(family, got, logits, value, gating, heads_merge_matrix, factor, edge)
    gathered = lax.all_gather(send, "dap", axis=0, tiled=False)
    pair_out, pair_grad = pl.pallas_call(
        functools.partial(pair_kernel, "dap", width, own, hidden, seqs),
        out_shape=(
            jax.ShapeDtypeStruct((pairs, chans), BF16),
            jax.ShapeDtypeStruct((pairs, chans), F32),
        ),
        in_specs=[vmem] * 6,
        out_specs=(vmem, vmem),
        scratch_shapes=[
            pltpu.VMEM((width * hidden * hidden // 128, 128 // hidden * 128), BF16),
            pltpu.VMEM((every, hidden * hidden), BF16),
            pltpu.VMEM((every, chans), F32),
            pltpu.VMEM((every, chans), F32),
            pltpu.VMEM((every, chans), F32),
            pltpu.VMEM((every, chans), F32),
            pltpu.VMEM((every, chans), F32),
            pltpu.VMEM((2 * pairs, chans), F32),
        ],
        compiler_params=pltpu.CompilerParams(vmem_limit_bytes=16 << 20),
        name="pair_update",
    )(gathered, got, loss, covariance, edges_gate_factor_matrix, cycle_merge_matrix)
    return (
        family_out.reshape(seqs, width, depth),
        pair_out.reshape(own, width, chans),
        pair_grad.reshape(own, width, chans),
    )


def fits_resident(dap, family, edge, logit, factor):
    seqs, width, depth = family.shape
    own, _, chans = edge.shape
    return (
        own * dap == width
        and width == 32
        and factor.shape[1] == 64
        and depth == 32 * logit.shape[1]
        and depth % 128 == 0
        and chans == 128
        and own * width == 128
        and seqs % 16 == 0
        and seqs * dap == 128
    )


def body(*args):
    dap = lax.axis_size("dap")
    if fits_resident(dap, args[0], args[1], args[4], args[6]):
        return body_resident(*args)
    return body_general(*args)


def solution(mesh):
    in_specs = (
        P(("dp", "dap"), None, None),
        P(("dp", "dap"), None, None),
        P(("dp", "dap"), None),
        P(),
        P(),
        P(),
        P(),
        P(),
        P(),
        P(),
        P(("dp", "dap"), None, None),
    )
    out_specs = (
        P(("dp", "dap"), None, None),
        P(("dp", "dap"), None, None),
        P(("dp", "dap"), None, None),
    )
    return jax.shard_map(body, mesh=mesh, in_specs=in_specs, out_specs=out_specs, check_vma=False)
```

```python
import functools
import math

import jax
import jax.numpy as jnp
from jax import lax
from jax.experimental import pallas as pl
from jax.experimental.pallas import tpu as pltpu
from jax.sharding import PartitionSpec as P

EPSILON = 1e-05


def standardize_features(values):
    center = values - jnp.mean(values, -1, keepdims=True)
    scale_inv = lax.rsqrt(jnp.mean(center * center, -1, keepdims=True) + EPSILON)
    return center * scale_inv


def norm_back(values, grad_out):
    center = values - jnp.mean(values, -1, keepdims=True)
    scale_inv = lax.rsqrt(jnp.mean(center * center, -1, keepdims=True) + EPSILON)
    standardized_source = center * scale_inv
    return scale_inv * (
        grad_out
        - jnp.mean(grad_out, -1, keepdims=True)
        - standardized_source * jnp.mean(grad_out * standardized_source, -1, keepdims=True)
    )


def lateral_heads_mixing(
    family_shard_slice, logit_offset_whole, query_key_value_gate_matrix, heads_merge_matrix
):
    homolog_number, amino_number, feature_depth = family_shard_slice.shape
    head_count = logit_offset_whole.shape[1]
    head_size = feature_depth // head_count
    standardized_source = standardize_features(family_shard_slice.astype(jnp.float32)).astype(
        jnp.bfloat16
    )
    projected = jnp.dot(
        standardized_source.reshape(-1, feature_depth),
        query_key_value_gate_matrix,
        preferred_element_type=jnp.float32,
    )
    projected = projected.reshape(homolog_number, amino_number, 4 * feature_depth)
    shape_heads = (homolog_number, amino_number, head_count, head_size)
    queries = projected[..., :feature_depth].astype(jnp.bfloat16).reshape(shape_heads)
    key_rows = (
        projected[..., feature_depth : 2 * feature_depth].astype(jnp.bfloat16).reshape(shape_heads)
    )
    value_rows = (
        projected[..., 2 * feature_depth : 3 * feature_depth]
        .astype(jnp.bfloat16)
        .reshape(shape_heads)
    )
    gating = jax.nn.sigmoid(projected[..., 3 * feature_depth :])
    logits = jnp.einsum("sihd,sjhd->sihj", queries, key_rows, preferred_element_type=jnp.float32)
    logits = logits / math.sqrt(head_size) + logit_offset_whole.astype(jnp.float32)[None]
    weights = jax.nn.softmax(logits, axis=-1).astype(jnp.bfloat16)
    mixed = jnp.einsum("sihj,sjhd->sihd", weights, value_rows, preferred_element_type=jnp.float32)
    gated = (gating * mixed.reshape(homolog_number, amino_number, feature_depth)).astype(
        jnp.bfloat16
    )
    edge_increment = jnp.dot(
        gated.reshape(-1, feature_depth), heads_merge_matrix, preferred_element_type=jnp.float32
    )
    return (
        family_shard_slice.astype(jnp.float32)
        + edge_increment.reshape(homolog_number, amino_number, feature_depth)
    ).astype(jnp.bfloat16)


def pair_projection_step(alignment_rows, left_right_factor_matrix):
    standardized_source = standardize_features(alignment_rows.astype(jnp.float32)).astype(
        jnp.bfloat16
    )
    edge_result = jnp.dot(
        standardized_source.reshape(-1, alignment_rows.shape[2]),
        left_right_factor_matrix,
        preferred_element_type=jnp.float32,
    )
    return edge_result.reshape(alignment_rows.shape[0], alignment_rows.shape[1], -1).astype(
        jnp.bfloat16
    )


def body_general(
    family_matrix,
    edge_matrix,
    edge_validity,
    query_key_value_gate_matrix,
    logit_offset_matrix,
    heads_merge_matrix,
    left_right_factor_matrix,
    covariance_merge_matrix,
    edges_gate_factor_matrix,
    cycle_merge_matrix,
    loss_sensitivity,
):
    res_rows, width, pair_chans = edge_matrix.shape
    pair_normed = standardize_features(edge_matrix.astype(jnp.float32)).astype(jnp.bfloat16)
    bias_local = jnp.einsum(
        "ijc,ch->ihj", pair_normed, logit_offset_matrix, preferred_element_type=jnp.float32
    ).astype(jnp.bfloat16)
    logit_offset_whole = lax.all_gather(bias_local, "dap", axis=0, tiled=True)
    homolog_lines = family_matrix.shape[0]
    homolog_subset = math.gcd(homolog_lines, 8)
    batched_lines = family_matrix.reshape(
        homolog_lines // homolog_subset,
        homolog_subset,
        family_matrix.shape[1],
        family_matrix.shape[2],
    )
    family_after_heads = lax.map(
        lambda family_shard_slice: lateral_heads_mixing(
            family_shard_slice, logit_offset_whole, query_key_value_gate_matrix, heads_merge_matrix
        ),
        batched_lines,
    ).reshape(family_matrix.shape)
    hidden = left_right_factor_matrix.shape[1] // 2
    weight_f32 = covariance_merge_matrix.astype(jnp.float32)
    alignment_columns = lax.all_to_all(
        family_after_heads, "dap", split_axis=1, concat_axis=0, tiled=True
    )
    edge_result = pair_projection_step(alignment_columns, left_right_factor_matrix)
    left_part = edge_result[..., :hidden]
    right_part = edge_result[..., hidden:]
    sequence_full_count = alignment_columns.shape[0]
    shard_in = lax.all_gather(right_part, "dap", axis=1, tiled=True)
    outer_sum = (
        jnp.einsum("sia,sjb->ijab", left_part, shard_in, preferred_element_type=jnp.float32)
        / sequence_full_count
    )
    row_count = shard_in.shape[1]
    flat = outer_sum.reshape(res_rows * row_count, hidden * hidden)
    edge_increment = jnp.dot(flat, weight_f32, precision=lax.Precision.HIGHEST).reshape(
        res_rows, row_count, pair_chans
    )
    pair_mid = (edge_matrix.astype(jnp.float32) + edge_increment).astype(jnp.bfloat16)
    tri_normed = standardize_features(pair_mid.astype(jnp.float32)).astype(jnp.bfloat16)
    tri_proj = jnp.dot(
        tri_normed.reshape(-1, pair_chans),
        edges_gate_factor_matrix,
        preferred_element_type=jnp.float32,
    ).reshape(res_rows, width, 3 * pair_chans)
    mask_f = edge_validity.astype(jnp.float32)[..., None]
    side_a = (mask_f * tri_proj[..., :pair_chans]).astype(jnp.bfloat16)
    side_b = (mask_f * tri_proj[..., pair_chans : 2 * pair_chans]).astype(jnp.bfloat16)
    gating = jax.nn.sigmoid(tri_proj[..., 2 * pair_chans :])
    tri_prod = jnp.einsum(
        "ikc,jkc->ijc",
        side_a,
        lax.all_gather(side_b, "dap", axis=0, tiled=True),
        preferred_element_type=jnp.float32,
    )
    prod_normed = standardize_features(tri_prod).astype(jnp.bfloat16)
    tri_update = jnp.dot(
        prod_normed.reshape(-1, pair_chans), cycle_merge_matrix, preferred_element_type=jnp.float32
    ).reshape(res_rows, width, pair_chans)
    pair_output = (pair_mid.astype(jnp.float32) + gating * tri_update).astype(jnp.bfloat16)
    cot_f32 = loss_sensitivity.astype(jnp.float32)
    grad_update = (cot_f32 * gating).astype(jnp.bfloat16)
    grad_normed = jnp.dot(
        grad_update.reshape(-1, pair_chans),
        cycle_merge_matrix.T,
        preferred_element_type=jnp.float32,
    ).reshape(res_rows, width, pair_chans)
    grad_prod = norm_back(tri_prod, grad_normed).astype(jnp.bfloat16)
    grad_part = grad_prod
    grad_a = jnp.einsum(
        "ijc,jkc->ikc",
        grad_part,
        lax.all_gather(side_b, "dap", axis=0, tiled=True),
        preferred_element_type=jnp.float32,
    )
    grad_part = grad_prod
    grad_b = lax.psum_scatter(
        jnp.einsum("ijc,ikc->jkc", grad_part, side_a, preferred_element_type=jnp.float32).astype(
            jnp.bfloat16
        ),
        "dap",
        scatter_dimension=0,
        tiled=True,
    ).astype(jnp.float32)
    grad_gate = cot_f32 * tri_update * gating * (1.0 - gating)
    grad_proj = jnp.concatenate([mask_f * grad_a, mask_f * grad_b, grad_gate], -1).astype(
        jnp.bfloat16
    )
    grad_input = jnp.dot(
        grad_proj.reshape(-1, 3 * pair_chans),
        edges_gate_factor_matrix.T,
        preferred_element_type=jnp.float32,
    ).reshape(res_rows, width, pair_chans)
    pair_gradient = cot_f32 + norm_back(pair_mid.astype(jnp.float32), grad_input)
    return (family_after_heads, pair_output, pair_gradient)


F32 = jnp.float32
BF16 = jnp.bfloat16
NT = (((1,), (1,)), ((), ()))
PARTS = 2


def dot(a, b):
    return jnp.dot(a, b, preferred_element_type=F32)


def dot_nt(a, b):
    return lax.dot_general(a, b, NT, preferred_element_type=F32)


def iota(shape, dim):
    return lax.broadcasted_iota(jnp.int32, shape, dim)


def pack_kernel(
    width, edge_ref, weight_ref, loss_ref, mask_ref, send_ref, edge_s, weight_s, loss_s, mask_s,
    tile_s, sems
):
    copies = [
        pltpu.make_async_copy(source, target, sems.at[k])
        for k, (source, target) in enumerate(
            (
                (edge_ref, edge_s),
                (weight_ref, weight_s),
                (loss_ref, loss_s),
                (mask_ref, mask_s),
            )
        )
    ]
    for copy in copies:
        copy.start()
    rows, chans = edge_s.shape
    heads = weight_s.shape[0]
    own = rows // width
    lanes = heads * width
    peers = width // own
    spread = (iota((heads, lanes), 0) == iota((heads, lanes), 1) // width).astype(F32)
    keep = iota((width, lanes), 0) == iota((width, lanes), 1) % width
    goal = iota((rows, rows), 0)
    source = goal % own * width + goal // (own * own) * own + goal // own % own
    place = (source == iota((rows, rows), 1)).astype(F32).astype(BF16)
    tile_s[...] = jnp.zeros(tile_s.shape, F32)
    for copy in copies:
        copy.wait()
    weight = lax.dot_general(
        weight_s[...], spread.astype(BF16), (((0,), (0,)), ((), ())), preferred_element_type=F32
    ).astype(BF16)
    column = dot(jnp.ones((8, chans), BF16), weight)[:1]
    every = dot(edge_s[...], weight)
    edge = edge_s[...].astype(F32)
    middle = jnp.mean(edge, -1, keepdims=True)
    center = edge - middle
    scale = lax.rsqrt(jnp.mean(center * center, -1, keepdims=True) + EPSILON)
    bias = scale * (every - middle * column)
    losses = dot(place, loss_s[...]).astype(BF16)
    tile_s[2 * own : 3 * own, :width] = mask_s[...].astype(F32)
    packed = tile_s[...]
    for r in range(own):
        picked = jnp.where(keep, bias[width * r : width * (r + 1)], 0.0)
        total = jnp.sum(picked, 0, keepdims=True)
        for t in range(lanes // 128):
            packed = jnp.where(
                iota((16, 128), 0) == own * t + r, total[:, 128 * t : 128 * t + 128], packed
            )
    packed = packed.astype(BF16)
    for e in range(peers):
        rank = e ^ 1
        send_ref[32 * rank : 32 * rank + 16, :] = packed
        send_ref[32 * rank + 16 : 32 * rank + 32, :] = losses[16 * e : 16 * e + 16]


def project_kernel(
    width,
    heads,
    hidden,
    family_ref,
    project_hbm,
    covariance_hbm,
    logits_ref,
    value_ref,
    gating_ref,
    cov_ref,
    project_ref,
    covariance_ref,
    sems,
    query_s,
    key_s,
    value_s,
    logits_s,
    cov_s,
):
    copies = [
        pltpu.make_async_copy(project_hbm, project_ref, sems.at[0]),
        pltpu.make_async_copy(covariance_hbm, covariance_ref, sems.at[1]),
    ]
    for copy in copies:
        copy.start()
    rows, depth = family_ref.shape
    seqs = rows // width
    group = 128 // width
    normed = standardize_features(family_ref[...].astype(F32)).astype(BF16)
    copies[0].wait()
    query_s[...] = dot(normed, project_ref[:, :depth]).astype(BF16)
    key_s[...] = dot(normed, project_ref[:, depth : 2 * depth]).astype(BF16)
    value_s[...] = dot(normed, project_ref[:, 2 * depth : 3 * depth]).astype(BF16)
    gating_ref[...] = jax.nn.sigmoid(dot(normed, project_ref[:, 3 * depth :]))
    same = (iota((128, 128), 0) // width == iota((128, 128), 1) // width).astype(F32).astype(BF16)
    scale = 1.0 / math.sqrt(depth // heads)
    for t in range(depth // 128):
        cols = slice(128 * t, 128 * t + 128)
        for s in range(seqs):
            span = slice(width * s, width * s + width)
            keys = jnp.concatenate([key_s[span, cols]] * group, 0) * same
            logits_s[span, :] = dot_nt(query_s[span, cols], keys) * scale
            values = jnp.concatenate([value_s[span, cols]] * group, 0) * same
            value_ref[128 * s : 128 * (s + 1), cols] = values
        for k in range(rows // 128):
            span = slice(128 * k, 128 * (k + 1))
            logits_ref[span, cols] = logits_s[span, :].T
    copies[1].wait()
    cov_s[...] = covariance_ref[...].astype(F32)
    for b in range(hidden):
        rows_b = cov_s[pl.ds(b, hidden, stride=hidden), :].astype(BF16)
        cov_ref[0, hidden * b : hidden * (b + 1), :] = rows_b
        swapped = b ^ (group // 2)
        cov_ref[1, hidden * swapped : hidden * (swapped + 1), :] = rows_b


def attention_kernel(
    width,
    own,
    family_ref,
    got_ref,
    logits_ref,
    value_ref,
    gating_ref,
    merge_ref,
    factor_ref,
    edge_ref,
    family_out_ref,
    send_ref,
    after_s,
    weight_s,
    row_s,
    turn_s,
    line_s,
    sem,
):
    rows, depth = family_ref.shape
    seqs = rows // width
    tiles = depth // 128
    group = 128 // width
    biases = jnp.concatenate([got_ref[d ^ 1, :16, :] for d in range(got_ref.shape[0])], 0)
    gated = []
    for t in range(tiles):
        cols = slice(128 * t, 128 * t + 128)
        row = iota((128, biases.shape[0]), 0) % width
        take = iota((128, biases.shape[0]), 1) == 16 * (row // own) + own * t + row % own
        bias = dot(take.astype(F32).astype(BF16), biases).T
        for k in range(rows // 128):
            span = slice(128 * k, 128 * (k + 1))
            flipped = logits_ref[span, cols] + bias
            parts = []
            for h in range(group):
                some = flipped[width * h : width * (h + 1)]
                raised = jnp.exp(some - jnp.max(some, 0, keepdims=True))
                parts.append(raised * (1.0 / jnp.sum(raised, 0, keepdims=True)))
            weight_s[span, cols] = jnp.concatenate(parts, 0).astype(BF16).T
    for t in range(tiles):
        cols = slice(128 * t, 128 * t + 128)
        mixed = jnp.concatenate(
            [
                dot(weight_s[width * s : width * (s + 1), cols], value_ref[128 * s : 128 * (s + 1), cols])
                for s in range(seqs)
            ],
            0,
        )
        gated.append((gating_ref[:, cols] * mixed).astype(BF16))
    after = (
        family_ref[...].astype(F32) + dot(jnp.concatenate(gated, 1), merge_ref[...])
    ).astype(BF16)
    after_s[...] = after
    leave = pltpu.make_async_copy(after_s, family_out_ref, sem)
    leave.start()
    ready = standardize_features(after.astype(F32)).astype(BF16)
    hidden = factor_ref.shape[0] // 2
    groups = width // group
    row_s[:, : 2 * hidden] = dot_nt(ready, factor_ref[...])
    placed = jnp.zeros((groups * seqs, 128), F32)
    for q in range(group):
        picked = jnp.concatenate(
            [row_s[pl.ds(group * g + q, seqs, stride=width), :] for g in range(groups)], 0
        )[:, :hidden].astype(BF16)
        here = iota((hidden, 128), 0) + hidden * q == iota((hidden, 128), 1)
        placed = placed + dot(picked, here.astype(F32).astype(BF16))
    for g in range(groups):
        send_ref[seqs * g : seqs * (g + 1), :] = placed[seqs * g : seqs * (g + 1), :].astype(BF16)
    turned = dot_nt(factor_ref[hidden : 2 * hidden, :], ready)
    for k in range(rows // 128):
        turn_s[hidden * k : hidden * (k + 1), :] = turned[:, 128 * k : 128 * k + 128]
    chunks = hidden // group
    for k in range(rows // 128):
        blocks = [
            turn_s[pl.ds(hidden * k + q, chunks, stride=group), :] for q in range(group)
        ]
        for p, block in enumerate(block_transpose(blocks, width)):
            first = chunks * (group * k + p)
            line_s[first : first + chunks, :] = block
    base = seqs * groups
    for g in range(chunks):
        send_ref[base + seqs * g : base + seqs * (g + 1), :] = line_s[
            pl.ds(g, seqs, stride=chunks), :
        ].astype(BF16)
    send_ref[2 * base :, :] = edge_ref[...]
    leave.wait()


def block_transpose(blocks, step):
    lane = iota(blocks[0].shape, 1)
    for shift in (2 * step, step):
        low = lane // shift % 2 == 0
        stride = shift // step
        out = list(blocks)
        for q in range(len(blocks)):
            if q // stride % 2 == 0:
                x, y = blocks[q], blocks[q + stride]
                up = pltpu.roll(y, shift, 1)
                down = pltpu.roll(x, 4 * step - shift, 1)
                out[q] = jnp.where(low, x, up)
                out[q + stride] = jnp.where(low, down, y)
        blocks = out
    return blocks


def mean(values):
    return jnp.mean(values, -1, keepdims=True)


def merge_rows(parts):
    row = iota(parts[0].shape, 0)
    step = 1
    while len(parts) > 1:
        low = row // step % 2 == 0
        parts = [
            jnp.where(low, x, y) + pltpu.roll(jnp.where(low, y, x), step, 0)
            for x, y in zip(parts[::2], parts[1::2])
        ]
        step *= 2
    return parts[0]


def pair_kernel(
    axis,
    width,
    own,
    hidden,
    seqs,
    sides_ref,
    got_ref,
    own_loss_ref,
    covariance_ref,
    edges_ref,
    cycle_ref,
    out_ref,
    grad_ref,
    right_s,
    flat_s,
    mid_s,
    unit_s,
    scale_s,
    a_s,
    b_s,
    tri_s,
):
    me = lax.axis_index(axis)
    rank = me + 1 - 2 * (me % 2)
    n = sides_ref.shape[0]
    every = width * width
    group = 128 // hidden
    groups = width // group
    chunks = hidden // group
    pairs = own * width
    chans = 128
    total = seqs * n
    base = 2 * seqs * groups

    def gathered(first):
        return jnp.concatenate([sides_ref[d, first : first + seqs, :] for d in range(n)], 0)

    for g in range(chunks):
        turned = gathered(seqs * (groups + g)).T
        for q in range(group):
            right_s[width * g : width * (g + 1), total * q : total * (q + 1)] = turned[
                width * q : width * (q + 1), :
            ]
    block = iota((total, 128), 1) // hidden
    low_half = iota((width * chunks, 128), 1) < 64
    zero = jnp.zeros((total, 128), BF16)
    for g in range(groups):
        left = gathered(seqs * g)
        wide = left.astype(F32)
        rolled = [left] + [
            pltpu.roll(wide, hidden * d, 1).astype(BF16) for d in range(1, group)
        ]

        def placed(first, second, lane):
            return jnp.where(
                block == lane,
                rolled[(lane - first) % group],
                jnp.where(block == lane + 2, rolled[(lane + 2 - second) % group], zero),
            )

        halves = []
        for h in range(2):
            columns = []
            for even in range(0, group, 2):
                first, second = (even, even + 1) if h == 0 else (even + 1, even)
                columns.append(
                    jnp.concatenate([placed(first, second, lane) for lane in range(2)], 0)
                )
            halves.append(
                dot(
                    right_s[:, 2 * total * h : 2 * total * (h + 1)],
                    jnp.concatenate(columns, 1),
                ).astype(BF16)
            )
        for e in range(group // 2):
            x, y = (half[:, 128 * e : 128 * e + 128] for half in halves)
            for odd, outer in enumerate(
                (jnp.where(low_half, x, y), jnp.where(low_half, y, x))
            ):
                first = every // 2 * odd + width * (group // 2 * g + e)
                for c in range(chunks):
                    flat_s[first : first + width, 128 * c : 128 * c + 128] = outer[
                        width * c : width * (c + 1)
                    ]
    tiles = jnp.concatenate([got_ref[d ^ 1, :16, :] for d in range(n)], 0)
    pick = (iota((width, 128), 0) == iota((width, 128), 1)).astype(F32).astype(BF16)
    masks = dot_nt(pick, tiles)

    def kept(columns, first):
        return jnp.concatenate(
            [
                jnp.broadcast_to(columns[:, first + r : first + r + 1], (width, chans))
                for r in range(own)
            ],
            0,
        )

    count = width // PARTS
    lists = [
        [2 * (count * (p // 2) + k) + p % 2 for k in range(count)] for p in range(PARTS)
    ]
    centered = jnp.where(
        iota((chans, chans), 0) == iota((chans, chans), 1), 1.0 - 1.0 / chans, -1.0 / chans
    ).astype(BF16)
    added = [
        dot(
            flat_s[
                every // 2 * (p % 2) + width * count * (p // 2) : every // 2 * (p % 2)
                + width * count * (p // 2 + 1),
                :,
            ],
            covariance_ref[p % 2],
        )
        for p in range(PARTS)
    ]
    mids = []
    for p, residues in enumerate(lists):
        edge = jnp.concatenate(
            [
                sides_ref[i // own, base + width * (i % own) : base + width * (i % own + 1), :]
                for i in residues
            ],
            0,
        ).astype(F32)
        mids.append((edge + added[p] * (1.0 / total)).astype(BF16))
    centers = [dot(mid, centered) for mid in mids]
    scales = [lax.rsqrt(mean(c * c) + EPSILON) for c in centers]
    units = [c * scale for c, scale in zip(centers, scales)]
    sides = [dot(unit.astype(BF16), edges_ref[:, : 2 * chans]) for unit in units]
    for p, residues in enumerate(lists):
        for k, i in enumerate(residues):
            here = slice(width * k, width * (k + 1))
            there = slice(width * i, width * (i + 1))
            mid_s[there, :] = mids[p][here].astype(F32)
            scale_s[there, :] = jnp.broadcast_to(scales[p][here], (width, chans))
            unit_s[there, :] = units[p][here]
            lane = 16 * (i // own) + 2 * own + i % own
            keep = jnp.broadcast_to(masks[:, lane : lane + 1], (width, chans))
            a_s[there, :] = (keep * sides[p][here, :chans]).astype(BF16).astype(F32)
            b_s[there, :] = (keep * sides[p][here, chans:]).astype(BF16).astype(F32)

    rows = pl.ds(pl.multiple_of(me * pairs, pairs), pairs)

    def rows_and_columns(ref):
        return jnp.concatenate(
            [ref[rows, :]] + [ref[pl.ds(me * own + r, width, stride=width), :] for r in range(own)],
            0,
        )

    mid = mid_s[rows, :]
    losses = jnp.concatenate([got_ref[d ^ 1, 16:, :] for d in range(n)], 0)
    goal = iota((pairs, pairs), 0)
    source = goal % width // own * 16 + goal // width * own + goal % own
    place = (source == iota((pairs, pairs), 1)).astype(F32).astype(BF16)
    loss = jnp.concatenate([own_loss_ref[...].astype(F32), dot(place, losses)], 0)
    gating = jax.nn.sigmoid(
        dot(rows_and_columns(unit_s).astype(BF16), edges_ref[:, 2 * chans :])
    )
    tri = []
    for fixed, moving in ((a_s, b_s), (b_s, a_s)):
        held = fixed[rows, :]
        for r in range(own):
            mine = [held[width * r + 8 * v : width * r + 8 * v + 8] for v in range(width // 8)]
            for j in range(0, width, 8):
                parts = []
                for jj in range(j, j + 8):
                    prods = [
                        mine[v] * moving[width * jj + 8 * v : width * jj + 8 * v + 8, :]
                        for v in range(width // 8)
                    ]
                    parts.append(functools.reduce(jnp.add, prods))
                tri.append(merge_rows(parts))
    tri = jnp.concatenate(tri, 0)
    center = tri - mean(tri)
    scale_inv = lax.rsqrt(mean(center * center) + EPSILON)
    unit = center * scale_inv
    update = dot(unit[:pairs].astype(BF16), cycle_ref[...])
    out_ref[...] = (mid + gating[:pairs] * update).astype(BF16)
    grad_normed = dot_nt((loss * gating).astype(BF16), cycle_ref[...])
    tri_s[...] = (
        (
            scale_inv
            * (
                grad_normed - mean(grad_normed) - unit * mean(grad_normed * unit)
            )
        )
        .astype(BF16)
        .astype(F32)
    )

    acc = []
    for first, ref in ((0, b_s), (own, a_s)):
        sums = [[jnp.zeros((8, chans), F32) for _ in range(width // 8)] for _ in range(own)]
        for j in range(width):
            parts = [ref[width * j + 8 * v : width * j + 8 * v + 8, :] for v in range(width // 8)]
            for r in range(own):
                at = width * (first + r) + j
                row = jnp.broadcast_to(tri_s[at : at + 1, :], (8, chans))
                sums[r] = [old + row * part for old, part in zip(sums[r], parts)]
        acc += [jnp.concatenate(vregs, 0) for vregs in sums]
    keep = kept(dot_nt(pick, got_ref[rank, :16, :]), 2 * own)
    gate_own = gating[:pairs]
    grad_gate = loss[:pairs] * update * gate_own * (1.0 - gate_own)
    grad_proj = jnp.concatenate(
        [
            keep * jnp.concatenate(acc[:own], 0),
            keep * jnp.concatenate(acc[own:], 0),
            grad_gate,
        ],
        1,
    ).astype(BF16)
    grad_input = dot_nt(grad_proj, edges_ref[...])
    scale_inv = scale_s[rows, :]
    unit = unit_s[rows, :]
    grad_ref[...] = loss[:pairs] + scale_inv * (
        grad_input - mean(grad_input) - unit * mean(grad_input * unit)
    )


def body_resident(
    family_matrix,
    edge_matrix,
    edge_validity,
    query_key_value_gate_matrix,
    logit_offset_matrix,
    heads_merge_matrix,
    left_right_factor_matrix,
    covariance_merge_matrix,
    edges_gate_factor_matrix,
    cycle_merge_matrix,
    loss_sensitivity,
):
    seqs, width, depth = family_matrix.shape
    own, _, chans = edge_matrix.shape
    heads = logit_offset_matrix.shape[1]
    hidden = left_right_factor_matrix.shape[1] // 2
    pairs = own * width
    every = width * width
    edge = edge_matrix.reshape(pairs, chans)
    loss = loss_sensitivity.reshape(pairs, chans)
    vmem = pl.BlockSpec(memory_space=pltpu.VMEM)
    hbm = pl.BlockSpec(memory_space=pltpu.HBM)
    family = family_matrix.reshape(seqs * width, depth)
    factor = left_right_factor_matrix.T
    sided = 2 * seqs * width * hidden // 128
    peers = width // own
    packed = pl.pallas_call(
        functools.partial(pack_kernel, width),
        out_shape=jax.ShapeDtypeStruct((32 * peers, chans), BF16),
        in_specs=[hbm] * 4,
        out_specs=vmem,
        scratch_shapes=[
            pltpu.VMEM((pairs, chans), BF16),
            pltpu.VMEM((heads, chans), BF16),
            pltpu.VMEM((pairs, chans), BF16),
            pltpu.VMEM((own, width), jnp.int32),
            pltpu.VMEM((16, 128), F32),
            pltpu.SemaphoreType.DMA((4,)),
        ],
        name="pack_pairs",
    )(edge, logit_offset_matrix.T, loss, edge_validity)
    got = lax.all_to_all(
        packed, "dap", split_axis=0, concat_axis=0, axis_index_groups=[[d ^ 1 for d in range(peers)]], tiled=True
    )
    got = got.reshape(peers, 32, chans)
    logits, value, gating, covariance = pl.pallas_call(
        functools.partial(project_kernel, width, heads, hidden),
        out_shape=(
            jax.ShapeDtypeStruct((seqs * width, depth), F32),
            jax.ShapeDtypeStruct((seqs * 128, depth), BF16),
            jax.ShapeDtypeStruct((seqs * width, depth), F32),
            jax.ShapeDtypeStruct((2, hidden * hidden, chans), BF16),
        ),
        in_specs=[vmem, hbm, hbm],
        out_specs=(vmem,) * 4,
        scratch_shapes=[
            pltpu.VMEM(query_key_value_gate_matrix.shape, BF16),
            pltpu.VMEM(covariance_merge_matrix.shape, BF16),
            pltpu.SemaphoreType.DMA((2,)),
        ]
        + [pltpu.VMEM((seqs * width, depth), BF16)] * 3
        + [pltpu.VMEM((seqs * width, 128), F32)]
        + [pltpu.VMEM((hidden * hidden, chans), F32)],
        compiler_params=pltpu.CompilerParams(vmem_limit_bytes=16 << 20),
        cost_estimate=pl.CostEstimate(
            flops=16 * seqs * width * depth * depth,
            bytes_accessed=32 * seqs * width * depth,
            transcendentals=seqs * width * depth,
        ),
        name="project_family",
    )(
        family,
        pltpu.with_memory_space_constraint(query_key_value_gate_matrix, pltpu.HBM),
        pltpu.with_memory_space_constraint(covariance_merge_matrix, pltpu.HBM),
    )
    family_out, send = pl.pallas_call(
        functools.partial(attention_kernel, width, own),
        out_shape=(
            jax.ShapeDtypeStruct((seqs * width, depth), BF16),
            jax.ShapeDtypeStruct((sided + pairs, 128), BF16),
        ),
        in_specs=[vmem] * 8,
        out_specs=(hbm, vmem),
        scratch_shapes=[
            pltpu.VMEM((seqs * width, depth), BF16),
            pltpu.VMEM((seqs * width, depth), BF16),
            pltpu.VMEM((seqs * width, 128), F32),
            pltpu.VMEM((seqs * width * hidden // 128, 128), F32),
            pltpu.VMEM((seqs * width * hidden // 128, 128), F32),
            pltpu.SemaphoreType.DMA(()),
        ],
        compiler_params=pltpu.CompilerParams(vmem_limit_bytes=16 << 20),
        name="row_attention",
    )(family, got, logits, value, gating, heads_merge_matrix, factor, edge)
    gathered = lax.all_gather(send, "dap", axis=0, tiled=False)
    pair_out, pair_grad = pl.pallas_call(
        functools.partial(pair_kernel, "dap", width, own, hidden, seqs),
        out_shape=(
            jax.ShapeDtypeStruct((pairs, chans), BF16),
            jax.ShapeDtypeStruct((pairs, chans), F32),
        ),
        in_specs=[vmem] * 6,
        out_specs=(vmem, vmem),
        scratch_shapes=[
            pltpu.VMEM((width * hidden * hidden // 128, 128 // hidden * 128), BF16),
            pltpu.VMEM((every, hidden * hidden), BF16),
            pltpu.VMEM((every, chans), F32),
            pltpu.VMEM((every, chans), F32),
            pltpu.VMEM((every, chans), F32),
            pltpu.VMEM((every, chans), F32),
            pltpu.VMEM((every, chans), F32),
            pltpu.VMEM((2 * pairs, chans), F32),
        ],
        compiler_params=pltpu.CompilerParams(vmem_limit_bytes=16 << 20),
        name="pair_update",
    )(gathered, got, loss, covariance, edges_gate_factor_matrix, cycle_merge_matrix)
    return (
        family_out.reshape(seqs, width, depth),
        pair_out.reshape(own, width, chans),
        pair_grad.reshape(own, width, chans),
    )


def fits_resident(dap, family, edge, logit, factor):
    seqs, width, depth = family.shape
    own, _, chans = edge.shape
    return (
        own * dap == width
        and dap % 2 == 0
        and width == 32
        and factor.shape[1] == 64
        and depth == 32 * logit.shape[1]
        and depth % 128 == 0
        and chans == 128
        and own * width == 128
        and seqs % 16 == 0
        and seqs * dap == 128
    )


def body(*args):
    dap = lax.axis_size("dap")
    if fits_resident(dap, args[0], args[1], args[4], args[6]):
        return body_resident(*args)
    return body_general(*args)


def solution(mesh):
    in_specs = (
        P(("dp", "dap"), None, None),
        P(("dp", "dap"), None, None),
        P(("dp", "dap"), None),
        P(),
        P(),
        P(),
        P(),
        P(),
        P(),
        P(),
        P(("dp", "dap"), None, None),
    )
    out_specs = (
        P(("dp", "dap"), None, None),
        P(("dp", "dap"), None, None),
        P(("dp", "dap"), None, None),
    )
    return jax.shard_map(body, mesh=mesh, in_specs=in_specs, out_specs=out_specs, check_vma=False)
```

```python
import functools
import math

import jax
import jax.numpy as jnp
from jax import lax
from jax.experimental import pallas as pl
from jax.experimental.pallas import tpu as pltpu
from jax.sharding import PartitionSpec as P

EPSILON = 1e-05


def standardize_features(values):
    center = values - jnp.mean(values, -1, keepdims=True)
    scale_inv = lax.rsqrt(jnp.mean(center * center, -1, keepdims=True) + EPSILON)
    return center * scale_inv


def norm_back(values, grad_out):
    center = values - jnp.mean(values, -1, keepdims=True)
    scale_inv = lax.rsqrt(jnp.mean(center * center, -1, keepdims=True) + EPSILON)
    standardized_source = center * scale_inv
    return scale_inv * (
        grad_out
        - jnp.mean(grad_out, -1, keepdims=True)
        - standardized_source * jnp.mean(grad_out * standardized_source, -1, keepdims=True)
    )


def lateral_heads_mixing(
    family_shard_slice, logit_offset_whole, query_key_value_gate_matrix, heads_merge_matrix
):
    homolog_number, amino_number, feature_depth = family_shard_slice.shape
    head_count = logit_offset_whole.shape[1]
    head_size = feature_depth // head_count
    standardized_source = standardize_features(family_shard_slice.astype(jnp.float32)).astype(
        jnp.bfloat16
    )
    projected = jnp.dot(
        standardized_source.reshape(-1, feature_depth),
        query_key_value_gate_matrix,
        preferred_element_type=jnp.float32,
    )
    projected = projected.reshape(homolog_number, amino_number, 4 * feature_depth)
    shape_heads = (homolog_number, amino_number, head_count, head_size)
    queries = projected[..., :feature_depth].astype(jnp.bfloat16).reshape(shape_heads)
    key_rows = (
        projected[..., feature_depth : 2 * feature_depth].astype(jnp.bfloat16).reshape(shape_heads)
    )
    value_rows = (
        projected[..., 2 * feature_depth : 3 * feature_depth]
        .astype(jnp.bfloat16)
        .reshape(shape_heads)
    )
    gating = jax.nn.sigmoid(projected[..., 3 * feature_depth :])
    logits = jnp.einsum("sihd,sjhd->sihj", queries, key_rows, preferred_element_type=jnp.float32)
    logits = logits / math.sqrt(head_size) + logit_offset_whole.astype(jnp.float32)[None]
    weights = jax.nn.softmax(logits, axis=-1).astype(jnp.bfloat16)
    mixed = jnp.einsum("sihj,sjhd->sihd", weights, value_rows, preferred_element_type=jnp.float32)
    gated = (gating * mixed.reshape(homolog_number, amino_number, feature_depth)).astype(
        jnp.bfloat16
    )
    edge_increment = jnp.dot(
        gated.reshape(-1, feature_depth), heads_merge_matrix, preferred_element_type=jnp.float32
    )
    return (
        family_shard_slice.astype(jnp.float32)
        + edge_increment.reshape(homolog_number, amino_number, feature_depth)
    ).astype(jnp.bfloat16)


def pair_projection_step(alignment_rows, left_right_factor_matrix):
    standardized_source = standardize_features(alignment_rows.astype(jnp.float32)).astype(
        jnp.bfloat16
    )
    edge_result = jnp.dot(
        standardized_source.reshape(-1, alignment_rows.shape[2]),
        left_right_factor_matrix,
        preferred_element_type=jnp.float32,
    )
    return edge_result.reshape(alignment_rows.shape[0], alignment_rows.shape[1], -1).astype(
        jnp.bfloat16
    )


def body_general(
    family_matrix,
    edge_matrix,
    edge_validity,
    query_key_value_gate_matrix,
    logit_offset_matrix,
    heads_merge_matrix,
    left_right_factor_matrix,
    covariance_merge_matrix,
    edges_gate_factor_matrix,
    cycle_merge_matrix,
    loss_sensitivity,
):
    res_rows, width, pair_chans = edge_matrix.shape
    pair_normed = standardize_features(edge_matrix.astype(jnp.float32)).astype(jnp.bfloat16)
    bias_local = jnp.einsum(
        "ijc,ch->ihj", pair_normed, logit_offset_matrix, preferred_element_type=jnp.float32
    ).astype(jnp.bfloat16)
    logit_offset_whole = lax.all_gather(bias_local, "dap", axis=0, tiled=True)
    homolog_lines = family_matrix.shape[0]
    homolog_subset = math.gcd(homolog_lines, 8)
    batched_lines = family_matrix.reshape(
        homolog_lines // homolog_subset,
        homolog_subset,
        family_matrix.shape[1],
        family_matrix.shape[2],
    )
    family_after_heads = lax.map(
        lambda family_shard_slice: lateral_heads_mixing(
            family_shard_slice, logit_offset_whole, query_key_value_gate_matrix, heads_merge_matrix
        ),
        batched_lines,
    ).reshape(family_matrix.shape)
    hidden = left_right_factor_matrix.shape[1] // 2
    weight_f32 = covariance_merge_matrix.astype(jnp.float32)
    alignment_columns = lax.all_to_all(
        family_after_heads, "dap", split_axis=1, concat_axis=0, tiled=True
    )
    edge_result = pair_projection_step(alignment_columns, left_right_factor_matrix)
    left_part = edge_result[..., :hidden]
    right_part = edge_result[..., hidden:]
    sequence_full_count = alignment_columns.shape[0]
    shard_in = lax.all_gather(right_part, "dap", axis=1, tiled=True)
    outer_sum = (
        jnp.einsum("sia,sjb->ijab", left_part, shard_in, preferred_element_type=jnp.float32)
        / sequence_full_count
    )
    row_count = shard_in.shape[1]
    flat = outer_sum.reshape(res_rows * row_count, hidden * hidden)
    edge_increment = jnp.dot(flat, weight_f32, precision=lax.Precision.HIGHEST).reshape(
        res_rows, row_count, pair_chans
    )
    pair_mid = (edge_matrix.astype(jnp.float32) + edge_increment).astype(jnp.bfloat16)
    tri_normed = standardize_features(pair_mid.astype(jnp.float32)).astype(jnp.bfloat16)
    tri_proj = jnp.dot(
        tri_normed.reshape(-1, pair_chans),
        edges_gate_factor_matrix,
        preferred_element_type=jnp.float32,
    ).reshape(res_rows, width, 3 * pair_chans)
    mask_f = edge_validity.astype(jnp.float32)[..., None]
    side_a = (mask_f * tri_proj[..., :pair_chans]).astype(jnp.bfloat16)
    side_b = (mask_f * tri_proj[..., pair_chans : 2 * pair_chans]).astype(jnp.bfloat16)
    gating = jax.nn.sigmoid(tri_proj[..., 2 * pair_chans :])
    tri_prod = jnp.einsum(
        "ikc,jkc->ijc",
        side_a,
        lax.all_gather(side_b, "dap", axis=0, tiled=True),
        preferred_element_type=jnp.float32,
    )
    prod_normed = standardize_features(tri_prod).astype(jnp.bfloat16)
    tri_update = jnp.dot(
        prod_normed.reshape(-1, pair_chans), cycle_merge_matrix, preferred_element_type=jnp.float32
    ).reshape(res_rows, width, pair_chans)
    pair_output = (pair_mid.astype(jnp.float32) + gating * tri_update).astype(jnp.bfloat16)
    cot_f32 = loss_sensitivity.astype(jnp.float32)
    grad_update = (cot_f32 * gating).astype(jnp.bfloat16)
    grad_normed = jnp.dot(
        grad_update.reshape(-1, pair_chans),
        cycle_merge_matrix.T,
        preferred_element_type=jnp.float32,
    ).reshape(res_rows, width, pair_chans)
    grad_prod = norm_back(tri_prod, grad_normed).astype(jnp.bfloat16)
    grad_part = grad_prod
    grad_a = jnp.einsum(
        "ijc,jkc->ikc",
        grad_part,
        lax.all_gather(side_b, "dap", axis=0, tiled=True),
        preferred_element_type=jnp.float32,
    )
    grad_part = grad_prod
    grad_b = lax.psum_scatter(
        jnp.einsum("ijc,ikc->jkc", grad_part, side_a, preferred_element_type=jnp.float32).astype(
            jnp.bfloat16
        ),
        "dap",
        scatter_dimension=0,
        tiled=True,
    ).astype(jnp.float32)
    grad_gate = cot_f32 * tri_update * gating * (1.0 - gating)
    grad_proj = jnp.concatenate([mask_f * grad_a, mask_f * grad_b, grad_gate], -1).astype(
        jnp.bfloat16
    )
    grad_input = jnp.dot(
        grad_proj.reshape(-1, 3 * pair_chans),
        edges_gate_factor_matrix.T,
        preferred_element_type=jnp.float32,
    ).reshape(res_rows, width, pair_chans)
    pair_gradient = cot_f32 + norm_back(pair_mid.astype(jnp.float32), grad_input)
    return (family_after_heads, pair_output, pair_gradient)


F32 = jnp.float32
BF16 = jnp.bfloat16
NT = (((1,), (1,)), ((), ()))
PARTS = 2


def dot(a, b):
    return jnp.dot(a, b, preferred_element_type=F32)


def dot_nt(a, b):
    return lax.dot_general(a, b, NT, preferred_element_type=F32)


def iota(shape, dim):
    return lax.broadcasted_iota(jnp.int32, shape, dim)


def pack_kernel(
    width, edge_ref, weight_ref, loss_ref, mask_ref, send_ref, edge_s, weight_s, loss_s, mask_s,
    tile_s, sems
):
    copies = [
        pltpu.make_async_copy(source, target, sems.at[k])
        for k, (source, target) in enumerate(
            (
                (edge_ref, edge_s),
                (weight_ref, weight_s),
                (loss_ref, loss_s),
                (mask_ref, mask_s),
            )
        )
    ]
    for copy in copies:
        copy.start()
    rows, chans = edge_s.shape
    heads = weight_s.shape[0]
    own = rows // width
    lanes = heads * width
    peers = width // own
    spread = (iota((heads, lanes), 0) == iota((heads, lanes), 1) // width).astype(F32)
    keep = iota((width, lanes), 0) == iota((width, lanes), 1) % width
    goal = iota((rows, rows), 0)
    source = goal % own * width + goal // (own * own) * own + goal // own % own
    place = (source == iota((rows, rows), 1)).astype(F32).astype(BF16)
    tile_s[...] = jnp.zeros(tile_s.shape, F32)
    for copy in copies:
        copy.wait()
    weight = lax.dot_general(
        weight_s[...], spread.astype(BF16), (((0,), (0,)), ((), ())), preferred_element_type=F32
    ).astype(BF16)
    column = dot(jnp.ones((8, chans), BF16), weight)[:1]
    every = dot(edge_s[...], weight)
    edge = edge_s[...].astype(F32)
    middle = jnp.mean(edge, -1, keepdims=True)
    center = edge - middle
    scale = lax.rsqrt(jnp.mean(center * center, -1, keepdims=True) + EPSILON)
    bias = scale * (every - middle * column)
    losses = dot(place, loss_s[...]).astype(BF16)
    tile_s[2 * own : 3 * own, :width] = mask_s[...].astype(F32)
    packed = tile_s[...]
    for r in range(own):
        picked = jnp.where(keep, bias[width * r : width * (r + 1)], 0.0)
        total = jnp.sum(picked, 0, keepdims=True)
        for t in range(lanes // 128):
            packed = jnp.where(
                iota((16, 128), 0) == own * t + r, total[:, 128 * t : 128 * t + 128], packed
            )
    packed = packed.astype(BF16)
    for e in range(peers):
        rank = e ^ 1
        send_ref[32 * rank : 32 * rank + 16, :] = packed
        send_ref[32 * rank + 16 : 32 * rank + 32, :] = losses[16 * e : 16 * e + 16]


def project_kernel(
    width,
    heads,
    hidden,
    family_hbm,
    project_hbm,
    covariance_hbm,
    logits_ref,
    value_ref,
    gating_ref,
    cov_ref,
    family_ref,
    project_ref,
    covariance_ref,
    sems,
    query_s,
    key_s,
    value_s,
    logits_s,
    cov_s,
):
    copies = [
        pltpu.make_async_copy(family_hbm, family_ref, sems.at[2]),
        pltpu.make_async_copy(project_hbm, project_ref, sems.at[0]),
        pltpu.make_async_copy(covariance_hbm, covariance_ref, sems.at[1]),
    ]
    for copy in copies:
        copy.start()
    rows, depth = family_ref.shape
    seqs = rows // width
    group = 128 // width
    copies[0].wait()
    normed = standardize_features(family_ref[...].astype(F32)).astype(BF16)
    copies[1].wait()
    query_s[...] = dot(normed, project_ref[:, :depth]).astype(BF16)
    key_s[...] = dot(normed, project_ref[:, depth : 2 * depth]).astype(BF16)
    value_s[...] = dot(normed, project_ref[:, 2 * depth : 3 * depth]).astype(BF16)
    gating_ref[...] = jax.nn.sigmoid(dot(normed, project_ref[:, 3 * depth :]))
    same = (iota((128, 128), 0) // width == iota((128, 128), 1) // width).astype(F32).astype(BF16)
    scale = 1.0 / math.sqrt(depth // heads)
    for t in range(depth // 128):
        cols = slice(128 * t, 128 * t + 128)
        for s in range(seqs):
            span = slice(width * s, width * s + width)
            keys = jnp.concatenate([key_s[span, cols]] * group, 0) * same
            logits_s[span, :] = dot_nt(query_s[span, cols], keys) * scale
            values = jnp.concatenate([value_s[span, cols]] * group, 0) * same
            value_ref[128 * s : 128 * (s + 1), cols] = values
        for k in range(rows // 128):
            span = slice(128 * k, 128 * (k + 1))
            logits_ref[span, cols] = logits_s[span, :].T
    copies[2].wait()
    cov_s[...] = covariance_ref[...].astype(F32)
    for b in range(hidden):
        rows_b = cov_s[pl.ds(b, hidden, stride=hidden), :].astype(BF16)
        cov_ref[0, hidden * b : hidden * (b + 1), :] = rows_b
        swapped = b ^ (group // 2)
        cov_ref[1, hidden * swapped : hidden * (swapped + 1), :] = rows_b


def attention_kernel(
    width,
    own,
    family_ref,
    got_ref,
    logits_ref,
    value_ref,
    gating_ref,
    merge_ref,
    factor_ref,
    edge_ref,
    after_ref,
    send_ref,
    weight_s,
    row_s,
    turn_s,
    line_s,
):
    rows, depth = family_ref.shape
    seqs = rows // width
    tiles = depth // 128
    group = 128 // width
    biases = jnp.concatenate([got_ref[d ^ 1, :16, :] for d in range(got_ref.shape[0])], 0)
    gated = []
    for t in range(tiles):
        cols = slice(128 * t, 128 * t + 128)
        row = iota((128, biases.shape[0]), 0) % width
        take = iota((128, biases.shape[0]), 1) == 16 * (row // own) + own * t + row % own
        bias = dot(take.astype(F32).astype(BF16), biases).T
        for k in range(rows // 128):
            span = slice(128 * k, 128 * (k + 1))
            flipped = logits_ref[span, cols] + bias
            parts = []
            for h in range(group):
                some = flipped[width * h : width * (h + 1)]
                raised = jnp.exp(some - jnp.max(some, 0, keepdims=True))
                parts.append(raised * (1.0 / jnp.sum(raised, 0, keepdims=True)))
            weight_s[span, cols] = jnp.concatenate(parts, 0).astype(BF16).T
    for t in range(tiles):
        cols = slice(128 * t, 128 * t + 128)
        mixed = jnp.concatenate(
            [
                dot(weight_s[width * s : width * (s + 1), cols], value_ref[128 * s : 128 * (s + 1), cols])
                for s in range(seqs)
            ],
            0,
        )
        gated.append((gating_ref[:, cols] * mixed).astype(BF16))
    after = (
        family_ref[...].astype(F32) + dot(jnp.concatenate(gated, 1), merge_ref[...])
    ).astype(BF16)
    after_ref[...] = after
    ready = standardize_features(after.astype(F32)).astype(BF16)
    hidden = factor_ref.shape[0] // 2
    groups = width // group
    row_s[:, : 2 * hidden] = dot_nt(ready, factor_ref[...])
    placed = jnp.zeros((groups * seqs, 128), F32)
    for q in range(group):
        picked = jnp.concatenate(
            [row_s[pl.ds(group * g + q, seqs, stride=width), :] for g in range(groups)], 0
        )[:, :hidden].astype(BF16)
        here = iota((hidden, 128), 0) + hidden * q == iota((hidden, 128), 1)
        placed = placed + dot(picked, here.astype(F32).astype(BF16))
    for g in range(groups):
        send_ref[seqs * g : seqs * (g + 1), :] = placed[seqs * g : seqs * (g + 1), :].astype(BF16)
    turned = dot_nt(factor_ref[hidden : 2 * hidden, :], ready)
    for k in range(rows // 128):
        turn_s[hidden * k : hidden * (k + 1), :] = turned[:, 128 * k : 128 * k + 128]
    chunks = hidden // group
    for k in range(rows // 128):
        blocks = [
            turn_s[pl.ds(hidden * k + q, chunks, stride=group), :] for q in range(group)
        ]
        for p, block in enumerate(block_transpose(blocks, width)):
            first = chunks * (group * k + p)
            line_s[first : first + chunks, :] = block
    base = seqs * groups
    for g in range(chunks):
        send_ref[base + seqs * g : base + seqs * (g + 1), :] = line_s[
            pl.ds(g, seqs, stride=chunks), :
        ].astype(BF16)
    send_ref[2 * base :, :] = edge_ref[...]


def block_transpose(blocks, step):
    lane = iota(blocks[0].shape, 1)
    for shift in (2 * step, step):
        low = lane // shift % 2 == 0
        stride = shift // step
        out = list(blocks)
        for q in range(len(blocks)):
            if q // stride % 2 == 0:
                x, y = blocks[q], blocks[q + stride]
                up = pltpu.roll(y, shift, 1)
                down = pltpu.roll(x, 4 * step - shift, 1)
                out[q] = jnp.where(low, x, up)
                out[q + stride] = jnp.where(low, down, y)
        blocks = out
    return blocks


def mean(values):
    return jnp.mean(values, -1, keepdims=True)


def merge_rows(parts):
    row = iota(parts[0].shape, 0)
    step = 1
    while len(parts) > 1:
        low = row // step % 2 == 0
        parts = [
            jnp.where(low, x, y) + pltpu.roll(jnp.where(low, y, x), step, 0)
            for x, y in zip(parts[::2], parts[1::2])
        ]
        step *= 2
    return parts[0]


def pair_kernel(
    axis,
    width,
    own,
    hidden,
    seqs,
    sides_ref,
    got_ref,
    own_loss_ref,
    after_ref,
    covariance_ref,
    edges_ref,
    cycle_ref,
    family_out_ref,
    out_ref,
    grad_ref,
    sem,
    right_s,
    flat_s,
    mid_s,
    unit_s,
    scale_s,
    a_s,
    b_s,
    tri_s,
):
    leave = pltpu.make_async_copy(after_ref, family_out_ref, sem)
    leave.start()
    me = lax.axis_index(axis)
    rank = me + 1 - 2 * (me % 2)
    n = sides_ref.shape[0]
    every = width * width
    group = 128 // hidden
    groups = width // group
    chunks = hidden // group
    pairs = own * width
    chans = 128
    total = seqs * n
    base = 2 * seqs * groups

    def gathered(first):
        return jnp.concatenate([sides_ref[d, first : first + seqs, :] for d in range(n)], 0)

    for g in range(chunks):
        turned = gathered(seqs * (groups + g)).T
        for q in range(group):
            right_s[width * g : width * (g + 1), total * q : total * (q + 1)] = turned[
                width * q : width * (q + 1), :
            ]
    block = iota((total, 128), 1) // hidden
    low_half = iota((width * chunks, 128), 1) < 64
    zero = jnp.zeros((total, 128), BF16)
    for g in range(groups):
        left = gathered(seqs * g)
        wide = left.astype(F32)
        rolled = [left] + [
            pltpu.roll(wide, hidden * d, 1).astype(BF16) for d in range(1, group)
        ]

        def placed(first, second, lane):
            return jnp.where(
                block == lane,
                rolled[(lane - first) % group],
                jnp.where(block == lane + 2, rolled[(lane + 2 - second) % group], zero),
            )

        halves = []
        for h in range(2):
            columns = []
            for even in range(0, group, 2):
                first, second = (even, even + 1) if h == 0 else (even + 1, even)
                columns.append(
                    jnp.concatenate([placed(first, second, lane) for lane in range(2)], 0)
                )
            halves.append(
                dot(
                    right_s[:, 2 * total * h : 2 * total * (h + 1)],
                    jnp.concatenate(columns, 1),
                ).astype(BF16)
            )
        for e in range(group // 2):
            x, y = (half[:, 128 * e : 128 * e + 128] for half in halves)
            for odd, outer in enumerate(
                (jnp.where(low_half, x, y), jnp.where(low_half, y, x))
            ):
                first = every // 2 * odd + width * (group // 2 * g + e)
                for c in range(chunks):
                    flat_s[first : first + width, 128 * c : 128 * c + 128] = outer[
                        width * c : width * (c + 1)
                    ]
    tiles = jnp.concatenate([got_ref[d ^ 1, :16, :] for d in range(n)], 0)
    pick = (iota((width, 128), 0) == iota((width, 128), 1)).astype(F32).astype(BF16)
    masks = dot_nt(pick, tiles)

    def kept(columns, first):
        return jnp.concatenate(
            [
                jnp.broadcast_to(columns[:, first + r : first + r + 1], (width, chans))
                for r in range(own)
            ],
            0,
        )

    count = width // PARTS
    lists = [
        [2 * (count * (p // 2) + k) + p % 2 for k in range(count)] for p in range(PARTS)
    ]
    centered = jnp.where(
        iota((chans, chans), 0) == iota((chans, chans), 1), 1.0 - 1.0 / chans, -1.0 / chans
    ).astype(BF16)
    added = [
        dot(
            flat_s[
                every // 2 * (p % 2) + width * count * (p // 2) : every // 2 * (p % 2)
                + width * count * (p // 2 + 1),
                :,
            ],
            covariance_ref[p % 2],
        )
        for p in range(PARTS)
    ]
    mids = []
    for p, residues in enumerate(lists):
        edge = jnp.concatenate(
            [
                sides_ref[i // own, base + width * (i % own) : base + width * (i % own + 1), :]
                for i in residues
            ],
            0,
        ).astype(F32)
        mids.append((edge + added[p] * (1.0 / total)).astype(BF16))
    centers = [dot(mid, centered) for mid in mids]
    scales = [lax.rsqrt(mean(c * c) + EPSILON) for c in centers]
    units = [c * scale for c, scale in zip(centers, scales)]
    sides = [dot(unit.astype(BF16), edges_ref[:, : 2 * chans]) for unit in units]
    for p, residues in enumerate(lists):
        for k, i in enumerate(residues):
            here = slice(width * k, width * (k + 1))
            there = slice(width * i, width * (i + 1))
            mid_s[there, :] = mids[p][here].astype(F32)
            scale_s[there, :] = jnp.broadcast_to(scales[p][here], (width, chans))
            unit_s[there, :] = units[p][here]
            lane = 16 * (i // own) + 2 * own + i % own
            keep = jnp.broadcast_to(masks[:, lane : lane + 1], (width, chans))
            a_s[there, :] = (keep * sides[p][here, :chans]).astype(BF16).astype(F32)
            b_s[there, :] = (keep * sides[p][here, chans:]).astype(BF16).astype(F32)

    rows = pl.ds(pl.multiple_of(me * pairs, pairs), pairs)

    def rows_and_columns(ref):
        return jnp.concatenate(
            [ref[rows, :]] + [ref[pl.ds(me * own + r, width, stride=width), :] for r in range(own)],
            0,
        )

    mid = mid_s[rows, :]
    losses = jnp.concatenate([got_ref[d ^ 1, 16:, :] for d in range(n)], 0)
    goal = iota((pairs, pairs), 0)
    source = goal % width // own * 16 + goal // width * own + goal % own
    place = (source == iota((pairs, pairs), 1)).astype(F32).astype(BF16)
    loss = jnp.concatenate([own_loss_ref[...].astype(F32), dot(place, losses)], 0)
    gating = jax.nn.sigmoid(
        dot(rows_and_columns(unit_s).astype(BF16), edges_ref[:, 2 * chans :])
    )
    leave.wait()
    tri = []
    for fixed, moving in ((a_s, b_s), (b_s, a_s)):
        held = fixed[rows, :]
        for r in range(own):
            mine = [held[width * r + 8 * v : width * r + 8 * v + 8] for v in range(width // 8)]
            for j in range(0, width, 8):
                parts = []
                for jj in range(j, j + 8):
                    prods = [
                        mine[v] * moving[width * jj + 8 * v : width * jj + 8 * v + 8, :]
                        for v in range(width // 8)
                    ]
                    parts.append(functools.reduce(jnp.add, prods))
                tri.append(merge_rows(parts))
    tri = jnp.concatenate(tri, 0)
    center = tri - mean(tri)
    scale_inv = lax.rsqrt(mean(center * center) + EPSILON)
    unit = center * scale_inv
    update = dot(unit[:pairs].astype(BF16), cycle_ref[...])
    out_ref[...] = (mid + gating[:pairs] * update).astype(BF16)
    grad_normed = dot_nt((loss * gating).astype(BF16), cycle_ref[...])
    tri_s[...] = (
        (
            scale_inv
            * (
                grad_normed - mean(grad_normed) - unit * mean(grad_normed * unit)
            )
        )
        .astype(BF16)
        .astype(F32)
    )

    acc = []
    for first, ref in ((0, b_s), (own, a_s)):
        sums = [[jnp.zeros((8, chans), F32) for _ in range(width // 8)] for _ in range(own)]
        for j in range(width):
            parts = [ref[width * j + 8 * v : width * j + 8 * v + 8, :] for v in range(width // 8)]
            for r in range(own):
                at = width * (first + r) + j
                row = jnp.broadcast_to(tri_s[at : at + 1, :], (8, chans))
                sums[r] = [old + row * part for old, part in zip(sums[r], parts)]
        acc += [jnp.concatenate(vregs, 0) for vregs in sums]
    keep = kept(dot_nt(pick, got_ref[rank, :16, :]), 2 * own)
    gate_own = gating[:pairs]
    grad_gate = loss[:pairs] * update * gate_own * (1.0 - gate_own)
    grad_proj = jnp.concatenate(
        [
            keep * jnp.concatenate(acc[:own], 0),
            keep * jnp.concatenate(acc[own:], 0),
            grad_gate,
        ],
        1,
    ).astype(BF16)
    grad_input = dot_nt(grad_proj, edges_ref[...])
    scale_inv = scale_s[rows, :]
    unit = unit_s[rows, :]
    grad_ref[...] = loss[:pairs] + scale_inv * (
        grad_input - mean(grad_input) - unit * mean(grad_input * unit)
    )


def body_resident(
    family_matrix,
    edge_matrix,
    edge_validity,
    query_key_value_gate_matrix,
    logit_offset_matrix,
    heads_merge_matrix,
    left_right_factor_matrix,
    covariance_merge_matrix,
    edges_gate_factor_matrix,
    cycle_merge_matrix,
    loss_sensitivity,
):
    seqs, width, depth = family_matrix.shape
    own, _, chans = edge_matrix.shape
    heads = logit_offset_matrix.shape[1]
    hidden = left_right_factor_matrix.shape[1] // 2
    pairs = own * width
    every = width * width
    edge = edge_matrix.reshape(pairs, chans)
    loss = loss_sensitivity.reshape(pairs, chans)
    vmem = pl.BlockSpec(memory_space=pltpu.VMEM)
    hbm = pl.BlockSpec(memory_space=pltpu.HBM)
    family = family_matrix.reshape(seqs * width, depth)
    factor = left_right_factor_matrix.T
    sided = 2 * seqs * width * hidden // 128
    peers = width // own
    packed = pl.pallas_call(
        functools.partial(pack_kernel, width),
        out_shape=jax.ShapeDtypeStruct((32 * peers, chans), BF16),
        in_specs=[hbm] * 4,
        out_specs=vmem,
        scratch_shapes=[
            pltpu.VMEM((pairs, chans), BF16),
            pltpu.VMEM((heads, chans), BF16),
            pltpu.VMEM((pairs, chans), BF16),
            pltpu.VMEM((own, width), jnp.int32),
            pltpu.VMEM((16, 128), F32),
            pltpu.SemaphoreType.DMA((4,)),
        ],
        name="pack_pairs",
    )(edge, logit_offset_matrix.T, loss, edge_validity)
    got = lax.all_to_all(
        packed, "dap", split_axis=0, concat_axis=0, axis_index_groups=[[d ^ 1 for d in range(peers)]], tiled=True
    )
    got = got.reshape(peers, 32, chans)
    logits, value, gating, covariance = pl.pallas_call(
        functools.partial(project_kernel, width, heads, hidden),
        out_shape=(
            jax.ShapeDtypeStruct((seqs * width, depth), F32),
            jax.ShapeDtypeStruct((seqs * 128, depth), BF16),
            jax.ShapeDtypeStruct((seqs * width, depth), F32),
            jax.ShapeDtypeStruct((2, hidden * hidden, chans), BF16),
        ),
        in_specs=[hbm, hbm, hbm],
        out_specs=(vmem,) * 4,
        scratch_shapes=[
            pltpu.VMEM((seqs * width, depth), BF16),
            pltpu.VMEM(query_key_value_gate_matrix.shape, BF16),
            pltpu.VMEM(covariance_merge_matrix.shape, BF16),
            pltpu.SemaphoreType.DMA((3,)),
        ]
        + [pltpu.VMEM((seqs * width, depth), BF16)] * 3
        + [pltpu.VMEM((seqs * width, 128), F32)]
        + [pltpu.VMEM((hidden * hidden, chans), F32)],
        compiler_params=pltpu.CompilerParams(vmem_limit_bytes=16 << 20),
        cost_estimate=pl.CostEstimate(
            flops=16 * seqs * width * depth * depth,
            bytes_accessed=32 * seqs * width * depth,
            transcendentals=seqs * width * depth,
        ),
        name="project_family",
    )(
        pltpu.with_memory_space_constraint(family, pltpu.HBM),
        pltpu.with_memory_space_constraint(query_key_value_gate_matrix, pltpu.HBM),
        pltpu.with_memory_space_constraint(covariance_merge_matrix, pltpu.HBM),
    )
    after, send = pl.pallas_call(
        functools.partial(attention_kernel, width, own),
        out_shape=(
            jax.ShapeDtypeStruct((seqs * width, depth), BF16),
            jax.ShapeDtypeStruct((sided + pairs, 128), BF16),
        ),
        in_specs=[vmem] * 8,
        out_specs=(vmem, vmem),
        scratch_shapes=[
            pltpu.VMEM((seqs * width, depth), BF16),
            pltpu.VMEM((seqs * width, 128), F32),
            pltpu.VMEM((seqs * width * hidden // 128, 128), F32),
            pltpu.VMEM((seqs * width * hidden // 128, 128), F32),
        ],
        compiler_params=pltpu.CompilerParams(vmem_limit_bytes=16 << 20),
        name="row_attention",
    )(family, got, logits, value, gating, heads_merge_matrix, factor, edge)
    gathered = lax.all_gather(send, "dap", axis=0, tiled=False)
    family_out, pair_out, pair_grad = pl.pallas_call(
        functools.partial(pair_kernel, "dap", width, own, hidden, seqs),
        out_shape=(
            jax.ShapeDtypeStruct((seqs * width, depth), BF16),
            jax.ShapeDtypeStruct((pairs, chans), BF16),
            jax.ShapeDtypeStruct((pairs, chans), F32),
        ),
        in_specs=[vmem] * 7,
        out_specs=(hbm, vmem, vmem),
        scratch_shapes=[
            pltpu.SemaphoreType.DMA(()),
            pltpu.VMEM((width * hidden * hidden // 128, 128 // hidden * 128), BF16),
            pltpu.VMEM((every, hidden * hidden), BF16),
            pltpu.VMEM((every, chans), F32),
            pltpu.VMEM((every, chans), F32),
            pltpu.VMEM((every, chans), F32),
            pltpu.VMEM((every, chans), F32),
            pltpu.VMEM((every, chans), F32),
            pltpu.VMEM((2 * pairs, chans), F32),
        ],
        compiler_params=pltpu.CompilerParams(vmem_limit_bytes=16 << 20),
        name="pair_update",
    )(gathered, got, loss, after, covariance, edges_gate_factor_matrix, cycle_merge_matrix)
    return (
        family_out.reshape(seqs, width, depth),
        pair_out.reshape(own, width, chans),
        pair_grad.reshape(own, width, chans),
    )


def fits_resident(dap, family, edge, logit, factor):
    seqs, width, depth = family.shape
    own, _, chans = edge.shape
    return (
        own * dap == width
        and dap % 2 == 0
        and width == 32
        and factor.shape[1] == 64
        and depth == 32 * logit.shape[1]
        and depth % 128 == 0
        and chans == 128
        and own * width == 128
        and seqs % 16 == 0
        and seqs * dap == 128
    )


def body(*args):
    dap = lax.axis_size("dap")
    if fits_resident(dap, args[0], args[1], args[4], args[6]):
        return body_resident(*args)
    return body_general(*args)


def solution(mesh):
    in_specs = (
        P(("dp", "dap"), None, None),
        P(("dp", "dap"), None, None),
        P(("dp", "dap"), None),
        P(),
        P(),
        P(),
        P(),
        P(),
        P(),
        P(),
        P(("dp", "dap"), None, None),
    )
    out_specs = (
        P(("dp", "dap"), None, None),
        P(("dp", "dap"), None, None),
        P(("dp", "dap"), None, None),
    )
    return jax.shard_map(body, mesh=mesh, in_specs=in_specs, out_specs=out_specs, check_vma=False)
```

```python
import functools
import math

import jax
import jax.numpy as jnp
from jax import lax
from jax.experimental import pallas as pl
from jax.experimental.pallas import tpu as pltpu
from jax.sharding import PartitionSpec as P

EPSILON = 1e-05


def standardize_features(values):
    center = values - jnp.mean(values, -1, keepdims=True)
    scale_inv = lax.rsqrt(jnp.mean(center * center, -1, keepdims=True) + EPSILON)
    return center * scale_inv


def norm_back(values, grad_out):
    center = values - jnp.mean(values, -1, keepdims=True)
    scale_inv = lax.rsqrt(jnp.mean(center * center, -1, keepdims=True) + EPSILON)
    standardized_source = center * scale_inv
    return scale_inv * (
        grad_out
        - jnp.mean(grad_out, -1, keepdims=True)
        - standardized_source * jnp.mean(grad_out * standardized_source, -1, keepdims=True)
    )


def lateral_heads_mixing(
    family_shard_slice, logit_offset_whole, query_key_value_gate_matrix, heads_merge_matrix
):
    homolog_number, amino_number, feature_depth = family_shard_slice.shape
    head_count = logit_offset_whole.shape[1]
    head_size = feature_depth // head_count
    standardized_source = standardize_features(family_shard_slice.astype(jnp.float32)).astype(
        jnp.bfloat16
    )
    projected = jnp.dot(
        standardized_source.reshape(-1, feature_depth),
        query_key_value_gate_matrix,
        preferred_element_type=jnp.float32,
    )
    projected = projected.reshape(homolog_number, amino_number, 4 * feature_depth)
    shape_heads = (homolog_number, amino_number, head_count, head_size)
    queries = projected[..., :feature_depth].astype(jnp.bfloat16).reshape(shape_heads)
    key_rows = (
        projected[..., feature_depth : 2 * feature_depth].astype(jnp.bfloat16).reshape(shape_heads)
    )
    value_rows = (
        projected[..., 2 * feature_depth : 3 * feature_depth]
        .astype(jnp.bfloat16)
        .reshape(shape_heads)
    )
    gating = jax.nn.sigmoid(projected[..., 3 * feature_depth :])
    logits = jnp.einsum("sihd,sjhd->sihj", queries, key_rows, preferred_element_type=jnp.float32)
    logits = logits / math.sqrt(head_size) + logit_offset_whole.astype(jnp.float32)[None]
    weights = jax.nn.softmax(logits, axis=-1).astype(jnp.bfloat16)
    mixed = jnp.einsum("sihj,sjhd->sihd", weights, value_rows, preferred_element_type=jnp.float32)
    gated = (gating * mixed.reshape(homolog_number, amino_number, feature_depth)).astype(
        jnp.bfloat16
    )
    edge_increment = jnp.dot(
        gated.reshape(-1, feature_depth), heads_merge_matrix, preferred_element_type=jnp.float32
    )
    return (
        family_shard_slice.astype(jnp.float32)
        + edge_increment.reshape(homolog_number, amino_number, feature_depth)
    ).astype(jnp.bfloat16)


def pair_projection_step(alignment_rows, left_right_factor_matrix):
    standardized_source = standardize_features(alignment_rows.astype(jnp.float32)).astype(
        jnp.bfloat16
    )
    edge_result = jnp.dot(
        standardized_source.reshape(-1, alignment_rows.shape[2]),
        left_right_factor_matrix,
        preferred_element_type=jnp.float32,
    )
    return edge_result.reshape(alignment_rows.shape[0], alignment_rows.shape[1], -1).astype(
        jnp.bfloat16
    )


def body_general(
    family_matrix,
    edge_matrix,
    edge_validity,
    query_key_value_gate_matrix,
    logit_offset_matrix,
    heads_merge_matrix,
    left_right_factor_matrix,
    covariance_merge_matrix,
    edges_gate_factor_matrix,
    cycle_merge_matrix,
    loss_sensitivity,
):
    res_rows, width, pair_chans = edge_matrix.shape
    pair_normed = standardize_features(edge_matrix.astype(jnp.float32)).astype(jnp.bfloat16)
    bias_local = jnp.einsum(
        "ijc,ch->ihj", pair_normed, logit_offset_matrix, preferred_element_type=jnp.float32
    ).astype(jnp.bfloat16)
    logit_offset_whole = lax.all_gather(bias_local, "dap", axis=0, tiled=True)
    homolog_lines = family_matrix.shape[0]
    homolog_subset = math.gcd(homolog_lines, 8)
    batched_lines = family_matrix.reshape(
        homolog_lines // homolog_subset,
        homolog_subset,
        family_matrix.shape[1],
        family_matrix.shape[2],
    )
    family_after_heads = lax.map(
        lambda family_shard_slice: lateral_heads_mixing(
            family_shard_slice, logit_offset_whole, query_key_value_gate_matrix, heads_merge_matrix
        ),
        batched_lines,
    ).reshape(family_matrix.shape)
    hidden = left_right_factor_matrix.shape[1] // 2
    weight_f32 = covariance_merge_matrix.astype(jnp.float32)
    alignment_columns = lax.all_to_all(
        family_after_heads, "dap", split_axis=1, concat_axis=0, tiled=True
    )
    edge_result = pair_projection_step(alignment_columns, left_right_factor_matrix)
    left_part = edge_result[..., :hidden]
    right_part = edge_result[..., hidden:]
    sequence_full_count = alignment_columns.shape[0]
    shard_in = lax.all_gather(right_part, "dap", axis=1, tiled=True)
    outer_sum = (
        jnp.einsum("sia,sjb->ijab", left_part, shard_in, preferred_element_type=jnp.float32)
        / sequence_full_count
    )
    row_count = shard_in.shape[1]
    flat = outer_sum.reshape(res_rows * row_count, hidden * hidden)
    edge_increment = jnp.dot(flat, weight_f32, precision=lax.Precision.HIGHEST).reshape(
        res_rows, row_count, pair_chans
    )
    pair_mid = (edge_matrix.astype(jnp.float32) + edge_increment).astype(jnp.bfloat16)
    tri_normed = standardize_features(pair_mid.astype(jnp.float32)).astype(jnp.bfloat16)
    tri_proj = jnp.dot(
        tri_normed.reshape(-1, pair_chans),
        edges_gate_factor_matrix,
        preferred_element_type=jnp.float32,
    ).reshape(res_rows, width, 3 * pair_chans)
    mask_f = edge_validity.astype(jnp.float32)[..., None]
    side_a = (mask_f * tri_proj[..., :pair_chans]).astype(jnp.bfloat16)
    side_b = (mask_f * tri_proj[..., pair_chans : 2 * pair_chans]).astype(jnp.bfloat16)
    gating = jax.nn.sigmoid(tri_proj[..., 2 * pair_chans :])
    tri_prod = jnp.einsum(
        "ikc,jkc->ijc",
        side_a,
        lax.all_gather(side_b, "dap", axis=0, tiled=True),
        preferred_element_type=jnp.float32,
    )
    prod_normed = standardize_features(tri_prod).astype(jnp.bfloat16)
    tri_update = jnp.dot(
        prod_normed.reshape(-1, pair_chans), cycle_merge_matrix, preferred_element_type=jnp.float32
    ).reshape(res_rows, width, pair_chans)
    pair_output = (pair_mid.astype(jnp.float32) + gating * tri_update).astype(jnp.bfloat16)
    cot_f32 = loss_sensitivity.astype(jnp.float32)
    grad_update = (cot_f32 * gating).astype(jnp.bfloat16)
    grad_normed = jnp.dot(
        grad_update.reshape(-1, pair_chans),
        cycle_merge_matrix.T,
        preferred_element_type=jnp.float32,
    ).reshape(res_rows, width, pair_chans)
    grad_prod = norm_back(tri_prod, grad_normed).astype(jnp.bfloat16)
    grad_part = grad_prod
    grad_a = jnp.einsum(
        "ijc,jkc->ikc",
        grad_part,
        lax.all_gather(side_b, "dap", axis=0, tiled=True),
        preferred_element_type=jnp.float32,
    )
    grad_part = grad_prod
    grad_b = lax.psum_scatter(
        jnp.einsum("ijc,ikc->jkc", grad_part, side_a, preferred_element_type=jnp.float32).astype(
            jnp.bfloat16
        ),
        "dap",
        scatter_dimension=0,
        tiled=True,
    ).astype(jnp.float32)
    grad_gate = cot_f32 * tri_update * gating * (1.0 - gating)
    grad_proj = jnp.concatenate([mask_f * grad_a, mask_f * grad_b, grad_gate], -1).astype(
        jnp.bfloat16
    )
    grad_input = jnp.dot(
        grad_proj.reshape(-1, 3 * pair_chans),
        edges_gate_factor_matrix.T,
        preferred_element_type=jnp.float32,
    ).reshape(res_rows, width, pair_chans)
    pair_gradient = cot_f32 + norm_back(pair_mid.astype(jnp.float32), grad_input)
    return (family_after_heads, pair_output, pair_gradient)


F32 = jnp.float32
BF16 = jnp.bfloat16
NT = (((1,), (1,)), ((), ()))
PARTS = 2


def dot(a, b):
    return jnp.dot(a, b, preferred_element_type=F32)


def dot_nt(a, b):
    return lax.dot_general(a, b, NT, preferred_element_type=F32)


def iota(shape, dim):
    return lax.broadcasted_iota(jnp.int32, shape, dim)


def pack_kernel(
    width, edge_ref, weight_ref, loss_ref, mask_ref, send_ref, edge_s, weight_s, loss_s, mask_s,
    tile_s, sems
):
    copies = [
        pltpu.make_async_copy(source, target, sems.at[k])
        for k, (source, target) in enumerate(
            (
                (edge_ref, edge_s),
                (weight_ref, weight_s),
                (loss_ref, loss_s),
                (mask_ref, mask_s),
            )
        )
    ]
    for copy in copies:
        copy.start()
    rows, chans = edge_s.shape
    heads = weight_s.shape[0]
    own = rows // width
    lanes = heads * width
    peers = width // own
    spread = (iota((heads, lanes), 0) == iota((heads, lanes), 1) // width).astype(F32)
    keep = iota((width, lanes), 0) == iota((width, lanes), 1) % width
    goal = iota((rows, rows), 0)
    source = goal % own * width + goal // (own * own) * own + goal // own % own
    place = (source == iota((rows, rows), 1)).astype(F32).astype(BF16)
    tile_s[...] = jnp.zeros(tile_s.shape, F32)
    for copy in copies:
        copy.wait()
    weight = lax.dot_general(
        weight_s[...], spread.astype(BF16), (((0,), (0,)), ((), ())), preferred_element_type=F32
    ).astype(BF16)
    column = dot(jnp.ones((8, chans), BF16), weight)[:1]
    every = dot(edge_s[...], weight)
    edge = edge_s[...].astype(F32)
    middle = jnp.mean(edge, -1, keepdims=True)
    center = edge - middle
    scale = lax.rsqrt(jnp.mean(center * center, -1, keepdims=True) + EPSILON)
    bias = scale * (every - middle * column)
    losses = dot(place, loss_s[...]).astype(BF16)
    tile_s[2 * own : 3 * own, :width] = mask_s[...].astype(F32)
    packed = tile_s[...]
    for r in range(own):
        picked = jnp.where(keep, bias[width * r : width * (r + 1)], 0.0)
        total = jnp.sum(picked, 0, keepdims=True)
        for t in range(lanes // 128):
            packed = jnp.where(
                iota((16, 128), 0) == own * t + r, total[:, 128 * t : 128 * t + 128], packed
            )
    packed = packed.astype(BF16)
    for e in range(peers):
        rank = e ^ 1
        send_ref[32 * rank : 32 * rank + 16, :] = packed
        send_ref[32 * rank + 16 : 32 * rank + 32, :] = losses[16 * e : 16 * e + 16]


def project_kernel(
    width,
    heads,
    hidden,
    family_hbm,
    project_hbm,
    covariance_hbm,
    logits_ref,
    value_ref,
    gating_ref,
    cov_ref,
    family_ref,
    project_ref,
    covariance_ref,
    sems,
    query_s,
    key_s,
    value_s,
    logits_s,
    cov_s,
):
    copies = [
        pltpu.make_async_copy(family_hbm, family_ref, sems.at[2]),
        pltpu.make_async_copy(project_hbm, project_ref, sems.at[0]),
        pltpu.make_async_copy(covariance_hbm, covariance_ref, sems.at[1]),
    ]
    for copy in copies:
        copy.start()
    rows, depth = family_ref.shape
    seqs = rows // width
    group = 128 // width
    copies[0].wait()
    normed = standardize_features(family_ref[...].astype(F32)).astype(BF16)
    copies[1].wait()
    query_s[...] = dot(normed, project_ref[:, :depth]).astype(BF16)
    key_s[...] = dot(normed, project_ref[:, depth : 2 * depth]).astype(BF16)
    value_s[...] = dot(normed, project_ref[:, 2 * depth : 3 * depth]).astype(BF16)
    gating_ref[...] = jax.nn.sigmoid(dot(normed, project_ref[:, 3 * depth :]))
    same = (iota((128, 128), 0) // width == iota((128, 128), 1) // width).astype(F32).astype(BF16)
    scale = 1.0 / math.sqrt(depth // heads)
    for t in range(depth // 128):
        cols = slice(128 * t, 128 * t + 128)
        for s in range(seqs):
            span = slice(width * s, width * s + width)
            keys = jnp.concatenate([key_s[span, cols]] * group, 0) * same
            logits_s[span, :] = dot_nt(query_s[span, cols], keys) * scale
            values = jnp.concatenate([value_s[span, cols]] * group, 0) * same
            value_ref[128 * s : 128 * (s + 1), cols] = values
        for k in range(rows // 128):
            span = slice(128 * k, 128 * (k + 1))
            logits_ref[span, cols] = logits_s[span, :].T
    copies[2].wait()
    cov_s[...] = covariance_ref[...].astype(F32)
    for b in range(hidden):
        rows_b = cov_s[pl.ds(b, hidden, stride=hidden), :].astype(BF16)
        cov_ref[0, hidden * b : hidden * (b + 1), :] = rows_b
        swapped = b ^ (group // 2)
        cov_ref[1, hidden * swapped : hidden * (swapped + 1), :] = rows_b


def attention_kernel(
    width,
    own,
    family_ref,
    got_ref,
    logits_ref,
    value_ref,
    gating_ref,
    merge_ref,
    factor_ref,
    edge_ref,
    after_ref,
    send_ref,
    weight_s,
    row_s,
    turn_s,
    line_s,
):
    rows, depth = family_ref.shape
    seqs = rows // width
    tiles = depth // 128
    group = 128 // width
    biases = jnp.concatenate([got_ref[d ^ 1, :16, :] for d in range(got_ref.shape[0])], 0)
    gated = []
    for t in range(tiles):
        cols = slice(128 * t, 128 * t + 128)
        row = iota((128, biases.shape[0]), 0) % width
        take = iota((128, biases.shape[0]), 1) == 16 * (row // own) + own * t + row % own
        bias = dot(take.astype(F32).astype(BF16), biases).T
        for k in range(rows // 128):
            span = slice(128 * k, 128 * (k + 1))
            flipped = logits_ref[span, cols] + bias
            parts = []
            for h in range(group):
                some = flipped[width * h : width * (h + 1)]
                raised = jnp.exp(some - jnp.max(some, 0, keepdims=True))
                parts.append(raised * (1.0 / jnp.sum(raised, 0, keepdims=True)))
            weight_s[span, cols] = jnp.concatenate(parts, 0).astype(BF16).T
    for t in range(tiles):
        cols = slice(128 * t, 128 * t + 128)
        mixed = jnp.concatenate(
            [
                dot(weight_s[width * s : width * (s + 1), cols], value_ref[128 * s : 128 * (s + 1), cols])
                for s in range(seqs)
            ],
            0,
        )
        gated.append((gating_ref[:, cols] * mixed).astype(BF16))
    after = (
        family_ref[...].astype(F32) + dot(jnp.concatenate(gated, 1), merge_ref[...])
    ).astype(BF16)
    after_ref[...] = after
    ready = standardize_features(after.astype(F32)).astype(BF16)
    hidden = factor_ref.shape[0] // 2
    groups = width // group
    row_s[:, : 2 * hidden] = dot_nt(ready, factor_ref[...])
    placed = jnp.zeros((groups * seqs, 128), F32)
    for q in range(group):
        picked = jnp.concatenate(
            [row_s[pl.ds(group * g + q, seqs, stride=width), :] for g in range(groups)], 0
        )[:, :hidden].astype(BF16)
        here = iota((hidden, 128), 0) + hidden * q == iota((hidden, 128), 1)
        placed = placed + dot(picked, here.astype(F32).astype(BF16))
    for g in range(groups):
        send_ref[seqs * g : seqs * (g + 1), :] = placed[seqs * g : seqs * (g + 1), :].astype(BF16)
    turned = dot_nt(factor_ref[hidden : 2 * hidden, :], ready)
    for k in range(rows // 128):
        turn_s[hidden * k : hidden * (k + 1), :] = turned[:, 128 * k : 128 * k + 128]
    chunks = hidden // group
    for k in range(rows // 128):
        blocks = [
            turn_s[pl.ds(hidden * k + q, chunks, stride=group), :] for q in range(group)
        ]
        for p, block in enumerate(block_transpose(blocks, width)):
            first = chunks * (group * k + p)
            line_s[first : first + chunks, :] = block
    base = seqs * groups
    for g in range(chunks):
        send_ref[base + seqs * g : base + seqs * (g + 1), :] = line_s[
            pl.ds(g, seqs, stride=chunks), :
        ].astype(BF16)
    send_ref[2 * base :, :] = edge_ref[...]


def block_transpose(blocks, step):
    lane = iota(blocks[0].shape, 1)
    for shift in (2 * step, step):
        low = lane // shift % 2 == 0
        stride = shift // step
        out = list(blocks)
        for q in range(len(blocks)):
            if q // stride % 2 == 0:
                x, y = blocks[q], blocks[q + stride]
                up = pltpu.roll(y, shift, 1)
                down = pltpu.roll(x, 4 * step - shift, 1)
                out[q] = jnp.where(low, x, up)
                out[q + stride] = jnp.where(low, down, y)
        blocks = out
    return blocks


def mean(values):
    return jnp.mean(values, -1, keepdims=True)


def merge_rows(parts):
    row = iota(parts[0].shape, 0)
    step = 1
    while len(parts) > 1:
        low = row // step % 2 == 0
        parts = [
            jnp.where(low, x, y) + pltpu.roll(jnp.where(low, y, x), step, 0)
            for x, y in zip(parts[::2], parts[1::2])
        ]
        step *= 2
    return parts[0]


def pair_kernel(
    axis,
    width,
    own,
    hidden,
    seqs,
    sides_ref,
    got_ref,
    own_loss_ref,
    after_ref,
    covariance_ref,
    edges_ref,
    cycle_ref,
    family_out_ref,
    out_ref,
    grad_ref,
    sem,
    right_s,
    flat_s,
    mid_s,
    unit_s,
    scale_s,
    a_s,
    b_s,
    tri_s,
):
    leave = pltpu.make_async_copy(after_ref, family_out_ref, sem)
    leave.start()
    me = lax.axis_index(axis)
    rank = me + 1 - 2 * (me % 2)
    n = sides_ref.shape[0]
    every = width * width
    group = 128 // hidden
    groups = width // group
    chunks = hidden // group
    pairs = own * width
    chans = 128
    total = seqs * n
    base = 2 * seqs * groups

    def gathered(first):
        return jnp.concatenate([sides_ref[d, first : first + seqs, :] for d in range(n)], 0)

    for g in range(chunks):
        turned = gathered(seqs * (groups + g)).T
        for q in range(group):
            right_s[width * g : width * (g + 1), total * q : total * (q + 1)] = turned[
                width * q : width * (q + 1), :
            ]
    block = iota((total, 128), 1) // hidden
    low_half = iota((width * chunks, 128), 1) < 64
    zero = jnp.zeros((total, 128), BF16)
    for g in range(groups):
        left = gathered(seqs * g)
        wide = left.astype(F32)
        rolled = [left] + [
            pltpu.roll(wide, hidden * d, 1).astype(BF16) for d in range(1, group)
        ]

        def placed(first, second, lane):
            return jnp.where(
                block == lane,
                rolled[(lane - first) % group],
                jnp.where(block == lane + 2, rolled[(lane + 2 - second) % group], zero),
            )

        halves = []
        for h in range(2):
            columns = []
            for even in range(0, group, 2):
                first, second = (even, even + 1) if h == 0 else (even + 1, even)
                columns.append(
                    jnp.concatenate([placed(first, second, lane) for lane in range(2)], 0)
                )
            halves.append(
                dot(
                    right_s[:, 2 * total * h : 2 * total * (h + 1)],
                    jnp.concatenate(columns, 1),
                ).astype(BF16)
            )
        for e in range(group // 2):
            x, y = (half[:, 128 * e : 128 * e + 128] for half in halves)
            for odd, outer in enumerate(
                (jnp.where(low_half, x, y), jnp.where(low_half, y, x))
            ):
                first = every // 2 * odd + width * (group // 2 * g + e)
                for c in range(chunks):
                    flat_s[first : first + width, 128 * c : 128 * c + 128] = outer[
                        width * c : width * (c + 1)
                    ]
    tiles = jnp.concatenate([got_ref[d ^ 1, :16, :] for d in range(n)], 0)
    pick = (iota((width, 128), 0) == iota((width, 128), 1)).astype(F32).astype(BF16)
    masks = dot_nt(pick, tiles)

    def kept(columns, first):
        return jnp.concatenate(
            [
                jnp.broadcast_to(columns[:, first + r : first + r + 1], (width, chans))
                for r in range(own)
            ],
            0,
        )

    count = width // PARTS
    lists = [
        [2 * (count * (p // 2) + k) + p % 2 for k in range(count)] for p in range(PARTS)
    ]
    centered = jnp.where(
        iota((chans, chans), 0) == iota((chans, chans), 1), 1.0 - 1.0 / chans, -1.0 / chans
    ).astype(BF16)
    added = [
        dot(
            flat_s[
                every // 2 * (p % 2) + width * count * (p // 2) : every // 2 * (p % 2)
                + width * count * (p // 2 + 1),
                :,
            ],
            covariance_ref[p % 2],
        )
        for p in range(PARTS)
    ]
    mids = []
    for p, residues in enumerate(lists):
        edge = jnp.concatenate(
            [
                sides_ref[i // own, base + width * (i % own) : base + width * (i % own + 1), :]
                for i in residues
            ],
            0,
        ).astype(F32)
        mids.append((edge + added[p] * (1.0 / total)).astype(BF16))
    centers = [dot(mid, centered) for mid in mids]
    scales = [lax.rsqrt(mean(c * c) + EPSILON) for c in centers]
    units = [c * scale for c, scale in zip(centers, scales)]
    sides = [dot(unit.astype(BF16), edges_ref[:, : 2 * chans]) for unit in units]
    for p, residues in enumerate(lists):
        for k, i in enumerate(residues):
            here = slice(width * k, width * (k + 1))
            there = slice(width * i, width * (i + 1))
            mid_s[there, :] = mids[p][here].astype(F32)
            scale_s[there, :] = jnp.broadcast_to(scales[p][here], (width, chans))
            unit_s[there, :] = units[p][here]
            lane = 16 * (i // own) + 2 * own + i % own
            keep = jnp.broadcast_to(masks[:, lane : lane + 1], (width, chans))
            a_s[there, :] = (keep * sides[p][here, :chans]).astype(BF16).astype(F32)
            b_s[there, :] = (keep * sides[p][here, chans:]).astype(BF16).astype(F32)

    rows = pl.ds(pl.multiple_of(me * pairs, pairs), pairs)

    def rows_and_columns(ref):
        return jnp.concatenate(
            [ref[rows, :]] + [ref[pl.ds(me * own + r, width, stride=width), :] for r in range(own)],
            0,
        )

    mid = mid_s[rows, :]
    losses = jnp.concatenate([got_ref[d ^ 1, 16:, :] for d in range(n)], 0)
    goal = iota((pairs, pairs), 0)
    source = goal % width // own * 16 + goal // width * own + goal % own
    place = (source == iota((pairs, pairs), 1)).astype(F32).astype(BF16)
    loss = jnp.concatenate([own_loss_ref[...].astype(F32), dot(place, losses)], 0)
    gating = jax.nn.sigmoid(
        dot(rows_and_columns(unit_s).astype(BF16), edges_ref[:, 2 * chans :])
    )
    tri = []
    for fixed, moving in ((a_s, b_s), (b_s, a_s)):
        held = fixed[rows, :]
        for r in range(own):
            mine = [held[width * r + 8 * v : width * r + 8 * v + 8] for v in range(width // 8)]
            for j in range(0, width, 8):
                parts = []
                for jj in range(j, j + 8):
                    prods = [
                        mine[v] * moving[width * jj + 8 * v : width * jj + 8 * v + 8, :]
                        for v in range(width // 8)
                    ]
                    parts.append(functools.reduce(jnp.add, prods))
                tri.append(merge_rows(parts))
    leave.wait()
    tri = jnp.concatenate(tri, 0)
    center = tri - mean(tri)
    scale_inv = lax.rsqrt(mean(center * center) + EPSILON)
    unit = center * scale_inv
    update = dot(unit[:pairs].astype(BF16), cycle_ref[...])
    out_ref[...] = (mid + gating[:pairs] * update).astype(BF16)
    grad_normed = dot_nt((loss * gating).astype(BF16), cycle_ref[...])
    tri_s[...] = (
        (
            scale_inv
            * (
                grad_normed - mean(grad_normed) - unit * mean(grad_normed * unit)
            )
        )
        .astype(BF16)
        .astype(F32)
    )

    acc = []
    for first, ref in ((0, b_s), (own, a_s)):
        sums = [[jnp.zeros((8, chans), F32) for _ in range(width // 8)] for _ in range(own)]
        for j in range(width):
            parts = [ref[width * j + 8 * v : width * j + 8 * v + 8, :] for v in range(width // 8)]
            for r in range(own):
                at = width * (first + r) + j
                row = jnp.broadcast_to(tri_s[at : at + 1, :], (8, chans))
                sums[r] = [old + row * part for old, part in zip(sums[r], parts)]
        acc += [jnp.concatenate(vregs, 0) for vregs in sums]
    keep = kept(dot_nt(pick, got_ref[rank, :16, :]), 2 * own)
    gate_own = gating[:pairs]
    grad_gate = loss[:pairs] * update * gate_own * (1.0 - gate_own)
    grad_proj = jnp.concatenate(
        [
            keep * jnp.concatenate(acc[:own], 0),
            keep * jnp.concatenate(acc[own:], 0),
            grad_gate,
        ],
        1,
    ).astype(BF16)
    grad_input = dot_nt(grad_proj, edges_ref[...])
    scale_inv = scale_s[rows, :]
    unit = unit_s[rows, :]
    grad_ref[...] = loss[:pairs] + scale_inv * (
        grad_input - mean(grad_input) - unit * mean(grad_input * unit)
    )


def body_resident(
    family_matrix,
    edge_matrix,
    edge_validity,
    query_key_value_gate_matrix,
    logit_offset_matrix,
    heads_merge_matrix,
    left_right_factor_matrix,
    covariance_merge_matrix,
    edges_gate_factor_matrix,
    cycle_merge_matrix,
    loss_sensitivity,
):
    seqs, width, depth = family_matrix.shape
    own, _, chans = edge_matrix.shape
    heads = logit_offset_matrix.shape[1]
    hidden = left_right_factor_matrix.shape[1] // 2
    pairs = own * width
    every = width * width
    edge = edge_matrix.reshape(pairs, chans)
    loss = loss_sensitivity.reshape(pairs, chans)
    vmem = pl.BlockSpec(memory_space=pltpu.VMEM)
    hbm = pl.BlockSpec(memory_space=pltpu.HBM)
    family = family_matrix.reshape(seqs * width, depth)
    factor = left_right_factor_matrix.T
    sided = 2 * seqs * width * hidden // 128
    peers = width // own
    packed = pl.pallas_call(
        functools.partial(pack_kernel, width),
        out_shape=jax.ShapeDtypeStruct((32 * peers, chans), BF16),
        in_specs=[hbm] * 4,
        out_specs=vmem,
        scratch_shapes=[
            pltpu.VMEM((pairs, chans), BF16),
            pltpu.VMEM((heads, chans), BF16),
            pltpu.VMEM((pairs, chans), BF16),
            pltpu.VMEM((own, width), jnp.int32),
            pltpu.VMEM((16, 128), F32),
            pltpu.SemaphoreType.DMA((4,)),
        ],
        name="pack_pairs",
    )(edge, logit_offset_matrix.T, loss, edge_validity)
    got = lax.all_to_all(
        packed, "dap", split_axis=0, concat_axis=0, axis_index_groups=[[d ^ 1 for d in range(peers)]], tiled=True
    )
    got = got.reshape(peers, 32, chans)
    logits, value, gating, covariance = pl.pallas_call(
        functools.partial(project_kernel, width, heads, hidden),
        out_shape=(
            jax.ShapeDtypeStruct((seqs * width, depth), F32),
            jax.ShapeDtypeStruct((seqs * 128, depth), BF16),
            jax.ShapeDtypeStruct((seqs * width, depth), F32),
            jax.ShapeDtypeStruct((2, hidden * hidden, chans), BF16),
        ),
        in_specs=[hbm, hbm, hbm],
        out_specs=(vmem,) * 4,
        scratch_shapes=[
            pltpu.VMEM((seqs * width, depth), BF16),
            pltpu.VMEM(query_key_value_gate_matrix.shape, BF16),
            pltpu.VMEM(covariance_merge_matrix.shape, BF16),
            pltpu.SemaphoreType.DMA((3,)),
        ]
        + [pltpu.VMEM((seqs * width, depth), BF16)] * 3
        + [pltpu.VMEM((seqs * width, 128), F32)]
        + [pltpu.VMEM((hidden * hidden, chans), F32)],
        compiler_params=pltpu.CompilerParams(vmem_limit_bytes=16 << 20),
        cost_estimate=pl.CostEstimate(
            flops=16 * seqs * width * depth * depth,
            bytes_accessed=32 * seqs * width * depth,
            transcendentals=seqs * width * depth,
        ),
        name="project_family",
    )(
        pltpu.with_memory_space_constraint(family, pltpu.HBM),
        pltpu.with_memory_space_constraint(query_key_value_gate_matrix, pltpu.HBM),
        pltpu.with_memory_space_constraint(covariance_merge_matrix, pltpu.HBM),
    )
    after, send = pl.pallas_call(
        functools.partial(attention_kernel, width, own),
        out_shape=(
            jax.ShapeDtypeStruct((seqs * width, depth), BF16),
            jax.ShapeDtypeStruct((sided + pairs, 128), BF16),
        ),
        in_specs=[vmem] * 8,
        out_specs=(vmem, vmem),
        scratch_shapes=[
            pltpu.VMEM((seqs * width, depth), BF16),
            pltpu.VMEM((seqs * width, 128), F32),
            pltpu.VMEM((seqs * width * hidden // 128, 128), F32),
            pltpu.VMEM((seqs * width * hidden // 128, 128), F32),
        ],
        compiler_params=pltpu.CompilerParams(vmem_limit_bytes=16 << 20),
        name="row_attention",
    )(family, got, logits, value, gating, heads_merge_matrix, factor, edge)
    gathered = lax.all_gather(send, "dap", axis=0, tiled=False)
    family_out, pair_out, pair_grad = pl.pallas_call(
        functools.partial(pair_kernel, "dap", width, own, hidden, seqs),
        out_shape=(
            jax.ShapeDtypeStruct((seqs * width, depth), BF16),
            jax.ShapeDtypeStruct((pairs, chans), BF16),
            jax.ShapeDtypeStruct((pairs, chans), F32),
        ),
        in_specs=[vmem] * 7,
        out_specs=(hbm, vmem, vmem),
        scratch_shapes=[
            pltpu.SemaphoreType.DMA(()),
            pltpu.VMEM((width * hidden * hidden // 128, 128 // hidden * 128), BF16),
            pltpu.VMEM((every, hidden * hidden), BF16),
            pltpu.VMEM((every, chans), F32),
            pltpu.VMEM((every, chans), F32),
            pltpu.VMEM((every, chans), F32),
            pltpu.VMEM((every, chans), F32),
            pltpu.VMEM((every, chans), F32),
            pltpu.VMEM((2 * pairs, chans), F32),
        ],
        compiler_params=pltpu.CompilerParams(vmem_limit_bytes=16 << 20),
        name="pair_update",
    )(gathered, got, loss, after, covariance, edges_gate_factor_matrix, cycle_merge_matrix)
    return (
        family_out.reshape(seqs, width, depth),
        pair_out.reshape(own, width, chans),
        pair_grad.reshape(own, width, chans),
    )


def fits_resident(dap, family, edge, logit, factor):
    seqs, width, depth = family.shape
    own, _, chans = edge.shape
    return (
        own * dap == width
        and dap % 2 == 0
        and width == 32
        and factor.shape[1] == 64
        and depth == 32 * logit.shape[1]
        and depth % 128 == 0
        and chans == 128
        and own * width == 128
        and seqs % 16 == 0
        and seqs * dap == 128
    )


def body(*args):
    dap = lax.axis_size("dap")
    if fits_resident(dap, args[0], args[1], args[4], args[6]):
        return body_resident(*args)
    return body_general(*args)


def solution(mesh):
    in_specs = (
        P(("dp", "dap"), None, None),
        P(("dp", "dap"), None, None),
        P(("dp", "dap"), None),
        P(),
        P(),
        P(),
        P(),
        P(),
        P(),
        P(),
        P(("dp", "dap"), None, None),
    )
    out_specs = (
        P(("dp", "dap"), None, None),
        P(("dp", "dap"), None, None),
        P(("dp", "dap"), None, None),
    )
    return jax.shard_map(body, mesh=mesh, in_specs=in_specs, out_specs=out_specs, check_vma=False)
```

```python
import functools
import math

import jax
import jax.numpy as jnp
from jax import lax
from jax.experimental import pallas as pl
from jax.experimental.pallas import tpu as pltpu
from jax.sharding import PartitionSpec as P

EPSILON = 1e-05


def standardize_features(values):
    center = values - jnp.mean(values, -1, keepdims=True)
    scale_inv = lax.rsqrt(jnp.mean(center * center, -1, keepdims=True) + EPSILON)
    return center * scale_inv


def norm_back(values, grad_out):
    center = values - jnp.mean(values, -1, keepdims=True)
    scale_inv = lax.rsqrt(jnp.mean(center * center, -1, keepdims=True) + EPSILON)
    standardized_source = center * scale_inv
    return scale_inv * (
        grad_out
        - jnp.mean(grad_out, -1, keepdims=True)
        - standardized_source * jnp.mean(grad_out * standardized_source, -1, keepdims=True)
    )


def lateral_heads_mixing(
    family_shard_slice, logit_offset_whole, query_key_value_gate_matrix, heads_merge_matrix
):
    homolog_number, amino_number, feature_depth = family_shard_slice.shape
    head_count = logit_offset_whole.shape[1]
    head_size = feature_depth // head_count
    standardized_source = standardize_features(family_shard_slice.astype(jnp.float32)).astype(
        jnp.bfloat16
    )
    projected = jnp.dot(
        standardized_source.reshape(-1, feature_depth),
        query_key_value_gate_matrix,
        preferred_element_type=jnp.float32,
    )
    projected = projected.reshape(homolog_number, amino_number, 4 * feature_depth)
    shape_heads = (homolog_number, amino_number, head_count, head_size)
    queries = projected[..., :feature_depth].astype(jnp.bfloat16).reshape(shape_heads)
    key_rows = (
        projected[..., feature_depth : 2 * feature_depth].astype(jnp.bfloat16).reshape(shape_heads)
    )
    value_rows = (
        projected[..., 2 * feature_depth : 3 * feature_depth]
        .astype(jnp.bfloat16)
        .reshape(shape_heads)
    )
    gating = jax.nn.sigmoid(projected[..., 3 * feature_depth :])
    logits = jnp.einsum("sihd,sjhd->sihj", queries, key_rows, preferred_element_type=jnp.float32)
    logits = logits / math.sqrt(head_size) + logit_offset_whole.astype(jnp.float32)[None]
    weights = jax.nn.softmax(logits, axis=-1).astype(jnp.bfloat16)
    mixed = jnp.einsum("sihj,sjhd->sihd", weights, value_rows, preferred_element_type=jnp.float32)
    gated = (gating * mixed.reshape(homolog_number, amino_number, feature_depth)).astype(
        jnp.bfloat16
    )
    edge_increment = jnp.dot(
        gated.reshape(-1, feature_depth), heads_merge_matrix, preferred_element_type=jnp.float32
    )
    return (
        family_shard_slice.astype(jnp.float32)
        + edge_increment.reshape(homolog_number, amino_number, feature_depth)
    ).astype(jnp.bfloat16)


def pair_projection_step(alignment_rows, left_right_factor_matrix):
    standardized_source = standardize_features(alignment_rows.astype(jnp.float32)).astype(
        jnp.bfloat16
    )
    edge_result = jnp.dot(
        standardized_source.reshape(-1, alignment_rows.shape[2]),
        left_right_factor_matrix,
        preferred_element_type=jnp.float32,
    )
    return edge_result.reshape(alignment_rows.shape[0], alignment_rows.shape[1], -1).astype(
        jnp.bfloat16
    )


def body_general(
    family_matrix,
    edge_matrix,
    edge_validity,
    query_key_value_gate_matrix,
    logit_offset_matrix,
    heads_merge_matrix,
    left_right_factor_matrix,
    covariance_merge_matrix,
    edges_gate_factor_matrix,
    cycle_merge_matrix,
    loss_sensitivity,
):
    res_rows, width, pair_chans = edge_matrix.shape
    pair_normed = standardize_features(edge_matrix.astype(jnp.float32)).astype(jnp.bfloat16)
    bias_local = jnp.einsum(
        "ijc,ch->ihj", pair_normed, logit_offset_matrix, preferred_element_type=jnp.float32
    ).astype(jnp.bfloat16)
    logit_offset_whole = lax.all_gather(bias_local, "dap", axis=0, tiled=True)
    homolog_lines = family_matrix.shape[0]
    homolog_subset = math.gcd(homolog_lines, 8)
    batched_lines = family_matrix.reshape(
        homolog_lines // homolog_subset,
        homolog_subset,
        family_matrix.shape[1],
        family_matrix.shape[2],
    )
    family_after_heads = lax.map(
        lambda family_shard_slice: lateral_heads_mixing(
            family_shard_slice, logit_offset_whole, query_key_value_gate_matrix, heads_merge_matrix
        ),
        batched_lines,
    ).reshape(family_matrix.shape)
    hidden = left_right_factor_matrix.shape[1] // 2
    weight_f32 = covariance_merge_matrix.astype(jnp.float32)
    alignment_columns = lax.all_to_all(
        family_after_heads, "dap", split_axis=1, concat_axis=0, tiled=True
    )
    edge_result = pair_projection_step(alignment_columns, left_right_factor_matrix)
    left_part = edge_result[..., :hidden]
    right_part = edge_result[..., hidden:]
    sequence_full_count = alignment_columns.shape[0]
    shard_in = lax.all_gather(right_part, "dap", axis=1, tiled=True)
    outer_sum = (
        jnp.einsum("sia,sjb->ijab", left_part, shard_in, preferred_element_type=jnp.float32)
        / sequence_full_count
    )
    row_count = shard_in.shape[1]
    flat = outer_sum.reshape(res_rows * row_count, hidden * hidden)
    edge_increment = jnp.dot(flat, weight_f32, precision=lax.Precision.HIGHEST).reshape(
        res_rows, row_count, pair_chans
    )
    pair_mid = (edge_matrix.astype(jnp.float32) + edge_increment).astype(jnp.bfloat16)
    tri_normed = standardize_features(pair_mid.astype(jnp.float32)).astype(jnp.bfloat16)
    tri_proj = jnp.dot(
        tri_normed.reshape(-1, pair_chans),
        edges_gate_factor_matrix,
        preferred_element_type=jnp.float32,
    ).reshape(res_rows, width, 3 * pair_chans)
    mask_f = edge_validity.astype(jnp.float32)[..., None]
    side_a = (mask_f * tri_proj[..., :pair_chans]).astype(jnp.bfloat16)
    side_b = (mask_f * tri_proj[..., pair_chans : 2 * pair_chans]).astype(jnp.bfloat16)
    gating = jax.nn.sigmoid(tri_proj[..., 2 * pair_chans :])
    tri_prod = jnp.einsum(
        "ikc,jkc->ijc",
        side_a,
        lax.all_gather(side_b, "dap", axis=0, tiled=True),
        preferred_element_type=jnp.float32,
    )
    prod_normed = standardize_features(tri_prod).astype(jnp.bfloat16)
    tri_update = jnp.dot(
        prod_normed.reshape(-1, pair_chans), cycle_merge_matrix, preferred_element_type=jnp.float32
    ).reshape(res_rows, width, pair_chans)
    pair_output = (pair_mid.astype(jnp.float32) + gating * tri_update).astype(jnp.bfloat16)
    cot_f32 = loss_sensitivity.astype(jnp.float32)
    grad_update = (cot_f32 * gating).astype(jnp.bfloat16)
    grad_normed = jnp.dot(
        grad_update.reshape(-1, pair_chans),
        cycle_merge_matrix.T,
        preferred_element_type=jnp.float32,
    ).reshape(res_rows, width, pair_chans)
    grad_prod = norm_back(tri_prod, grad_normed).astype(jnp.bfloat16)
    grad_part = grad_prod
    grad_a = jnp.einsum(
        "ijc,jkc->ikc",
        grad_part,
        lax.all_gather(side_b, "dap", axis=0, tiled=True),
        preferred_element_type=jnp.float32,
    )
    grad_part = grad_prod
    grad_b = lax.psum_scatter(
        jnp.einsum("ijc,ikc->jkc", grad_part, side_a, preferred_element_type=jnp.float32).astype(
            jnp.bfloat16
        ),
        "dap",
        scatter_dimension=0,
        tiled=True,
    ).astype(jnp.float32)
    grad_gate = cot_f32 * tri_update * gating * (1.0 - gating)
    grad_proj = jnp.concatenate([mask_f * grad_a, mask_f * grad_b, grad_gate], -1).astype(
        jnp.bfloat16
    )
    grad_input = jnp.dot(
        grad_proj.reshape(-1, 3 * pair_chans),
        edges_gate_factor_matrix.T,
        preferred_element_type=jnp.float32,
    ).reshape(res_rows, width, pair_chans)
    pair_gradient = cot_f32 + norm_back(pair_mid.astype(jnp.float32), grad_input)
    return (family_after_heads, pair_output, pair_gradient)


F32 = jnp.float32
BF16 = jnp.bfloat16
NT = (((1,), (1,)), ((), ()))
PARTS = 2


def dot(a, b):
    return jnp.dot(a, b, preferred_element_type=F32)


def dot_nt(a, b):
    return lax.dot_general(a, b, NT, preferred_element_type=F32)


def iota(shape, dim):
    return lax.broadcasted_iota(jnp.int32, shape, dim)


def pack_kernel(
    width, edge_ref, weight_ref, loss_ref, mask_ref, send_ref, edge_s, weight_s, loss_s, mask_s,
    tile_s, sems
):
    copies = [
        pltpu.make_async_copy(source, target, sems.at[k])
        for k, (source, target) in enumerate(
            (
                (edge_ref, edge_s),
                (weight_ref, weight_s),
                (loss_ref, loss_s),
                (mask_ref, mask_s),
            )
        )
    ]
    for copy in copies:
        copy.start()
    rows, chans = edge_s.shape
    heads = weight_s.shape[0]
    own = rows // width
    lanes = heads * width
    peers = width // own
    spread = (iota((heads, lanes), 0) == iota((heads, lanes), 1) // width).astype(F32)
    keep = iota((width, lanes), 0) == iota((width, lanes), 1) % width
    goal = iota((rows, rows), 0)
    source = goal % own * width + goal // (own * own) * own + goal // own % own
    place = (source == iota((rows, rows), 1)).astype(F32).astype(BF16)
    tile_s[...] = jnp.zeros(tile_s.shape, F32)
    for copy in copies:
        copy.wait()
    weight = lax.dot_general(
        weight_s[...], spread.astype(BF16), (((0,), (0,)), ((), ())), preferred_element_type=F32
    ).astype(BF16)
    column = dot(jnp.ones((8, chans), BF16), weight)[:1]
    every = dot(edge_s[...], weight)
    edge = edge_s[...].astype(F32)
    middle = jnp.mean(edge, -1, keepdims=True)
    center = edge - middle
    scale = lax.rsqrt(jnp.mean(center * center, -1, keepdims=True) + EPSILON)
    bias = scale * (every - middle * column)
    losses = dot(place, loss_s[...]).astype(BF16)
    tile_s[2 * own : 3 * own, :width] = mask_s[...].astype(F32)
    packed = tile_s[...]
    for r in range(own):
        picked = jnp.where(keep, bias[width * r : width * (r + 1)], 0.0)
        total = jnp.sum(picked, 0, keepdims=True)
        for t in range(lanes // 128):
            packed = jnp.where(
                iota((16, 128), 0) == own * t + r, total[:, 128 * t : 128 * t + 128], packed
            )
    packed = packed.astype(BF16)
    for e in range(peers):
        rank = e ^ 1
        send_ref[32 * rank : 32 * rank + 16, :] = packed
        send_ref[32 * rank + 16 : 32 * rank + 32, :] = losses[16 * e : 16 * e + 16]


def project_kernel(
    width,
    heads,
    hidden,
    family_hbm,
    project_hbm,
    covariance_hbm,
    logits_ref,
    value_ref,
    gating_ref,
    cov_ref,
    family_ref,
    project_ref,
    covariance_ref,
    sems,
    query_s,
    key_s,
    value_s,
    logits_s,
    cov_s,
):
    copies = [
        pltpu.make_async_copy(family_hbm, family_ref, sems.at[2]),
        pltpu.make_async_copy(project_hbm, project_ref, sems.at[0]),
        pltpu.make_async_copy(covariance_hbm, covariance_ref, sems.at[1]),
    ]
    for copy in copies:
        copy.start()
    rows, depth = family_ref.shape
    seqs = rows // width
    group = 128 // width
    copies[0].wait()
    normed = standardize_features(family_ref[...].astype(F32)).astype(BF16)
    copies[1].wait()
    query_s[...] = dot(normed, project_ref[:, :depth]).astype(BF16)
    key_s[...] = dot(normed, project_ref[:, depth : 2 * depth]).astype(BF16)
    value_s[...] = dot(normed, project_ref[:, 2 * depth : 3 * depth]).astype(BF16)
    gating_ref[...] = jax.nn.sigmoid(dot(normed, project_ref[:, 3 * depth :]))
    same = (iota((128, 128), 0) // width == iota((128, 128), 1) // width).astype(F32).astype(BF16)
    scale = 1.0 / math.sqrt(depth // heads)
    for t in range(depth // 128):
        cols = slice(128 * t, 128 * t + 128)
        for s in range(seqs):
            span = slice(width * s, width * s + width)
            keys = jnp.concatenate([key_s[span, cols]] * group, 0) * same
            logits_s[span, :] = dot_nt(query_s[span, cols], keys) * scale
            values = jnp.concatenate([value_s[span, cols]] * group, 0) * same
            value_ref[128 * s : 128 * (s + 1), cols] = values
        for k in range(rows // 128):
            span = slice(128 * k, 128 * (k + 1))
            logits_ref[span, cols] = logits_s[span, :].T
    copies[2].wait()
    cov_s[...] = covariance_ref[...].astype(F32)
    for b in range(hidden):
        rows_b = cov_s[pl.ds(b, hidden, stride=hidden), :].astype(BF16)
        cov_ref[0, hidden * b : hidden * (b + 1), :] = rows_b
        swapped = b ^ (group // 2)
        cov_ref[1, hidden * swapped : hidden * (swapped + 1), :] = rows_b


def attention_kernel(
    width,
    own,
    family_ref,
    got_ref,
    logits_ref,
    value_ref,
    gating_ref,
    merge_ref,
    factor_ref,
    edge_ref,
    family_out_ref,
    send_ref,
    after_s,
    weight_s,
    row_s,
    turn_s,
    line_s,
    sem,
):
    rows, depth = family_ref.shape
    seqs = rows // width
    tiles = depth // 128
    group = 128 // width
    biases = jnp.concatenate([got_ref[d ^ 1, :16, :] for d in range(got_ref.shape[0])], 0)
    gated = []
    for t in range(tiles):
        cols = slice(128 * t, 128 * t + 128)
        row = iota((128, biases.shape[0]), 0) % width
        take = iota((128, biases.shape[0]), 1) == 16 * (row // own) + own * t + row % own
        bias = dot(take.astype(F32).astype(BF16), biases).T
        for k in range(rows // 128):
            span = slice(128 * k, 128 * (k + 1))
            flipped = logits_ref[span, cols] + bias
            parts = []
            for h in range(group):
                some = flipped[width * h : width * (h + 1)]
                raised = jnp.exp(some - jnp.max(some, 0, keepdims=True))
                parts.append(raised * (1.0 / jnp.sum(raised, 0, keepdims=True)))
            weight_s[span, cols] = jnp.concatenate(parts, 0).astype(BF16).T
    for t in range(tiles):
        cols = slice(128 * t, 128 * t + 128)
        mixed = jnp.concatenate(
            [
                dot(weight_s[width * s : width * (s + 1), cols], value_ref[128 * s : 128 * (s + 1), cols])
                for s in range(seqs)
            ],
            0,
        )
        gated.append((gating_ref[:, cols] * mixed).astype(BF16))
    after = (
        family_ref[...].astype(F32) + dot(jnp.concatenate(gated, 1), merge_ref[...])
    ).astype(BF16)
    after_s[...] = after
    leave = pltpu.make_async_copy(after_s, family_out_ref, sem)
    leave.start()
    ready = standardize_features(after.astype(F32)).astype(BF16)
    hidden = factor_ref.shape[0] // 2
    groups = width // group
    row_s[:, : 2 * hidden] = dot_nt(ready, factor_ref[...])
    placed = jnp.zeros((groups * seqs, 128), F32)
    for q in range(group):
        picked = jnp.concatenate(
            [row_s[pl.ds(group * g + q, seqs, stride=width), :] for g in range(groups)], 0
        )[:, :hidden].astype(BF16)
        here = iota((hidden, 128), 0) + hidden * q == iota((hidden, 128), 1)
        placed = placed + dot(picked, here.astype(F32).astype(BF16))
    for g in range(groups):
        send_ref[seqs * g : seqs * (g + 1), :] = placed[seqs * g : seqs * (g + 1), :].astype(BF16)
    turned = dot_nt(factor_ref[hidden : 2 * hidden, :], ready)
    for k in range(rows // 128):
        turn_s[hidden * k : hidden * (k + 1), :] = turned[:, 128 * k : 128 * k + 128]
    chunks = hidden // group
    for k in range(rows // 128):
        blocks = [
            turn_s[pl.ds(hidden * k + q, chunks, stride=group), :] for q in range(group)
        ]
        for p, block in enumerate(block_transpose(blocks, width)):
            first = chunks * (group * k + p)
            line_s[first : first + chunks, :] = block
    base = seqs * groups
    for g in range(chunks):
        send_ref[base + seqs * g : base + seqs * (g + 1), :] = line_s[
            pl.ds(g, seqs, stride=chunks), :
        ].astype(BF16)
    send_ref[2 * base :, :] = edge_ref[...]
    leave.wait()


def block_transpose(blocks, step):
    lane = iota(blocks[0].shape, 1)
    for shift in (2 * step, step):
        low = lane // shift % 2 == 0
        stride = shift // step
        out = list(blocks)
        for q in range(len(blocks)):
            if q // stride % 2 == 0:
                x, y = blocks[q], blocks[q + stride]
                up = pltpu.roll(y, shift, 1)
                down = pltpu.roll(x, 4 * step - shift, 1)
                out[q] = jnp.where(low, x, up)
                out[q + stride] = jnp.where(low, down, y)
        blocks = out
    return blocks


def mean(values):
    return jnp.mean(values, -1, keepdims=True)


def merge_rows(parts):
    row = iota(parts[0].shape, 0)
    step = 1
    while len(parts) > 1:
        low = row // step % 2 == 0
        parts = [
            jnp.where(low, x, y) + pltpu.roll(jnp.where(low, y, x), step, 0)
            for x, y in zip(parts[::2], parts[1::2])
        ]
        step *= 2
    return parts[0]


def pair_kernel(
    axis,
    width,
    own,
    hidden,
    seqs,
    sides_ref,
    got_ref,
    own_loss_ref,
    covariance_ref,
    edges_ref,
    cycle_ref,
    out_ref,
    grad_ref,
    right_s,
    flat_s,
    mid_s,
    unit_s,
    scale_s,
    a_s,
    b_s,
    tri_s,
):
    me = lax.axis_index(axis)
    rank = me + 1 - 2 * (me % 2)
    n = sides_ref.shape[0]
    every = width * width
    group = 128 // hidden
    groups = width // group
    chunks = hidden // group
    pairs = own * width
    chans = 128
    total = seqs * n
    base = 2 * seqs * groups

    def gathered(first):
        return jnp.concatenate([sides_ref[d, first : first + seqs, :] for d in range(n)], 0)

    for g in range(chunks):
        turned = gathered(seqs * (groups + g)).T
        for q in range(group):
            right_s[width * g : width * (g + 1), total * q : total * (q + 1)] = turned[
                width * q : width * (q + 1), :
            ]
    block = iota((total, 128), 1) // hidden
    low_half = iota((width * chunks, 128), 1) < 64
    zero = jnp.zeros((total, 128), BF16)
    for g in range(groups):
        left = gathered(seqs * g)
        wide = left.astype(F32)
        rolled = [left] + [
            pltpu.roll(wide, hidden * d, 1).astype(BF16) for d in range(1, group)
        ]

        def placed(first, second, lane):
            return jnp.where(
                block == lane,
                rolled[(lane - first) % group],
                jnp.where(block == lane + 2, rolled[(lane + 2 - second) % group], zero),
            )

        halves = []
        for h in range(2):
            columns = []
            for even in range(0, group, 2):
                first, second = (even, even + 1) if h == 0 else (even + 1, even)
                columns.append(
                    jnp.concatenate([placed(first, second, lane) for lane in range(2)], 0)
                )
            halves.append(
                dot(
                    right_s[:, 2 * total * h : 2 * total * (h + 1)],
                    jnp.concatenate(columns, 1),
                ).astype(BF16)
            )
        for e in range(group // 2):
            x, y = (half[:, 128 * e : 128 * e + 128] for half in halves)
            for odd, outer in enumerate(
                (jnp.where(low_half, x, y), jnp.where(low_half, y, x))
            ):
                first = every // 2 * odd + width * (group // 2 * g + e)
                for c in range(chunks):
                    flat_s[first : first + width, 128 * c : 128 * c + 128] = outer[
                        width * c : width * (c + 1)
                    ]
    tiles = jnp.concatenate([got_ref[d ^ 1, :16, :] for d in range(n)], 0)
    pick = (iota((width, 128), 0) == iota((width, 128), 1)).astype(F32).astype(BF16)
    masks = dot_nt(pick, tiles)

    def kept(columns, first):
        return jnp.concatenate(
            [
                jnp.broadcast_to(columns[:, first + r : first + r + 1], (width, chans))
                for r in range(own)
            ],
            0,
        )

    count = width // PARTS
    lists = [
        [2 * (count * (p // 2) + k) + p % 2 for k in range(count)] for p in range(PARTS)
    ]
    centered = jnp.where(
        iota((chans, chans), 0) == iota((chans, chans), 1), 1.0 - 1.0 / chans, -1.0 / chans
    ).astype(BF16)
    added = [
        dot(
            flat_s[
                every // 2 * (p % 2) + width * count * (p // 2) : every // 2 * (p % 2)
                + width * count * (p // 2 + 1),
                :,
            ],
            covariance_ref[p % 2],
        )
        for p in range(PARTS)
    ]
    mids = []
    for p, residues in enumerate(lists):
        edge = jnp.concatenate(
            [
                sides_ref[i // own, base + width * (i % own) : base + width * (i % own + 1), :]
                for i in residues
            ],
            0,
        ).astype(F32)
        mids.append((edge + added[p] * (1.0 / total)).astype(BF16))
    centers = [dot(mid, centered) for mid in mids]
    scales = [lax.rsqrt(mean(c * c) + EPSILON) for c in centers]
    units = [c * scale for c, scale in zip(centers, scales)]
    sides = [dot(unit.astype(BF16), edges_ref[:, : 2 * chans]) for unit in units]
    for p, residues in enumerate(lists):
        for k, i in enumerate(residues):
            here = slice(width * k, width * (k + 1))
            there = slice(width * i, width * (i + 1))
            mid_s[there, :] = mids[p][here].astype(F32)
            scale_s[there, :] = jnp.broadcast_to(scales[p][here], (width, chans))
            unit_s[there, :] = units[p][here]
            lane = 16 * (i // own) + 2 * own + i % own
            keep = jnp.broadcast_to(masks[:, lane : lane + 1], (width, chans))
            a_s[there, :] = (keep * sides[p][here, :chans]).astype(BF16).astype(F32)
            b_s[there, :] = (keep * sides[p][here, chans:]).astype(BF16).astype(F32)

    rows = pl.ds(pl.multiple_of(me * pairs, pairs), pairs)

    def rows_and_columns(ref):
        return jnp.concatenate(
            [ref[rows, :]] + [ref[pl.ds(me * own + r, width, stride=width), :] for r in range(own)],
            0,
        )

    mid = mid_s[rows, :]
    losses = jnp.concatenate([got_ref[d ^ 1, 16:, :] for d in range(n)], 0)
    goal = iota((pairs, pairs), 0)
    source = goal % width // own * 16 + goal // width * own + goal % own
    place = (source == iota((pairs, pairs), 1)).astype(F32).astype(BF16)
    loss = jnp.concatenate([own_loss_ref[...].astype(F32), dot(place, losses)], 0)
    gating = jax.nn.sigmoid(
        dot(rows_and_columns(unit_s).astype(BF16), edges_ref[:, 2 * chans :])
    )
    tri = []
    for fixed, moving in ((a_s, b_s), (b_s, a_s)):
        held = fixed[rows, :]
        for r in range(own):
            mine = [held[width * r + 8 * v : width * r + 8 * v + 8] for v in range(width // 8)]
            for j in range(0, width, 8):
                parts = []
                for jj in range(j, j + 8):
                    prods = [
                        mine[v] * moving[width * jj + 8 * v : width * jj + 8 * v + 8, :]
                        for v in range(width // 8)
                    ]
                    parts.append(functools.reduce(jnp.add, prods))
                tri.append(merge_rows(parts))
    tri = jnp.concatenate(tri, 0)
    center = tri - mean(tri)
    scale_inv = lax.rsqrt(mean(center * center) + EPSILON)
    unit = center * scale_inv
    update = dot(unit[:pairs].astype(BF16), cycle_ref[...])
    out_ref[...] = (mid + gating[:pairs] * update).astype(BF16)
    grad_normed = dot_nt((loss * gating).astype(BF16), cycle_ref[...])
    tri_s[...] = (
        (
            scale_inv
            * (
                grad_normed - mean(grad_normed) - unit * mean(grad_normed * unit)
            )
        )
        .astype(BF16)
        .astype(F32)
    )

    acc = []
    for first, ref in ((0, b_s), (own, a_s)):
        sums = [[jnp.zeros((8, chans), F32) for _ in range(width // 8)] for _ in range(own)]
        for j in range(width):
            parts = [ref[width * j + 8 * v : width * j + 8 * v + 8, :] for v in range(width // 8)]
            for r in range(own):
                at = width * (first + r) + j
                row = jnp.broadcast_to(tri_s[at : at + 1, :], (8, chans))
                sums[r] = [old + row * part for old, part in zip(sums[r], parts)]
        acc += [jnp.concatenate(vregs, 0) for vregs in sums]
    keep = kept(dot_nt(pick, got_ref[rank, :16, :]), 2 * own)
    gate_own = gating[:pairs]
    grad_gate = loss[:pairs] * update * gate_own * (1.0 - gate_own)
    grad_proj = jnp.concatenate(
        [
            keep * jnp.concatenate(acc[:own], 0),
            keep * jnp.concatenate(acc[own:], 0),
            grad_gate,
        ],
        1,
    ).astype(BF16)
    grad_input = dot_nt(grad_proj, edges_ref[...])
    scale_inv = scale_s[rows, :]
    unit = unit_s[rows, :]
    grad_ref[...] = loss[:pairs] + scale_inv * (
        grad_input - mean(grad_input) - unit * mean(grad_input * unit)
    )


def body_resident(
    family_matrix,
    edge_matrix,
    edge_validity,
    query_key_value_gate_matrix,
    logit_offset_matrix,
    heads_merge_matrix,
    left_right_factor_matrix,
    covariance_merge_matrix,
    edges_gate_factor_matrix,
    cycle_merge_matrix,
    loss_sensitivity,
):
    seqs, width, depth = family_matrix.shape
    own, _, chans = edge_matrix.shape
    heads = logit_offset_matrix.shape[1]
    hidden = left_right_factor_matrix.shape[1] // 2
    pairs = own * width
    every = width * width
    edge = edge_matrix.reshape(pairs, chans)
    loss = loss_sensitivity.reshape(pairs, chans)
    vmem = pl.BlockSpec(memory_space=pltpu.VMEM)
    hbm = pl.BlockSpec(memory_space=pltpu.HBM)
    family = family_matrix.reshape(seqs * width, depth)
    factor = left_right_factor_matrix.T
    sided = 2 * seqs * width * hidden // 128
    peers = width // own
    packed = pl.pallas_call(
        functools.partial(pack_kernel, width),
        out_shape=jax.ShapeDtypeStruct((32 * peers, chans), BF16),
        in_specs=[hbm] * 4,
        out_specs=vmem,
        scratch_shapes=[
            pltpu.VMEM((pairs, chans), BF16),
            pltpu.VMEM((heads, chans), BF16),
            pltpu.VMEM((pairs, chans), BF16),
            pltpu.VMEM((own, width), jnp.int32),
            pltpu.VMEM((16, 128), F32),
            pltpu.SemaphoreType.DMA((4,)),
        ],
        name="pack_pairs",
    )(edge, logit_offset_matrix.T, loss, edge_validity)
    got = lax.all_to_all(
        packed, "dap", split_axis=0, concat_axis=0, axis_index_groups=[[d ^ 1 for d in range(peers)]], tiled=True
    )
    got = got.reshape(peers, 32, chans)
    logits, value, gating, covariance = pl.pallas_call(
        functools.partial(project_kernel, width, heads, hidden),
        out_shape=(
            jax.ShapeDtypeStruct((seqs * width, depth), F32),
            jax.ShapeDtypeStruct((seqs * 128, depth), BF16),
            jax.ShapeDtypeStruct((seqs * width, depth), F32),
            jax.ShapeDtypeStruct((2, hidden * hidden, chans), BF16),
        ),
        in_specs=[hbm, hbm, hbm],
        out_specs=(vmem,) * 4,
        scratch_shapes=[
            pltpu.VMEM((seqs * width, depth), BF16),
            pltpu.VMEM(query_key_value_gate_matrix.shape, BF16),
            pltpu.VMEM(covariance_merge_matrix.shape, BF16),
            pltpu.SemaphoreType.DMA((3,)),
        ]
        + [pltpu.VMEM((seqs * width, depth), BF16)] * 3
        + [pltpu.VMEM((seqs * width, 128), F32)]
        + [pltpu.VMEM((hidden * hidden, chans), F32)],
        compiler_params=pltpu.CompilerParams(vmem_limit_bytes=16 << 20),
        cost_estimate=pl.CostEstimate(
            flops=16 * seqs * width * depth * depth,
            bytes_accessed=32 * seqs * width * depth,
            transcendentals=seqs * width * depth,
        ),
        name="project_family",
    )(
        pltpu.with_memory_space_constraint(family, pltpu.HBM),
        pltpu.with_memory_space_constraint(query_key_value_gate_matrix, pltpu.HBM),
        pltpu.with_memory_space_constraint(covariance_merge_matrix, pltpu.HBM),
    )
    family_out, send = pl.pallas_call(
        functools.partial(attention_kernel, width, own),
        out_shape=(
            jax.ShapeDtypeStruct((seqs * width, depth), BF16),
            jax.ShapeDtypeStruct((sided + pairs, 128), BF16),
        ),
        in_specs=[vmem] * 8,
        out_specs=(hbm, vmem),
        scratch_shapes=[
            pltpu.VMEM((seqs * width, depth), BF16),
            pltpu.VMEM((seqs * width, depth), BF16),
            pltpu.VMEM((seqs * width, 128), F32),
            pltpu.VMEM((seqs * width * hidden // 128, 128), F32),
            pltpu.VMEM((seqs * width * hidden // 128, 128), F32),
            pltpu.SemaphoreType.DMA(()),
        ],
        compiler_params=pltpu.CompilerParams(vmem_limit_bytes=16 << 20),
        name="row_attention",
    )(family, got, logits, value, gating, heads_merge_matrix, factor, edge)
    gathered = lax.all_gather(send, "dap", axis=0, tiled=False)
    pair_out, pair_grad = pl.pallas_call(
        functools.partial(pair_kernel, "dap", width, own, hidden, seqs),
        out_shape=(
            jax.ShapeDtypeStruct((pairs, chans), BF16),
            jax.ShapeDtypeStruct((pairs, chans), F32),
        ),
        in_specs=[vmem] * 6,
        out_specs=(vmem, vmem),
        scratch_shapes=[
            pltpu.VMEM((width * hidden * hidden // 128, 128 // hidden * 128), BF16),
            pltpu.VMEM((every, hidden * hidden), BF16),
            pltpu.VMEM((every, chans), F32),
            pltpu.VMEM((every, chans), F32),
            pltpu.VMEM((every, chans), F32),
            pltpu.VMEM((every, chans), F32),
            pltpu.VMEM((every, chans), F32),
            pltpu.VMEM((2 * pairs, chans), F32),
        ],
        compiler_params=pltpu.CompilerParams(vmem_limit_bytes=16 << 20),
        name="pair_update",
    )(gathered, got, loss, covariance, edges_gate_factor_matrix, cycle_merge_matrix)
    return (
        family_out.reshape(seqs, width, depth),
        pair_out.reshape(own, width, chans),
        pair_grad.reshape(own, width, chans),
    )


def fits_resident(dap, family, edge, logit, factor):
    seqs, width, depth = family.shape
    own, _, chans = edge.shape
    return (
        own * dap == width
        and dap % 2 == 0
        and width == 32
        and factor.shape[1] == 64
        and depth == 32 * logit.shape[1]
        and depth % 128 == 0
        and chans == 128
        and own * width == 128
        and seqs % 16 == 0
        and seqs * dap == 128
    )


def body(*args):
    dap = lax.axis_size("dap")
    if fits_resident(dap, args[0], args[1], args[4], args[6]):
        return body_resident(*args)
    return body_general(*args)


def solution(mesh):
    in_specs = (
        P(("dp", "dap"), None, None),
        P(("dp", "dap"), None, None),
        P(("dp", "dap"), None),
        P(),
        P(),
        P(),
        P(),
        P(),
        P(),
        P(),
        P(("dp", "dap"), None, None),
    )
    out_specs = (
        P(("dp", "dap"), None, None),
        P(("dp", "dap"), None, None),
        P(("dp", "dap"), None, None),
    )
    return jax.shard_map(body, mesh=mesh, in_specs=in_specs, out_specs=out_specs, check_vma=False)
```
